512 devices in a mesh: state: 128 (over x, z, core), rep: 4 (over y).
Axes of the slice: x: 4, y: 4, z: 16, core: 2. Of those that a mesh axis runs over, the one named last changes fastest.
Arguments:
- ensemble: float32 [64, 524288], P('rep', 'state'), may hold values from -6 to 6
- obs_values: float32 [48], replicated, may hold values from -8 to 8
- obs_error: float32 [48], replicated, may hold values from 0.25 to 2
- obs_location: int32 [48], replicated, may hold values from 0 to 524287
Outputs:
- analysis: float32 [64, 524288], P('rep', 'state')
The draws below stay inside these ranges and needn't reach their ends.
All inputs are finite; a program needn't handle non-finite values.
Results may differ from the reference program's by a relative error of at most 0.0001.
Values sent between devices are 32-bit elements; how exact they have to be, the bound alone decides.
A program may use at most 64 MiB of HBM per device.

```python
import math
import jax
import jax.numpy as jnp
from jax import lax

M = 64
TILE = 128
NVAR = 524288
NOBS = 48
HALF = 4096


def place_ends(values, stream_key, smallest, high):
    spot = [jax.random.randint(jax.random.fold_in(stream_key, axis), (), 0, length) for axis, length in enumerate(values.shape)]
    main_axis = values.shape.index(max(values.shape))
    next_to = spot[:main_axis] + [(spot[main_axis] + 1) % values.shape[main_axis]] + spot[main_axis + 1:]
    return values.at[tuple(spot)].set(smallest).at[tuple(next_to)].set(high)


def block_scale(rng, extent, cuts, low, largest):
    level, own = 1.0, jax.random.fold_in(rng, 6)
    for dim, blocks in cuts:
        draws = jnp.exp(jax.random.uniform(jax.random.fold_in(own, dim), (blocks,), jnp.float32, low / len(cuts), largest / len(cuts)))
        level = level * jnp.repeat(draws, extent[dim] // blocks).reshape([-1 if axis == dim else 1 for axis in range(len(extent))])
    return level


def noise(own_key, extent, width, bound, cuts=(), held_as=jnp.bfloat16):
    loudness = block_scale(own_key, extent, cuts, -0.22, 0.18) if cuts else 1.0
    array = jax.random.normal(own_key, extent, jnp.float32) * width * loudness
    return jnp.minimum(jnp.maximum(array, -bound), bound).astype(held_as)


def setup_inputs(seed: int = 0) -> dict:
    splits = jax.random.split(jax.random.key(seed), 5)
    ensemble = noise(splits[0], (M, NVAR), 1.0, 6.0, ((0, 4), (1, 128)), jnp.float32)
    obs_values = noise(splits[1], (NOBS,), 1.5, 8.0, (), jnp.float32)
    obs_error = jnp.clip(jnp.exp(jax.random.uniform(splits[2], (NOBS,), jnp.float32, math.log(0.25), math.log(2.0))), 0.25, 2.0)
    obs_location = place_ends(jax.random.randint(splits[3], (NOBS,), 0, NVAR), jax.random.fold_in(splits[3], 1), 0, NVAR - 1).astype(jnp.int32)
    return {"ensemble": ensemble, "obs_values": obs_values, "obs_error": obs_error, "obs_location": obs_location}


def taper(distance):
    ratio = distance / HALF
    near_part = (((-0.25 * ratio + 0.5) * ratio + 0.625) * ratio - 5.0 / 3.0) * ratio * ratio + 1.0
    ratio_far = jnp.maximum(ratio, 1.0)
    far_part = ((((ratio_far / 12.0 - 0.5) * ratio_far + 0.625) * ratio_far + 5.0 / 3.0) * ratio_far - 5.0) * ratio_far + 4.0 - 2.0 / (3.0 * ratio_far)
    return jnp.where(ratio <= 1.0, near_part, jnp.where(ratio < 2.0, far_part, jnp.zeros_like(ratio)))

def centers_of(columns):
    return (columns // TILE * TILE).astype(jnp.float32) + (TILE - 1) * 0.5

def reference(ensemble, obs_values, obs_error, obs_location):
    tile_count = NVAR // TILE
    window_tiles = min(4 * HALF // TILE + 3, tile_count)
    window_width = window_tiles * TILE

    def assimilate(slot, analysis):
        location = obs_location[slot]
        prior_col = lax.dynamic_slice_in_dim(analysis, location, 1, 1)[:, 0]
        mean_value = jnp.mean(prior_col)
        spread = prior_col - mean_value
        variance = jnp.sum(spread * spread) / (M - 1)
        total_var = variance + obs_error[slot]
        shrink = 1.0 / (1.0 + jnp.sqrt(obs_error[slot] / total_var))
        u_vec = spread / ((M - 1) * total_var)
        w_vec = obs_values[slot] - mean_value - shrink * spread
        first_tile = jnp.clip(location // TILE - 2 * HALF // TILE - 1, 0, tile_count - window_tiles)
        window_start = (first_tile * TILE).astype(jnp.int32)
        window = lax.dynamic_slice_in_dim(analysis, window_start, window_width, 1)
        columns = window_start + lax.iota(jnp.int32, window_width)
        weights = taper(jnp.abs(centers_of(columns) - location.astype(jnp.float32)))
        coefficient = weights * jnp.dot(u_vec, window, precision=lax.Precision.HIGHEST)
        window = window + w_vec[:, None] * coefficient[None, :]
        return lax.dynamic_update_slice_in_dim(analysis, window, window_start, 1)
    return lax.fori_loop(0, NOBS, assimilate, ensemble)
```

```python
import functools

import jax
import jax.numpy as jnp
from jax import lax
from jax.experimental import pallas as pl
from jax.experimental.pallas import tpu as pltpu
from jax.sharding import PartitionSpec as P

MESH = pl.DeviceIdType.MESH
M = 64
TILE = 128
HALF = 4096
REACH = 2 * HALF
LINK = REACH + TILE // 2
NOBS = 48
REPS = 4
CORES = 2
WINDOW = 4
SLOTS = 8
CHUNKS = 4
ROWS = (2 * WINDOW + 1) * CORES * REPS


def taper(distance):
    ratio = distance * (1.0 / HALF)
    near_part = (((-0.25 * ratio + 0.5) * ratio + 0.625) * ratio - 5.0 / 3.0) * ratio * ratio + 1.0
    ratio_far = jnp.maximum(ratio, 1.0)
    far_part = (
        ((((ratio_far / 12.0 - 0.5) * ratio_far + 0.625) * ratio_far + 5.0 / 3.0) * ratio_far - 5.0)
        * ratio_far
        + 4.0
        - 2.0 / (3.0 * ratio_far)
    )
    return jnp.where(
        ratio <= 1.0, near_part, jnp.where(ratio < 2.0, far_part, jnp.zeros_like(ratio))
    )


def iota(shape, axis):
    return lax.broadcasted_iota(jnp.int32, shape, axis)


def gather_kernel(
    chips, held, loc_ref, ens_ref, rows_ref, all_ref, far_ref,
    local_ref, pick_ref, local_sem, own_sem, row_send, row_recv,
    send_right, send_left, recv_left, recv_right, pass_right, pass_left, far_left, far_right,
):
    state = lax.axis_index("state")
    rep = lax.axis_index("rep")
    chip = state // CORES
    core = state % CORES
    part_rows = ens_ref.shape[0]

    def partner(index):
        shift = index // (CORES * REPS) - WINDOW
        other_core = (core + (index // REPS) % CORES) % CORES
        other_rep = (rep + index % REPS) % REPS
        other_chip = (chip + shift + chips) % chips
        return shift, (other_chip * CORES + other_core, other_rep)

    itself = WINDOW * CORES * REPS
    tiles = held // TILE

    def load(tile):
        span = pl.ds(pl.multiple_of(tile * TILE, TILE), TILE)
        return pltpu.make_async_copy(ens_ref.at[:, span], local_ref.at[tile], local_sem)

    def fetch(tile, carry):
        load(tile).start()
        return carry

    lax.fori_loop(0, tiles, fetch, 0)
    barrier = pltpu.get_barrier_semaphore()

    def greet(index, carry):
        _, target = partner(index)
        pl.semaphore_signal(barrier, inc=1, device_id=target, device_id_type=MESH)
        return carry

    lax.fori_loop(0, itself, greet, 0)
    lax.fori_loop(itself + 1, ROWS, greet, 0)
    pltpu.make_async_copy(local_ref, local_ref, local_sem).wait()

    lane = iota((part_rows, TILE), 1)
    diagonal = lane - iota((part_rows, TILE), 0)

    def pick(j, carry):
        rank, packed = carry
        offset = loc_ref[j] - state * held
        inside = (offset >= 0) & (offset < held)
        safe = jnp.clip(offset, 0, held - 1)
        tile = local_ref[safe // TILE]
        wanted = jnp.where(inside, safe % TILE, -1)
        column = jnp.sum(jnp.where(lane == wanted, tile, 0.0), axis=1, keepdims=True)
        place = jnp.where(inside, rank * part_rows, -TILE * 2)
        packed = jnp.where(diagonal == place, column, packed)
        return rank + inside.astype(jnp.int32), packed

    _, packed = lax.fori_loop(
        0, NOBS, pick, (jnp.int32(0), jnp.zeros((part_rows, TILE), jnp.float32))
    )
    pick_ref[0] = jnp.sum(packed, axis=0, keepdims=True)

    pl.semaphore_wait(barrier, ROWS - 1)

    def row_copy(index):
        shift, target = partner(index)
        slot = ((WINDOW - shift) * CORES + core) * REPS + rep
        return pltpu.make_async_remote_copy(
            src_ref=pick_ref.at[0],
            dst_ref=rows_ref.at[slot],
            send_sem=row_send,
            recv_sem=row_recv,
            device_id=target,
            device_id_type=MESH,
        )

    def send_row(index, carry):
        row_copy(index).start()
        return carry

    lax.fori_loop(0, itself, send_row, 0)
    lax.fori_loop(itself + 1, ROWS, send_row, 0)
    own = pltpu.make_async_copy(
        pick_ref.at[0], rows_ref.at[(WINDOW * CORES + core) * REPS + rep], own_sem
    )
    own.start()

    right = (state, (rep + 1) % REPS)
    left = (state, (rep + REPS - 1) % REPS)
    width = held // CHUNKS

    def piece(ref, chunk):
        return ref.at[:, pl.ds(chunk * width, width)]

    def bulk(source, owner, chunk, target, send_sem, recv_sem):
        return pltpu.make_async_remote_copy(
            src_ref=piece(source, chunk),
            dst_ref=piece(all_ref.at[owner], chunk),
            send_sem=send_sem.at[chunk],
            recv_sem=recv_sem.at[chunk],
            device_id=target,
            device_id_type=MESH,
        )

    half = CHUNKS // 2
    to_right = [bulk(ens_ref, rep, c, right, send_right, recv_left) for c in range(CHUNKS)]
    to_left = [bulk(ens_ref, rep, c, left, send_left, recv_right) for c in range(CHUNKS)]
    for step in range(CHUNKS):
        to_right[step].start()
        to_left[(step + half) % CHUNKS].start()

    shards = iota((8, TILE), 1)
    first = shards * held

    def reach(i, carry):
        low, high, count, far = carry
        spot = loc_ref[NOBS - 1 - i]
        near = (spot >= low) & (spot <= high)
        away = jnp.abs(spot // (held * CORES) - shards // CORES) > WINDOW
        count = count + (spot // held == shards).astype(jnp.int32)
        far = jnp.where((near & away) | (count > SLOTS), 1, far)
        low = jnp.where(near, jnp.minimum(low, spot - LINK), low)
        high = jnp.where(near, jnp.maximum(high, spot + LINK), high)
        return low, high, count, far

    zeros = jnp.zeros((8, TILE), jnp.int32)
    far = lax.fori_loop(
        0, NOBS, reach, (first - REACH, first + held + REACH, zeros, zeros)
    )[3]
    far_ref[0, 0] = jnp.max(far)

    left_rep, right_rep, across = left[1], right[1], (rep + 2) % REPS
    relays = []
    for step in range(half):
        to_right[step].wait_recv()
        relay = bulk(all_ref.at[left_rep], left_rep, step, right, pass_right, far_left)
        relay.start()
        relays.append(relay)
        to_left[half + step].wait_recv()
        relay = bulk(all_ref.at[right_rep], right_rep, half + step, left, pass_left, far_right)
        relay.start()
        relays.append(relay)
    for step in range(half):
        to_right[half + step].wait_recv()
        to_left[step].wait_recv()
    for relay in relays:
        relay.wait()
    for copy in to_right + to_left:
        copy.wait_send()
    own.wait()
    pltpu.make_async_copy(
        rows_ref.at[pl.ds(0, ROWS - 1)], rows_ref.at[pl.ds(0, ROWS - 1)], row_send
    ).wait()
    pltpu.make_async_copy(
        rows_ref.at[pl.ds(0, ROWS - 1)], rows_ref.at[pl.ds(0, ROWS - 1)], row_recv
    ).wait()


def gather(mesh, ensemble, locations):
    part_rows, held = ensemble.shape
    dma = pltpu.SemaphoreType.DMA
    return pl.pallas_call(
        functools.partial(gather_kernel, mesh.shape["state"] // CORES, held),
        out_shape=(
            jax.ShapeDtypeStruct((ROWS, 1, TILE), jnp.float32),
            jax.ShapeDtypeStruct((REPS, part_rows, held), jnp.float32),
            jax.ShapeDtypeStruct((1, 1), jnp.int32),
        ),
        in_specs=[pl.BlockSpec(memory_space=pltpu.SMEM), pl.BlockSpec(memory_space=pl.ANY)],
        out_specs=(
            pl.BlockSpec(memory_space=pl.ANY),
            pl.BlockSpec(memory_space=pl.ANY),
            pl.BlockSpec(memory_space=pltpu.SMEM),
        ),
        scratch_shapes=[
            pltpu.VMEM((held // TILE, part_rows, TILE), jnp.float32),
            pltpu.VMEM((1, 1, TILE), jnp.float32),
            dma, dma, dma, dma,
            dma((CHUNKS,)), dma((CHUNKS,)), dma((CHUNKS,)), dma((CHUNKS,)),
            dma((CHUNKS,)), dma((CHUNKS,)), dma((CHUNKS,)), dma((CHUNKS,)),
        ],
        compiler_params=pltpu.CompilerParams(collective_id=0, has_side_effects=True),
        name="gather",
    )(locations, ensemble)


def solve_kernel(
    windowed, held, loc_ref, val_ref, err_ref, rows_ref, ens_ref, all_ref, out_ref,
    s_ref, y_ref, u_ref, w_ref, center_ref, mutual_ref, tile_ref,
    flag_ref, list_ref, slot_ref, direct_ref, count_ref, load_sem, out_sem,
):
    state = lax.axis_index("state")
    rep = lax.axis_index("rep")
    chip = state // CORES
    part_rows = ens_ref.shape[0]

    def rows_of(index):
        return pl.ds(pl.multiple_of(index * part_rows, part_rows), part_rows)

    loads = [pltpu.make_async_copy(ens_ref, s_ref.at[rows_of(rep)], load_sem.at[0])]
    for step in range(1, REPS):
        other = (rep + step) % REPS
        loads.append(
            pltpu.make_async_copy(all_ref.at[other], s_ref.at[rows_of(other)], load_sem.at[step])
        )
    for load in loads:
        load.start()

    low_own = state * held - REACH
    high_own = state * held + held + REACH

    def mark(i, carry):
        low, high = carry
        j = NOBS - 1 - i
        spot = loc_ref[j]
        near = (spot >= low) & (spot <= high)
        flag_ref[j] = near.astype(jnp.int32)
        count_ref[spot // held] = 0
        low = jnp.where(near, jnp.minimum(low, spot - LINK), low)
        high = jnp.where(near, jnp.maximum(high, spot + LINK), high)
        return low, high

    lax.fori_loop(0, NOBS, mark, (low_own, high_own))

    def enlist(j, carry):
        total, direct = carry
        spot = loc_ref[j]
        shard = spot // held
        rank = count_ref[shard]
        count_ref[shard] = rank + 1
        list_ref[total] = j
        slot_ref[total] = rank
        direct_ref[direct] = total
        touches = (spot >= low_own) & (spot <= high_own)
        return total + flag_ref[j], direct + touches.astype(jnp.int32)

    total, direct = lax.fori_loop(0, NOBS, enlist, (jnp.int32(0), jnp.int32(0)))

    diagonal = iota((part_rows, TILE), 1) - iota((part_rows, TILE), 0)

    def spread(t, carry):
        j = list_ref[t]
        spot = loc_ref[j]
        shard = spot // held
        if windowed:
            base = ((shard // CORES - chip + WINDOW) * CORES + shard % CORES) * REPS
            place = slot_ref[t] * part_rows
        else:
            base = j * REPS
            place = 0
        for r in range(REPS):
            row = jnp.broadcast_to(rows_ref[base + r], (part_rows, TILE))
            column = jnp.sum(jnp.where(diagonal == place, row, 0.0), axis=1, keepdims=True)
            y_ref[t, r * part_rows : (r + 1) * part_rows, :] = jnp.broadcast_to(
                column, (part_rows, TILE)
            )
        center = (spot // TILE * TILE).astype(jnp.float32) + (TILE - 1) * 0.5
        center_ref[pl.ds(t, 1), :] = jnp.full((1, TILE), center, jnp.float32)
        return carry

    lax.fori_loop(0, total, spread, 0)

    tiles = held // TILE
    tile_centers = (state * held + iota((tiles, TILE), 0) * TILE).astype(jnp.float32) + (
        TILE - 1
    ) * 0.5

    def assimilate(t, carry):
        j = list_ref[t]
        spot = loc_ref[j].astype(jnp.float32)
        error = err_ref[j]
        y = y_ref[t]
        mean = jnp.sum(y, axis=0, keepdims=True) * (1.0 / M)
        spread_of = y - mean
        variance = jnp.sum(spread_of * spread_of, axis=0, keepdims=True) * (1.0 / (M - 1))
        total_var = variance + error
        shrink = 1.0 / (1.0 + jnp.sqrt(error / total_var))
        u = spread_of * (1.0 / ((M - 1) * total_var))
        w = (val_ref[j] - mean) - shrink * spread_of
        u_ref[t] = u
        w_ref[t] = w
        mutual_ref[...] = taper(jnp.abs(center_ref[...] - spot))
        tile_ref[t] = taper(jnp.abs(tile_centers - spot))

        def update(k, inner):
            other = y_ref[k]
            projected = jnp.sum(u * other, axis=0, keepdims=True)
            y_ref[k] = other + w * (mutual_ref[pl.ds(k, 1), :] * projected)
            return inner

        lax.fori_loop(t + 1, total, update, 0)
        return carry

    lax.fori_loop(0, total, assimilate, 0)

    for load in loads:
        load.wait()
    group = 4

    def apply(g, carry):
        spans = [
            pl.ds(pl.multiple_of((g * group + i) * TILE, TILE), TILE) for i in range(group)
        ]

        def one(d, values):
            t = direct_ref[d]
            u = u_ref[t]
            w = w_ref[t]
            result = []
            for i in range(group):
                projected = jnp.sum(u * values[i], axis=0, keepdims=True)
                weight = tile_ref[t, pl.ds(g * group + i, 1), :]
                result.append(values[i] + w * (weight * projected))
            return tuple(result)

        values = lax.fori_loop(0, direct, one, tuple(s_ref[:, span] for span in spans))
        for span, value in zip(spans, values):
            s_ref[:, span] = value
        return carry

    lax.fori_loop(0, tiles // group, apply, 0)
    store = pltpu.make_async_copy(s_ref.at[rows_of(rep)], out_ref, out_sem)
    store.start()
    store.wait()


def solve(windowed, ensemble, values, errors, locations, rows, everything):
    part_rows, held = ensemble.shape
    smem = pl.BlockSpec(memory_space=pltpu.SMEM)
    anywhere = pl.BlockSpec(memory_space=pl.ANY)
    block = pltpu.VMEM((NOBS, M, TILE), jnp.float32)
    return pl.pallas_call(
        functools.partial(solve_kernel, windowed, held),
        out_shape=jax.ShapeDtypeStruct((part_rows, held), jnp.float32),
        in_specs=[smem, smem, smem, pl.BlockSpec(memory_space=pltpu.VMEM), anywhere, anywhere],
        out_specs=anywhere,
        scratch_shapes=[
            pltpu.VMEM((M, held), jnp.float32),
            block, block, block,
            pltpu.VMEM((NOBS, TILE), jnp.float32),
            pltpu.VMEM((NOBS, TILE), jnp.float32),
            pltpu.VMEM((NOBS, held // TILE, TILE), jnp.float32),
            pltpu.SMEM((NOBS,), jnp.int32),
            pltpu.SMEM((NOBS,), jnp.int32),
            pltpu.SMEM((NOBS,), jnp.int32),
            pltpu.SMEM((NOBS,), jnp.int32),
            pltpu.SMEM((128,), jnp.int32),
            pltpu.SemaphoreType.DMA((REPS,)),
            pltpu.SemaphoreType.DMA,
        ],
        name="solve",
    )(locations, values, errors, rows, ensemble, everything)


def full_rows(mesh, ensemble, locations):
    part_rows, held = ensemble.shape
    states = mesh.shape["state"]
    offsets = locations - lax.axis_index("state") * held
    inside = ((offsets >= 0) & (offsets < held)).astype(jnp.float32)
    columns = jnp.take(ensemble, jnp.clip(offsets, 0, held - 1), axis=1) * inside[None, :]
    placed = jnp.zeros((REPS, part_rows, NOBS), jnp.float32)
    placed = lax.dynamic_update_slice(placed, columns[None], (lax.axis_index("rep"), 0, 0))
    stride = 1
    while stride < states:
        pairs = [(i, i ^ stride) for i in range(states)]
        placed = placed + lax.ppermute(placed, "state", pairs)
        stride *= 2
    stride = 1
    while stride < REPS:
        pairs = [(i, i ^ stride) for i in range(REPS)]
        placed = placed + lax.ppermute(placed, "rep", pairs)
        stride *= 2
    by_obs = jnp.transpose(placed, (2, 0, 1)).reshape(NOBS * REPS, 1, part_rows)
    return jnp.pad(by_obs, ((0, 0), (0, 0), (0, TILE - part_rows)))


def on_device(mesh, ensemble, obs_values, obs_error, obs_location):
    rows, everything, far = gather(mesh, ensemble, obs_location)
    return lax.cond(
        far[0, 0] == 0,
        lambda: solve(True, ensemble, obs_values, obs_error, obs_location, rows, everything),
        lambda: solve(
            False, ensemble, obs_values, obs_error, obs_location,
            full_rows(mesh, ensemble, obs_location), everything,
        ),
    )


def solution(mesh):
    in_specs = (P("rep", "state"), P(), P(), P())
    out_specs = P("rep", "state")
    return jax.shard_map(
        functools.partial(on_device, mesh),
        mesh=mesh,
        in_specs=in_specs,
        out_specs=out_specs,
        check_vma=False,
    )
```

```python
import functools

import jax
import jax.numpy as jnp
from jax import lax
from jax.experimental import pallas as pl
from jax.experimental.pallas import tpu as pltpu
from jax.sharding import PartitionSpec as P

MESH = pl.DeviceIdType.MESH
M = 64
TILE = 128
HALF = 4096
REACH = 2 * HALF
LINK = REACH + TILE // 2
NOBS = 48
REPS = 4
CORES = 2
WINDOW = 4
DEPTH = 16
SLOTS = 8
CHUNKS = 4
ROWS = (2 * WINDOW + 1) * CORES * REPS


def taper(distance):
    ratio = distance * (1.0 / HALF)
    near_part = (((-0.25 * ratio + 0.5) * ratio + 0.625) * ratio - 5.0 / 3.0) * ratio * ratio + 1.0
    ratio_far = jnp.maximum(ratio, 1.0)
    far_part = (
        ((((ratio_far / 12.0 - 0.5) * ratio_far + 0.625) * ratio_far + 5.0 / 3.0) * ratio_far - 5.0)
        * ratio_far
        + 4.0
        - 2.0 / (3.0 * ratio_far)
    )
    return jnp.where(
        ratio <= 1.0, near_part, jnp.where(ratio < 2.0, far_part, jnp.zeros_like(ratio))
    )


def iota(shape, axis):
    return lax.broadcasted_iota(jnp.int32, shape, axis)


def gather_kernel(
    chips, held, loc_ref, ens_ref, rows_ref, all_ref, far_ref,
    local_ref, pick_ref, local_sem, own_sem, late_sem, row_send, row_recv,
    send_right, send_left, recv_left, recv_right, pass_right, pass_left, far_left, far_right,
):
    state = lax.axis_index("state")
    rep = lax.axis_index("rep")
    chip = state >> 1
    core = state & 1
    part_rows = ens_ref.shape[0]
    tiles = held // TILE

    def load(tile):
        span = pl.ds(pl.multiple_of(tile * TILE, TILE), TILE)
        return pltpu.make_async_copy(ens_ref.at[:, span], local_ref.at[tile], local_sem)

    for tile in range(tiles):
        load(tile).start()

    depth = chip & (DEPTH - 1)
    shifts = [shift for shift in range(-WINDOW, WINDOW + 1) if shift != 0]
    valid = {n: (chip + n >= 0) & (chip + n < chips) for n in shifts}
    ahead = {n: (depth + n < DEPTH) if n > 0 else (depth + n < 0) for n in shifts}
    later = {n: valid[n] & ahead[n] for n in shifts}
    earlier = {n: valid[n] & jnp.logical_not(ahead[n]) for n in shifts}
    members = [(c, r) for c in range(CORES) for r in range(REPS)]
    beside = members[1:]
    cores_of = [core, 1 - core]
    reps_of = [(rep + r) & (REPS - 1) for r in range(REPS)]

    def target(shift, member):
        return (chip + shift) * CORES + cores_of[member[0]], reps_of[member[1]]

    def signal(semaphore, shift, member):
        pl.semaphore_signal(
            semaphore, inc=1, device_id=target(shift, member), device_id_type=MESH
        )

    def count_of(flags):
        return sum(flags[n].astype(jnp.int32) for n in shifts) * len(members)

    barrier = pltpu.get_barrier_semaphore()
    for member in beside:
        signal(barrier, 0, member)
    for n in shifts:

        @pl.when(later[n])
        def _(n=n):
            for member in members:
                signal(barrier, n, member)

    pltpu.make_async_copy(local_ref, local_ref, local_sem).wait()
    lane = iota((part_rows, TILE), 1)
    diagonal = lane - iota((part_rows, TILE), 0)
    rank = jnp.int32(0)
    packed = jnp.zeros((part_rows, TILE), jnp.float32)
    for j in range(NOBS):
        offset = loc_ref[j] - state * held
        inside = (offset >= 0) & (offset < held)
        safe = jnp.clip(offset, 0, held - 1)
        tile = local_ref[safe >> 7]
        wanted = jnp.where(inside, safe & (TILE - 1), -1)
        column = jnp.sum(jnp.where(lane == wanted, tile, 0.0), axis=1, keepdims=True)
        place = jnp.where(inside, rank * part_rows, -TILE * 2)
        packed = jnp.where(diagonal == place, column, packed)
        rank = rank + inside.astype(jnp.int32)
    pick_ref[0] = jnp.sum(packed, axis=0, keepdims=True)

    pl.semaphore_wait(barrier, len(beside) + count_of(earlier))

    def send_row(shift, member):
        slot = ((WINDOW - shift) * CORES + core) * REPS + rep
        pltpu.make_async_remote_copy(
            src_ref=pick_ref.at[0],
            dst_ref=rows_ref.at[slot],
            send_sem=row_send.at[WINDOW + shift],
            recv_sem=row_recv.at[WINDOW - shift],
            device_id=target(shift, member),
            device_id_type=MESH,
        ).start()

    for n in shifts:

        @pl.when(earlier[n])
        def _(n=n):
            for member in members:
                signal(late_sem.at[WINDOW - n], n, member)
            for member in members:
                send_row(n, member)

    for member in beside:
        send_row(0, member)
    own = pltpu.make_async_copy(
        pick_ref.at[0], rows_ref.at[(WINDOW * CORES + core) * REPS + rep], own_sem
    )
    own.start()

    right = (state, reps_of[1])
    left = (state, reps_of[3])
    width = held // CHUNKS

    def piece(ref, chunk):
        return ref.at[:, pl.ds(chunk * width, width)]

    def bulk(source, owner, chunk, target, send_sem, recv_sem):
        return pltpu.make_async_remote_copy(
            src_ref=piece(source, chunk),
            dst_ref=piece(all_ref.at[owner], chunk),
            send_sem=send_sem.at[chunk],
            recv_sem=recv_sem.at[chunk],
            device_id=target,
            device_id_type=MESH,
        )

    half = CHUNKS // 2
    to_right = [bulk(ens_ref, rep, c, right, send_right, recv_left) for c in range(CHUNKS)]
    to_left = [bulk(ens_ref, rep, c, left, send_left, recv_right) for c in range(CHUNKS)]
    for step in range(CHUNKS):
        to_right[step].start()
        to_left[(step + half) % CHUNKS].start()

    shards = iota((8, TILE), 1)
    first = shards * held

    def reach(i, carry):
        low, high, count, far = carry
        spot = loc_ref[NOBS - 1 - i]
        near = (spot >= low) & (spot <= high)
        away = jnp.abs((spot >> 13) - (shards >> 1)) > WINDOW
        count = count + ((spot >> 12) == shards).astype(jnp.int32)
        far = jnp.where((near & away) | (count > SLOTS), 1, far)
        low = jnp.where(near, jnp.minimum(low, spot - LINK), low)
        high = jnp.where(near, jnp.maximum(high, spot + LINK), high)
        return low, high, count, far

    zeros = jnp.zeros((8, TILE), jnp.int32)
    far = lax.fori_loop(
        0, NOBS, reach, (first - REACH, first + held + REACH, zeros, zeros), unroll=8
    )[3]
    far_ref[0, 0] = jnp.max(far)

    relays = []
    for step in range(half):
        to_right[step].wait_recv()
        relay = bulk(all_ref.at[left[1]], left[1], step, right, pass_right, far_left)
        relay.start()
        relays.append(relay)
        to_left[half + step].wait_recv()
        relay = bulk(all_ref.at[right[1]], right[1], half + step, left, pass_left, far_right)
        relay.start()
        relays.append(relay)

    for n in shifts:

        @pl.when(later[n])
        def _(n=n):
            pl.semaphore_wait(late_sem.at[WINDOW + n], len(members))
            for member in members:
                send_row(n, member)

    for step in range(half):
        to_right[half + step].wait_recv()
        to_left[step].wait_recv()
    for relay in relays:
        relay.wait()
    for copy in to_right + to_left:
        copy.wait_send()
    own.wait()

    def drain(semaphores, shift, number):
        block = rows_ref.at[pl.ds((WINDOW + shift) * len(members), number)]
        pltpu.make_async_copy(block, block, semaphores.at[WINDOW + shift]).wait()

    drain(row_send, 0, len(beside))
    drain(row_recv, 0, len(beside))
    for n in shifts:

        @pl.when(valid[n])
        def _(n=n):
            drain(row_send, n, len(members))
            drain(row_recv, n, len(members))


def gather(mesh, ensemble, locations):
    part_rows, held = ensemble.shape
    dma = pltpu.SemaphoreType.DMA
    return pl.pallas_call(
        functools.partial(gather_kernel, mesh.shape["state"] // CORES, held),
        out_shape=(
            jax.ShapeDtypeStruct((ROWS, 1, TILE), jnp.float32),
            jax.ShapeDtypeStruct((REPS, part_rows, held), jnp.float32),
            jax.ShapeDtypeStruct((1, 1), jnp.int32),
        ),
        in_specs=[pl.BlockSpec(memory_space=pltpu.SMEM), pl.BlockSpec(memory_space=pl.ANY)],
        out_specs=(
            pl.BlockSpec(memory_space=pl.ANY),
            pl.BlockSpec(memory_space=pl.ANY),
            pl.BlockSpec(memory_space=pltpu.SMEM),
        ),
        scratch_shapes=[
            pltpu.VMEM((held // TILE, part_rows, TILE), jnp.float32),
            pltpu.VMEM((1, 1, TILE), jnp.float32),
            dma, dma, pltpu.SemaphoreType.REGULAR((2 * WINDOW + 1,)),
            dma((2 * WINDOW + 1,)), dma((2 * WINDOW + 1,)),
            dma((CHUNKS,)), dma((CHUNKS,)), dma((CHUNKS,)), dma((CHUNKS,)),
            dma((CHUNKS,)), dma((CHUNKS,)), dma((CHUNKS,)), dma((CHUNKS,)),
        ],
        compiler_params=pltpu.CompilerParams(collective_id=0, has_side_effects=True),
        name="gather",
    )(locations, ensemble)


def solve_kernel(
    windowed, held, loc_ref, val_ref, err_ref, rows_ref, ens_ref, all_ref, out_ref,
    s_ref, y_ref, u_ref, w_ref, center_ref, mutual_ref, tile_ref,
    flag_ref, list_ref, slot_ref, direct_ref, count_ref, load_sem, out_sem,
):
    state = lax.axis_index("state")
    rep = lax.axis_index("rep")
    chip = state // CORES
    part_rows = ens_ref.shape[0]

    def rows_of(index):
        return pl.ds(pl.multiple_of(index * part_rows, part_rows), part_rows)

    loads = [pltpu.make_async_copy(ens_ref, s_ref.at[rows_of(rep)], load_sem.at[0])]
    for step in range(1, REPS):
        other = (rep + step) % REPS
        loads.append(
            pltpu.make_async_copy(all_ref.at[other], s_ref.at[rows_of(other)], load_sem.at[step])
        )
    for load in loads:
        load.start()

    low_own = state * held - REACH
    high_own = state * held + held + REACH

    def mark(i, carry):
        low, high = carry
        j = NOBS - 1 - i
        spot = loc_ref[j]
        near = (spot >= low) & (spot <= high)
        flag_ref[j] = near.astype(jnp.int32)
        count_ref[spot // held] = 0
        low = jnp.where(near, jnp.minimum(low, spot - LINK), low)
        high = jnp.where(near, jnp.maximum(high, spot + LINK), high)
        return low, high

    lax.fori_loop(0, NOBS, mark, (low_own, high_own))

    def enlist(j, carry):
        total, direct = carry
        spot = loc_ref[j]
        shard = spot // held
        rank = count_ref[shard]
        count_ref[shard] = rank + 1
        list_ref[total] = j
        slot_ref[total] = rank
        direct_ref[direct] = total
        touches = (spot >= low_own) & (spot <= high_own)
        return total + flag_ref[j], direct + touches.astype(jnp.int32)

    total, direct = lax.fori_loop(0, NOBS, enlist, (jnp.int32(0), jnp.int32(0)))

    diagonal = iota((part_rows, TILE), 1) - iota((part_rows, TILE), 0)

    def spread(t, carry):
        j = list_ref[t]
        spot = loc_ref[j]
        shard = spot // held
        if windowed:
            base = ((shard // CORES - chip + WINDOW) * CORES + shard % CORES) * REPS
            place = slot_ref[t] * part_rows
        else:
            base = j * REPS
            place = 0
        for r in range(REPS):
            row = jnp.broadcast_to(rows_ref[base + r], (part_rows, TILE))
            column = jnp.sum(jnp.where(diagonal == place, row, 0.0), axis=1, keepdims=True)
            y_ref[t, r * part_rows : (r + 1) * part_rows, :] = jnp.broadcast_to(
                column, (part_rows, TILE)
            )
        center = (spot // TILE * TILE).astype(jnp.float32) + (TILE - 1) * 0.5
        center_ref[pl.ds(t, 1), :] = jnp.full((1, TILE), center, jnp.float32)
        return carry

    lax.fori_loop(0, total, spread, 0)

    tiles = held // TILE
    tile_centers = (state * held + iota((tiles, TILE), 0) * TILE).astype(jnp.float32) + (
        TILE - 1
    ) * 0.5

    def assimilate(t, carry):
        j = list_ref[t]
        spot = loc_ref[j].astype(jnp.float32)
        error = err_ref[j]
        y = y_ref[t]
        mean = jnp.sum(y, axis=0, keepdims=True) * (1.0 / M)
        spread_of = y - mean
        variance = jnp.sum(spread_of * spread_of, axis=0, keepdims=True) * (1.0 / (M - 1))
        total_var = variance + error
        shrink = 1.0 / (1.0 + jnp.sqrt(error / total_var))
        u = spread_of * (1.0 / ((M - 1) * total_var))
        w = (val_ref[j] - mean) - shrink * spread_of
        u_ref[t] = u
        w_ref[t] = w
        mutual_ref[...] = taper(jnp.abs(center_ref[...] - spot))
        tile_ref[t] = taper(jnp.abs(tile_centers - spot))

        def update(k, inner):
            other = y_ref[k]
            projected = jnp.sum(u * other, axis=0, keepdims=True)
            y_ref[k] = other + w * (mutual_ref[pl.ds(k, 1), :] * projected)
            return inner

        lax.fori_loop(t + 1, total, update, 0)
        return carry

    lax.fori_loop(0, total, assimilate, 0)

    for load in loads:
        load.wait()
    group = 4

    def apply(g, carry):
        spans = [
            pl.ds(pl.multiple_of((g * group + i) * TILE, TILE), TILE) for i in range(group)
        ]

        def one(d, values):
            t = direct_ref[d]
            u = u_ref[t]
            w = w_ref[t]
            result = []
            for i in range(group):
                projected = jnp.sum(u * values[i], axis=0, keepdims=True)
                weight = tile_ref[t, pl.ds(g * group + i, 1), :]
                result.append(values[i] + w * (weight * projected))
            return tuple(result)

        values = lax.fori_loop(0, direct, one, tuple(s_ref[:, span] for span in spans))
        for span, value in zip(spans, values):
            s_ref[:, span] = value
        return carry

    lax.fori_loop(0, tiles // group, apply, 0)
    store = pltpu.make_async_copy(s_ref.at[rows_of(rep)], out_ref, out_sem)
    store.start()
    store.wait()


def solve(windowed, ensemble, values, errors, locations, rows, everything):
    part_rows, held = ensemble.shape
    smem = pl.BlockSpec(memory_space=pltpu.SMEM)
    anywhere = pl.BlockSpec(memory_space=pl.ANY)
    block = pltpu.VMEM((NOBS, M, TILE), jnp.float32)
    return pl.pallas_call(
        functools.partial(solve_kernel, windowed, held),
        out_shape=jax.ShapeDtypeStruct((part_rows, held), jnp.float32),
        in_specs=[smem, smem, smem, pl.BlockSpec(memory_space=pltpu.VMEM), anywhere, anywhere],
        out_specs=anywhere,
        scratch_shapes=[
            pltpu.VMEM((M, held), jnp.float32),
            block, block, block,
            pltpu.VMEM((NOBS, TILE), jnp.float32),
            pltpu.VMEM((NOBS, TILE), jnp.float32),
            pltpu.VMEM((NOBS, held // TILE, TILE), jnp.float32),
            pltpu.SMEM((NOBS,), jnp.int32),
            pltpu.SMEM((NOBS,), jnp.int32),
            pltpu.SMEM((NOBS,), jnp.int32),
            pltpu.SMEM((NOBS,), jnp.int32),
            pltpu.SMEM((128,), jnp.int32),
            pltpu.SemaphoreType.DMA((REPS,)),
            pltpu.SemaphoreType.DMA,
        ],
        name="solve",
    )(locations, values, errors, rows, ensemble, everything)


def full_rows(mesh, ensemble, locations):
    part_rows, held = ensemble.shape
    states = mesh.shape["state"]
    offsets = locations - lax.axis_index("state") * held
    inside = ((offsets >= 0) & (offsets < held)).astype(jnp.float32)
    columns = jnp.take(ensemble, jnp.clip(offsets, 0, held - 1), axis=1) * inside[None, :]
    placed = jnp.zeros((REPS, part_rows, NOBS), jnp.float32)
    placed = lax.dynamic_update_slice(placed, columns[None], (lax.axis_index("rep"), 0, 0))
    stride = 1
    while stride < states:
        pairs = [(i, i ^ stride) for i in range(states)]
        placed = placed + lax.ppermute(placed, "state", pairs)
        stride *= 2
    stride = 1
    while stride < REPS:
        pairs = [(i, i ^ stride) for i in range(REPS)]
        placed = placed + lax.ppermute(placed, "rep", pairs)
        stride *= 2
    by_obs = jnp.transpose(placed, (2, 0, 1)).reshape(NOBS * REPS, 1, part_rows)
    return jnp.pad(by_obs, ((0, 0), (0, 0), (0, TILE - part_rows)))


def on_device(mesh, ensemble, obs_values, obs_error, obs_location):
    rows, everything, far = gather(mesh, ensemble, obs_location)
    return lax.cond(
        far[0, 0] == 0,
        lambda: solve(True, ensemble, obs_values, obs_error, obs_location, rows, everything),
        lambda: solve(
            False, ensemble, obs_values, obs_error, obs_location,
            full_rows(mesh, ensemble, obs_location), everything,
        ),
    )


def solution(mesh):
    in_specs = (P("rep", "state"), P(), P(), P())
    out_specs = P("rep", "state")
    return jax.shard_map(
        functools.partial(on_device, mesh),
        mesh=mesh,
        in_specs=in_specs,
        out_specs=out_specs,
        check_vma=False,
    )
```

```python
import functools

import jax
import jax.numpy as jnp
from jax import lax
from jax.experimental import pallas as pl
from jax.experimental.pallas import tpu as pltpu
from jax.sharding import PartitionSpec as P

MESH = pl.DeviceIdType.MESH
M = 64
TILE = 128
HALF = 4096
REACH = 2 * HALF
LINK = REACH + TILE // 2
NOBS = 48
REPS = 4
CORES = 2
WINDOW = 4
DEPTH = 16
SLOTS = 8
CHUNKS = 4
ROWS = (2 * WINDOW + 1) * CORES * REPS


def taper(distance):
    ratio = distance * (1.0 / HALF)
    near_part = (((-0.25 * ratio + 0.5) * ratio + 0.625) * ratio - 5.0 / 3.0) * ratio * ratio + 1.0
    ratio_far = jnp.maximum(ratio, 1.0)
    far_part = (
        ((((ratio_far / 12.0 - 0.5) * ratio_far + 0.625) * ratio_far + 5.0 / 3.0) * ratio_far - 5.0)
        * ratio_far
        + 4.0
        - 2.0 / (3.0 * ratio_far)
    )
    return jnp.where(
        ratio <= 1.0, near_part, jnp.where(ratio < 2.0, far_part, jnp.zeros_like(ratio))
    )


def iota(shape, axis):
    return lax.broadcasted_iota(jnp.int32, shape, axis)


def gather_kernel(
    chips, held, loc_ref, ens_ref, rows_ref, all_ref, far_ref,
    fetch_ref, local_ref, pick_ref, local_sem, own_sem, late_sem, near_send, near_recv, row_send, row_recv,
    send_right, send_left, recv_left, recv_right, pass_right, pass_left, far_left, far_right,
):
    state = lax.axis_index("state")
    rep = lax.axis_index("rep")
    chip = state >> 1
    core = state & 1
    part_rows = ens_ref.shape[0]
    tiles = held // TILE

    load = pltpu.make_async_copy(ens_ref, fetch_ref, local_sem)
    load.start()

    depth = chip & (DEPTH - 1)
    shifts = [shift for shift in range(-WINDOW, WINDOW + 1) if shift != 0]
    valid = {n: (chip + n >= 0) & (chip + n < chips) for n in shifts}
    ahead = {n: (depth + n < DEPTH) if n > 0 else (depth + n < 0) for n in shifts}
    later = {n: valid[n] & ahead[n] for n in shifts}
    earlier = {n: valid[n] & jnp.logical_not(ahead[n]) for n in shifts}
    members = [(c, r) for c in range(CORES) for r in range(REPS)]
    beside = members[1:]
    cores_of = [core, 1 - core]
    reps_of = [(rep + r) & (REPS - 1) for r in range(REPS)]

    def target(shift, member):
        return (chip + shift) * CORES + cores_of[member[0]], reps_of[member[1]]

    def signal(semaphore, shift, member):
        pl.semaphore_signal(
            semaphore, inc=1, device_id=target(shift, member), device_id_type=MESH
        )

    def count_of(flags):
        return sum(flags[n].astype(jnp.int32) for n in shifts)

    barrier = pltpu.get_barrier_semaphore()
    for member in beside:
        signal(barrier, 0, member)
    for n in shifts:

        @pl.when(later[n])
        def _(n=n):
            signal(barrier, n, members[0])

    load.wait()
    for tile in range(tiles):
        local_ref[tile] = fetch_ref[:, tile * TILE : (tile + 1) * TILE]
    lane = iota((part_rows, TILE), 1)
    diagonal = lane - iota((part_rows, TILE), 0)
    rank = jnp.int32(0)
    packed = jnp.zeros((part_rows, TILE), jnp.float32)
    for j in range(NOBS):
        offset = loc_ref[j] - state * held
        inside = (offset >= 0) & (offset < held)
        safe = jnp.clip(offset, 0, held - 1)
        tile = local_ref[safe >> 7]
        wanted = jnp.where(inside, safe & (TILE - 1), -1)
        column = jnp.sum(jnp.where(lane == wanted, tile, 0.0), axis=1, keepdims=True)
        place = jnp.where(inside, rank * part_rows, -TILE * 2)
        packed = jnp.where(diagonal == place, column, packed)
        rank = rank + inside.astype(jnp.int32)
    pick_ref[0] = jnp.sum(packed, axis=0, keepdims=True)

    pl.semaphore_wait(barrier, len(beside) + count_of(earlier))

    own_row = (WINDOW * CORES + core) * REPS + rep
    for member in beside:
        pltpu.make_async_remote_copy(
            src_ref=pick_ref.at[0],
            dst_ref=rows_ref.at[own_row],
            send_sem=near_send,
            recv_sem=near_recv,
            device_id=target(0, member),
            device_id_type=MESH,
        ).start()
    own = pltpu.make_async_copy(pick_ref.at[0], rows_ref.at[own_row], own_sem)
    own.start()
    for n in shifts:

        @pl.when(earlier[n])
        def _(n=n):
            signal(late_sem.at[WINDOW - n], n, members[0])

    def block(shift, number=len(members)):
        return rows_ref.at[pl.ds((WINDOW + shift) * len(members), number)]

    def send_block(shift):
        pltpu.make_async_remote_copy(
            src_ref=block(0),
            dst_ref=block(-shift),
            send_sem=row_send.at[WINDOW + shift],
            recv_sem=row_recv.at[WINDOW - shift],
            device_id=target(shift, members[0]),
            device_id_type=MESH,
        ).start()

    right = (state, reps_of[1])
    left = (state, reps_of[3])
    width = held // CHUNKS

    def piece(ref, chunk):
        return ref.at[:, pl.ds(chunk * width, width)]

    def bulk(source, owner, chunk, target, send_sem, recv_sem):
        return pltpu.make_async_remote_copy(
            src_ref=piece(source, chunk),
            dst_ref=piece(all_ref.at[owner], chunk),
            send_sem=send_sem.at[chunk],
            recv_sem=recv_sem.at[chunk],
            device_id=target,
            device_id_type=MESH,
        )

    half = CHUNKS // 2
    to_right = [bulk(ens_ref, rep, c, right, send_right, recv_left) for c in range(CHUNKS)]
    to_left = [bulk(ens_ref, rep, c, left, send_left, recv_right) for c in range(CHUNKS)]
    for step in range(CHUNKS):
        to_right[step].start()
        to_left[(step + half) % CHUNKS].start()

    own.wait()
    nearby = block(0, len(beside))
    pltpu.make_async_copy(nearby, nearby, near_recv).wait()
    for n in shifts:

        @pl.when(earlier[n])
        def _(n=n):
            send_block(n)

    shards = iota((8, TILE), 1)
    first = shards * held

    def reach(i, carry):
        low, high, count, far = carry
        spot = loc_ref[NOBS - 1 - i]
        near = (spot >= low) & (spot <= high)
        away = jnp.abs((spot >> 13) - (shards >> 1)) > WINDOW
        count = count + ((spot >> 12) == shards).astype(jnp.int32)
        far = jnp.where((near & away) | (count > SLOTS), 1, far)
        low = jnp.where(near, jnp.minimum(low, spot - LINK), low)
        high = jnp.where(near, jnp.maximum(high, spot + LINK), high)
        return low, high, count, far

    zeros = jnp.zeros((8, TILE), jnp.int32)
    far = lax.fori_loop(
        0, NOBS, reach, (first - REACH, first + held + REACH, zeros, zeros), unroll=8
    )[3]
    far_ref[0, 0] = jnp.max(far)

    relays = []
    for step in range(half):
        to_right[step].wait_recv()
        relay = bulk(all_ref.at[left[1]], left[1], step, right, pass_right, far_left)
        relay.start()
        relays.append(relay)
        to_left[half + step].wait_recv()
        relay = bulk(all_ref.at[right[1]], right[1], half + step, left, pass_left, far_right)
        relay.start()
        relays.append(relay)

    for n in shifts:

        @pl.when(later[n])
        def _(n=n):
            pl.semaphore_wait(late_sem.at[WINDOW + n], 1)
            send_block(n)

    for step in range(half):
        to_right[half + step].wait_recv()
        to_left[step].wait_recv()
    for relay in relays:
        relay.wait()
    for copy in to_right + to_left:
        copy.wait_send()
    pltpu.make_async_copy(nearby, nearby, near_send).wait()

    for n in shifts:

        @pl.when(valid[n])
        def _(n=n):
            pltpu.make_async_copy(block(n), block(n), row_send.at[WINDOW + n]).wait()
            pltpu.make_async_copy(block(n), block(n), row_recv.at[WINDOW + n]).wait()


def gather(mesh, ensemble, locations):
    part_rows, held = ensemble.shape
    dma = pltpu.SemaphoreType.DMA
    return pl.pallas_call(
        functools.partial(gather_kernel, mesh.shape["state"] // CORES, held),
        out_shape=(
            jax.ShapeDtypeStruct((ROWS, 1, TILE), jnp.float32),
            jax.ShapeDtypeStruct((REPS, part_rows, held), jnp.float32),
            jax.ShapeDtypeStruct((1, 1), jnp.int32),
        ),
        in_specs=[pl.BlockSpec(memory_space=pltpu.SMEM), pl.BlockSpec(memory_space=pl.ANY)],
        out_specs=(
            pl.BlockSpec(memory_space=pl.ANY),
            pl.BlockSpec(memory_space=pl.ANY),
            pl.BlockSpec(memory_space=pltpu.SMEM),
        ),
        scratch_shapes=[
            pltpu.VMEM((part_rows, held), jnp.float32),
            pltpu.VMEM((held // TILE, part_rows, TILE), jnp.float32),
            pltpu.VMEM((1, 1, TILE), jnp.float32),
            dma, dma, pltpu.SemaphoreType.REGULAR((2 * WINDOW + 1,)),
            dma, dma, dma((2 * WINDOW + 1,)), dma((2 * WINDOW + 1,)),
            dma((CHUNKS,)), dma((CHUNKS,)), dma((CHUNKS,)), dma((CHUNKS,)),
            dma((CHUNKS,)), dma((CHUNKS,)), dma((CHUNKS,)), dma((CHUNKS,)),
        ],
        compiler_params=pltpu.CompilerParams(collective_id=0, has_side_effects=True),
        name="gather",
    )(locations, ensemble)


def solve_kernel(
    windowed, held, loc_ref, val_ref, err_ref, rows_ref, ens_ref, all_ref, out_ref,
    s_ref, y_ref, u_ref, w_ref, center_ref, mutual_ref, tile_ref,
    flag_ref, list_ref, slot_ref, direct_ref, count_ref, load_sem, out_sem,
):
    state = lax.axis_index("state")
    rep = lax.axis_index("rep")
    chip = state // CORES
    part_rows = ens_ref.shape[0]

    def rows_of(index):
        return pl.ds(pl.multiple_of(index * part_rows, part_rows), part_rows)

    loads = [pltpu.make_async_copy(ens_ref, s_ref.at[rows_of(rep)], load_sem.at[0])]
    for step in range(1, REPS):
        other = (rep + step) % REPS
        loads.append(
            pltpu.make_async_copy(all_ref.at[other], s_ref.at[rows_of(other)], load_sem.at[step])
        )
    for load in loads:
        load.start()

    low_own = state * held - REACH
    high_own = state * held + held + REACH

    def mark(i, carry):
        low, high = carry
        j = NOBS - 1 - i
        spot = loc_ref[j]
        near = (spot >= low) & (spot <= high)
        flag_ref[j] = near.astype(jnp.int32)
        count_ref[spot // held] = 0
        low = jnp.where(near, jnp.minimum(low, spot - LINK), low)
        high = jnp.where(near, jnp.maximum(high, spot + LINK), high)
        return low, high

    lax.fori_loop(0, NOBS, mark, (low_own, high_own))

    def enlist(j, carry):
        total, direct = carry
        spot = loc_ref[j]
        shard = spot // held
        rank = count_ref[shard]
        count_ref[shard] = rank + 1
        list_ref[total] = j
        slot_ref[total] = rank
        direct_ref[direct] = total
        touches = (spot >= low_own) & (spot <= high_own)
        return total + flag_ref[j], direct + touches.astype(jnp.int32)

    total, direct = lax.fori_loop(0, NOBS, enlist, (jnp.int32(0), jnp.int32(0)))

    diagonal = iota((part_rows, TILE), 1) - iota((part_rows, TILE), 0)

    def spread(t, carry):
        j = list_ref[t]
        spot = loc_ref[j]
        shard = spot // held
        if windowed:
            base = ((shard // CORES - chip + WINDOW) * CORES + shard % CORES) * REPS
            place = slot_ref[t] * part_rows
        else:
            base = j * REPS
            place = 0
        for r in range(REPS):
            row = jnp.broadcast_to(rows_ref[base + r], (part_rows, TILE))
            column = jnp.sum(jnp.where(diagonal == place, row, 0.0), axis=1, keepdims=True)
            y_ref[t, r * part_rows : (r + 1) * part_rows, :] = jnp.broadcast_to(
                column, (part_rows, TILE)
            )
        center = (spot // TILE * TILE).astype(jnp.float32) + (TILE - 1) * 0.5
        center_ref[pl.ds(t, 1), :] = jnp.full((1, TILE), center, jnp.float32)
        return carry

    lax.fori_loop(0, total, spread, 0)

    tiles = held // TILE
    tile_centers = (state * held + iota((tiles, TILE), 0) * TILE).astype(jnp.float32) + (
        TILE - 1
    ) * 0.5

    def assimilate(t, carry):
        j = list_ref[t]
        spot = loc_ref[j].astype(jnp.float32)
        error = err_ref[j]
        y = y_ref[t]
        mean = jnp.sum(y, axis=0, keepdims=True) * (1.0 / M)
        spread_of = y - mean
        variance = jnp.sum(spread_of * spread_of, axis=0, keepdims=True) * (1.0 / (M - 1))
        total_var = variance + error
        shrink = 1.0 / (1.0 + jnp.sqrt(error / total_var))
        u = spread_of * (1.0 / ((M - 1) * total_var))
        w = (val_ref[j] - mean) - shrink * spread_of
        u_ref[t] = u
        w_ref[t] = w
        mutual_ref[...] = taper(jnp.abs(center_ref[...] - spot))
        tile_ref[t] = taper(jnp.abs(tile_centers - spot))

        def update(k, inner):
            other = y_ref[k]
            projected = jnp.sum(u * other, axis=0, keepdims=True)
            y_ref[k] = other + w * (mutual_ref[pl.ds(k, 1), :] * projected)
            return inner

        lax.fori_loop(t + 1, total, update, 0)
        return carry

    lax.fori_loop(0, total, assimilate, 0)

    for load in loads:
        load.wait()
    group = 4

    def apply(g, carry):
        spans = [
            pl.ds(pl.multiple_of((g * group + i) * TILE, TILE), TILE) for i in range(group)
        ]

        def one(d, values):
            t = direct_ref[d]
            u = u_ref[t]
            w = w_ref[t]
            result = []
            for i in range(group):
                projected = jnp.sum(u * values[i], axis=0, keepdims=True)
                weight = tile_ref[t, pl.ds(g * group + i, 1), :]
                result.append(values[i] + w * (weight * projected))
            return tuple(result)

        values = lax.fori_loop(0, direct, one, tuple(s_ref[:, span] for span in spans))
        for span, value in zip(spans, values):
            s_ref[:, span] = value
        return carry

    lax.fori_loop(0, tiles // group, apply, 0)
    store = pltpu.make_async_copy(s_ref.at[rows_of(rep)], out_ref, out_sem)
    store.start()
    store.wait()


def solve(windowed, ensemble, values, errors, locations, rows, everything):
    part_rows, held = ensemble.shape
    smem = pl.BlockSpec(memory_space=pltpu.SMEM)
    anywhere = pl.BlockSpec(memory_space=pl.ANY)
    block = pltpu.VMEM((NOBS, M, TILE), jnp.float32)
    return pl.pallas_call(
        functools.partial(solve_kernel, windowed, held),
        out_shape=jax.ShapeDtypeStruct((part_rows, held), jnp.float32),
        in_specs=[smem, smem, smem, pl.BlockSpec(memory_space=pltpu.VMEM), anywhere, anywhere],
        out_specs=anywhere,
        scratch_shapes=[
            pltpu.VMEM((M, held), jnp.float32),
            block, block, block,
            pltpu.VMEM((NOBS, TILE), jnp.float32),
            pltpu.VMEM((NOBS, TILE), jnp.float32),
            pltpu.VMEM((NOBS, held // TILE, TILE), jnp.float32),
            pltpu.SMEM((NOBS,), jnp.int32),
            pltpu.SMEM((NOBS,), jnp.int32),
            pltpu.SMEM((NOBS,), jnp.int32),
            pltpu.SMEM((NOBS,), jnp.int32),
            pltpu.SMEM((128,), jnp.int32),
            pltpu.SemaphoreType.DMA((REPS,)),
            pltpu.SemaphoreType.DMA,
        ],
        name="solve",
    )(locations, values, errors, rows, ensemble, everything)


def full_rows(mesh, ensemble, locations):
    part_rows, held = ensemble.shape
    states = mesh.shape["state"]
    offsets = locations - lax.axis_index("state") * held
    inside = ((offsets >= 0) & (offsets < held)).astype(jnp.float32)
    columns = jnp.take(ensemble, jnp.clip(offsets, 0, held - 1), axis=1) * inside[None, :]
    placed = jnp.zeros((REPS, part_rows, NOBS), jnp.float32)
    placed = lax.dynamic_update_slice(placed, columns[None], (lax.axis_index("rep"), 0, 0))
    stride = 1
    while stride < states:
        pairs = [(i, i ^ stride) for i in range(states)]
        placed = placed + lax.ppermute(placed, "state", pairs)
        stride *= 2
    stride = 1
    while stride < REPS:
        pairs = [(i, i ^ stride) for i in range(REPS)]
        placed = placed + lax.ppermute(placed, "rep", pairs)
        stride *= 2
    by_obs = jnp.transpose(placed, (2, 0, 1)).reshape(NOBS * REPS, 1, part_rows)
    return jnp.pad(by_obs, ((0, 0), (0, 0), (0, TILE - part_rows)))


def on_device(mesh, ensemble, obs_values, obs_error, obs_location):
    rows, everything, far = gather(mesh, ensemble, obs_location)
    return lax.cond(
        far[0, 0] == 0,
        lambda: solve(True, ensemble, obs_values, obs_error, obs_location, rows, everything),
        lambda: solve(
            False, ensemble, obs_values, obs_error, obs_location,
            full_rows(mesh, ensemble, obs_location), everything,
        ),
    )


def solution(mesh):
    in_specs = (P("rep", "state"), P(), P(), P())
    out_specs = P("rep", "state")
    return jax.shard_map(
        functools.partial(on_device, mesh),
        mesh=mesh,
        in_specs=in_specs,
        out_specs=out_specs,
        check_vma=False,
    )
```

```python
import functools

import jax
import jax.numpy as jnp
from jax import lax
from jax.experimental import pallas as pl
from jax.experimental.pallas import tpu as pltpu
from jax.sharding import PartitionSpec as P

MESH = pl.DeviceIdType.MESH
M = 64
TILE = 128
HALF = 4096
REACH = 2 * HALF
LINK = REACH + TILE // 2
NOBS = 48
REPS = 4
CORES = 2
WINDOW = 4
DEPTH = 16
SLOTS = 8
CHUNKS = 4
ROWS = (2 * WINDOW + 1) * CORES * REPS


def taper(distance):
    ratio = distance * (1.0 / HALF)
    near_part = (((-0.25 * ratio + 0.5) * ratio + 0.625) * ratio - 5.0 / 3.0) * ratio * ratio + 1.0
    ratio_far = jnp.maximum(ratio, 1.0)
    far_part = (
        ((((ratio_far / 12.0 - 0.5) * ratio_far + 0.625) * ratio_far + 5.0 / 3.0) * ratio_far - 5.0)
        * ratio_far
        + 4.0
        - 2.0 / (3.0 * ratio_far)
    )
    return jnp.where(
        ratio <= 1.0, near_part, jnp.where(ratio < 2.0, far_part, jnp.zeros_like(ratio))
    )


def iota(shape, axis):
    return lax.broadcasted_iota(jnp.int32, shape, axis)


def gather_kernel(
    chips, held, loc_any, val_any, err_any, ens_ref, rows_ref, all_ref, table_out, far_out,
    loc_ref, val_ref, err_ref, far_ref, table_ref, small_sem, block_sem, fetch_ref, local_ref, pick_ref, local_sem, own_sem, late_sem, near_send, near_recv, row_send, row_recv,
    send_right, send_left, recv_left, recv_right, pass_right, pass_left, far_left, far_right,
):
    state = lax.axis_index("state")
    rep = lax.axis_index("rep")
    chip = state >> 1
    core = state & 1
    part_rows = ens_ref.shape[0]
    tiles = held // TILE

    load = pltpu.make_async_copy(ens_ref, fetch_ref, local_sem)
    load.start()
    smalls = [
        pltpu.make_async_copy(loc_any, loc_ref, small_sem.at[0]),
        pltpu.make_async_copy(val_any, val_ref, small_sem.at[1]),
        pltpu.make_async_copy(err_any, err_ref, small_sem.at[2]),
    ]
    for small in smalls:
        small.start()

    depth = chip & (DEPTH - 1)
    shifts = list(range(1, WINDOW + 1)) + list(range(-1, -WINDOW - 1, -1))
    valid = {n: (chip + n >= 0) & (chip + n < chips) for n in shifts}

    def key(place):
        return place + jnp.where((place >> 2) == 2, DEPTH, 0)

    ahead = {n: key((depth + n) & (DEPTH - 1)) > key(depth) for n in shifts}
    later = {n: valid[n] & ahead[n] for n in shifts}
    earlier = {n: valid[n] & jnp.logical_not(ahead[n]) for n in shifts}
    members = [(c, r) for c in range(CORES) for r in range(REPS)]
    beside = members[1:]
    cores_of = [core, 1 - core]
    reps_of = [(rep + r) & (REPS - 1) for r in range(REPS)]

    def target(shift, member):
        return (chip + shift) * CORES + cores_of[member[0]], reps_of[member[1]]

    def signal(semaphore, shift, member):
        pl.semaphore_signal(
            semaphore, inc=1, device_id=target(shift, member), device_id_type=MESH
        )

    def count_of(flags):
        return sum(flags[n].astype(jnp.int32) for n in shifts)

    barrier = pltpu.get_barrier_semaphore()
    for member in beside:
        signal(barrier, 0, member)
    for n in shifts:

        @pl.when(later[n])
        def _(n=n):
            signal(barrier, n, members[0])

    smalls[0].wait()
    load.wait()
    block_copy = pltpu.make_async_copy(fetch_ref, all_ref.at[rep], block_sem)
    block_copy.start()
    for tile in range(tiles):
        local_ref[tile] = fetch_ref[:, tile * TILE : (tile + 1) * TILE]
    lane = iota((part_rows, TILE), 1)
    diagonal = lane - iota((part_rows, TILE), 0)
    rank = jnp.int32(0)
    packed = jnp.zeros((part_rows, TILE), jnp.float32)
    for j in range(NOBS):
        offset = loc_ref[j] - state * held
        inside = (offset >= 0) & (offset < held)
        safe = jnp.clip(offset, 0, held - 1)
        tile = local_ref[safe >> 7]
        wanted = jnp.where(inside, safe & (TILE - 1), -1)
        column = jnp.sum(jnp.where(lane == wanted, tile, 0.0), axis=1, keepdims=True)
        place = jnp.where(inside, rank * part_rows, -TILE * 2)
        packed = jnp.where(diagonal == place, column, packed)
        rank = rank + inside.astype(jnp.int32)
    pick_ref[0] = jnp.sum(packed, axis=0, keepdims=True)

    pl.semaphore_wait(barrier, len(beside) + count_of(earlier))

    own_row = (WINDOW * CORES + core) * REPS + rep
    for member in beside:
        pltpu.make_async_remote_copy(
            src_ref=pick_ref.at[0],
            dst_ref=rows_ref.at[own_row],
            send_sem=near_send,
            recv_sem=near_recv,
            device_id=target(0, member),
            device_id_type=MESH,
        ).start()
    own = pltpu.make_async_copy(pick_ref.at[0], rows_ref.at[own_row], own_sem)
    own.start()
    for n in shifts:

        @pl.when(earlier[n])
        def _(n=n):
            signal(late_sem.at[WINDOW - n], n, members[0])

    def block(shift, number=len(members)):
        return rows_ref.at[pl.ds((WINDOW + shift) * len(members), number)]

    def send_block(shift):
        pltpu.make_async_remote_copy(
            src_ref=block(0),
            dst_ref=block(-shift),
            send_sem=row_send.at[WINDOW + shift],
            recv_sem=row_recv.at[WINDOW - shift],
            device_id=target(shift, members[0]),
            device_id_type=MESH,
        ).start()

    right = (state, reps_of[1])
    left = (state, reps_of[3])
    width = held // CHUNKS

    def piece(ref, chunk):
        return ref.at[:, pl.ds(chunk * width, width)]

    def bulk(source, owner, chunk, target, send_sem, recv_sem):
        return pltpu.make_async_remote_copy(
            src_ref=piece(source, chunk),
            dst_ref=piece(all_ref.at[owner], chunk),
            send_sem=send_sem.at[chunk],
            recv_sem=recv_sem.at[chunk],
            device_id=target,
            device_id_type=MESH,
        )

    half = CHUNKS // 2
    to_right = [bulk(ens_ref, rep, c, right, send_right, recv_left) for c in range(CHUNKS)]
    to_left = [bulk(ens_ref, rep, c, left, send_left, recv_right) for c in range(CHUNKS)]
    for step in range(CHUNKS):
        to_right[step].start()
        to_left[(step + half) % CHUNKS].start()

    own.wait()
    nearby = block(0, len(beside))
    pltpu.make_async_copy(nearby, nearby, near_recv).wait()
    for n in shifts:

        @pl.when(earlier[n])
        def _(n=n):
            send_block(n)

    smalls[1].wait()
    smalls[2].wait()
    shards = iota((8, TILE), 1)
    first = shards * held
    zeros = jnp.zeros((8, TILE), jnp.int32)
    blank = jnp.zeros((1, TILE), jnp.int32)
    index = iota((1, TILE), 1)
    own_low = state * held - REACH
    own_high = state * held + held + REACH

    def relate(i, carry):
        lows, highs, count, far, low, high, total, direct, spots, slots, obs, touch, vals, errs = carry
        j = NOBS - 1 - i
        spot = loc_ref[j]
        near = (spot >= lows) & (spot <= highs)
        away = jnp.abs((spot >> 13) - (shards >> 1)) > WINDOW
        count = count + ((spot >> 12) == shards).astype(jnp.int32)
        far = jnp.where((near & away) | (count > SLOTS), 1, far)
        lows = jnp.where(near, jnp.minimum(lows, spot - LINK), lows)
        highs = jnp.where(near, jnp.maximum(highs, spot + LINK), highs)
        here = (spot >= low) & (spot <= high)
        low = jnp.where(here, jnp.minimum(low, spot - LINK), low)
        high = jnp.where(here, jnp.maximum(high, spot + LINK), high)
        touches = (spot >= own_low) & (spot <= own_high)
        slots = slots + ((spots >> 12) == (spot >> 12)).astype(jnp.int32)
        place = index == jnp.where(here, total, -1)
        spots = jnp.where(place, spot, spots)
        slots = jnp.where(place, 0, slots)
        obs = jnp.where(place, j, obs)
        vals = jnp.where(place, val_ref[j], vals)
        errs = jnp.where(place, err_ref[j], errs)
        touch = jnp.where(index == jnp.where(touches, direct, -1), total, touch)
        total = total + here.astype(jnp.int32)
        direct = direct + touches.astype(jnp.int32)
        return lows, highs, count, far, low, high, total, direct, spots, slots, obs, touch, vals, errs

    nothing = jnp.zeros((1, TILE), jnp.float32)
    related = lax.fori_loop(
        0,
        NOBS,
        relate,
        (
            first - REACH, first + held + REACH, zeros, zeros, own_low, own_high,
            jnp.int32(0), jnp.int32(0), blank - held, blank, blank, blank, nothing, nothing,
        ),
        unroll=4,
    )
    far, total, direct, spots, slots, obs, touch, vals, errs = (related[3],) + related[6:]
    far_ref[0, 0] = jnp.max(far)
    base = (((spots >> 13) - chip + WINDOW) * CORES + ((spots >> 12) & 1)) * REPS
    totals = jnp.where(index == 0, total, direct)
    columns = (spots, base, slots * part_rows, obs, touch, totals)
    for number, column in enumerate(columns):
        table_ref[number : number + 1, :] = column.astype(jnp.float32)
    table_ref[6:7, :] = vals
    table_ref[7:8, :] = errs
    outs = [
        pltpu.make_async_copy(far_ref, far_out, small_sem.at[3]),
        pltpu.make_async_copy(table_ref, table_out, small_sem.at[4]),
    ]
    for out in outs:
        out.start()

    relays = []
    for step in range(half):
        to_right[step].wait_recv()
        relay = bulk(all_ref.at[left[1]], left[1], step, right, pass_right, far_left)
        relay.start()
        relays.append(relay)
        to_left[half + step].wait_recv()
        relay = bulk(all_ref.at[right[1]], right[1], half + step, left, pass_left, far_right)
        relay.start()
        relays.append(relay)

    for n in shifts:

        @pl.when(later[n])
        def _(n=n):
            pl.semaphore_wait(late_sem.at[WINDOW + n], 1)
            send_block(n)

    for step in range(half):
        to_right[half + step].wait_recv()
        to_left[step].wait_recv()
    for relay in relays:
        relay.wait()
    for copy in to_right + to_left:
        copy.wait_send()
    pltpu.make_async_copy(nearby, nearby, near_send).wait()
    block_copy.wait()
    for out in outs:
        out.wait()

    for n in shifts:

        @pl.when(valid[n])
        def _(n=n):
            pltpu.make_async_copy(block(n), block(n), row_send.at[WINDOW + n]).wait()
            pltpu.make_async_copy(block(n), block(n), row_recv.at[WINDOW + n]).wait()


def gather(mesh, ensemble, locations, values, errors):
    part_rows, held = ensemble.shape
    dma = pltpu.SemaphoreType.DMA
    return pl.pallas_call(
        functools.partial(gather_kernel, mesh.shape["state"] // CORES, held),
        out_shape=(
            jax.ShapeDtypeStruct((ROWS, 1, TILE), jnp.float32),
            jax.ShapeDtypeStruct((REPS, part_rows, held), jnp.float32),
            jax.ShapeDtypeStruct((8, TILE), jnp.float32),
            jax.ShapeDtypeStruct((1, 1), jnp.int32),
        ),
        in_specs=[pl.BlockSpec(memory_space=pl.ANY)] * 4,
        out_specs=(pl.BlockSpec(memory_space=pl.ANY),) * 4,
        scratch_shapes=[
            pltpu.SMEM((NOBS,), jnp.int32),
            pltpu.SMEM((NOBS,), jnp.float32),
            pltpu.SMEM((NOBS,), jnp.float32),
            pltpu.SMEM((1, 1), jnp.int32),
            pltpu.VMEM((8, TILE), jnp.float32),
            dma((5,)), dma,
            pltpu.VMEM((part_rows, held), jnp.float32),
            pltpu.VMEM((held // TILE, part_rows, TILE), jnp.float32),
            pltpu.VMEM((1, 1, TILE), jnp.float32),
            dma, dma, pltpu.SemaphoreType.REGULAR((2 * WINDOW + 1,)),
            dma, dma, dma((2 * WINDOW + 1,)), dma((2 * WINDOW + 1,)),
            dma((CHUNKS,)), dma((CHUNKS,)), dma((CHUNKS,)), dma((CHUNKS,)),
            dma((CHUNKS,)), dma((CHUNKS,)), dma((CHUNKS,)), dma((CHUNKS,)),
        ],
        compiler_params=pltpu.CompilerParams(collective_id=0, has_side_effects=True),
        name="gather",
    )(locations, values, errors, ensemble)


def solve_kernel(
    windowed, held, table_ref, rows_ref, all_ref, out_ref,
    y_ref, u_ref, w_ref, center_ref, mutual_ref, tile_ref,
):
    state = lax.axis_index("state")
    rep = lax.axis_index("rep")
    part_rows = all_ref.shape[1]
    order = [(rep + step) & (REPS - 1) for step in range(REPS)]

    def entry(number, t):
        return table_ref[number, t].astype(jnp.int32)

    total = entry(5, 0)
    direct = entry(5, 1)
    diagonal = iota((part_rows, TILE), 1) - iota((part_rows, TILE), 0)

    def spread(t, carry):
        spot = entry(0, t)
        if windowed:
            base = entry(1, t)
            place = entry(2, t)
        else:
            base = entry(3, t) * REPS
            place = 0
        for step in range(REPS):
            row = jnp.broadcast_to(rows_ref[base + order[step]], (part_rows, TILE))
            column = jnp.sum(jnp.where(diagonal == place, row, 0.0), axis=1, keepdims=True)
            y_ref[t, step * part_rows : (step + 1) * part_rows, :] = jnp.broadcast_to(
                column, (part_rows, TILE)
            )
        center = (spot // TILE * TILE).astype(jnp.float32) + (TILE - 1) * 0.5
        center_ref[pl.ds(t, 1), :] = jnp.full((1, TILE), center, jnp.float32)
        return carry

    lax.fori_loop(0, total, spread, 0)

    tiles = held // TILE
    tile_centers = (state * held + iota((tiles, TILE), 0) * TILE).astype(jnp.float32) + (
        TILE - 1
    ) * 0.5

    def assimilate(i, carry):
        t = total - 1 - i
        spot = table_ref[0, t]
        error = table_ref[7, t]
        y = y_ref[t]
        mean = jnp.sum(y, axis=0, keepdims=True) * (1.0 / M)
        spread_of = y - mean
        variance = jnp.sum(spread_of * spread_of, axis=0, keepdims=True) * (1.0 / (M - 1))
        total_var = variance + error
        shrink = 1.0 / (1.0 + jnp.sqrt(error / total_var))
        u = spread_of * (1.0 / ((M - 1) * total_var))
        w = (table_ref[6, t] - mean) - shrink * spread_of
        u_ref[t] = u
        w_ref[t] = w
        mutual_ref[...] = taper(jnp.abs(center_ref[...] - spot))
        tile_ref[t] = taper(jnp.abs(tile_centers - spot))

        def update(k, inner):
            other = y_ref[k]
            projected = jnp.sum(u * other, axis=0, keepdims=True)
            y_ref[k] = other + w * (mutual_ref[pl.ds(k, 1), :] * projected)
            return inner

        lax.fori_loop(0, t, update, 0)
        return carry

    lax.fori_loop(0, total, assimilate, 0)
    group = 4

    def apply(g, carry):
        spans = [
            pl.ds(pl.multiple_of((g * group + i) * TILE, TILE), TILE) for i in range(group)
        ]

        def one(d, values):
            t = entry(4, direct - 1 - d)
            u = u_ref[t]
            w = w_ref[t]
            result = []
            for i in range(group):
                projected = jnp.sum(u * values[i], axis=0, keepdims=True)
                weight = tile_ref[t, pl.ds(g * group + i, 1), :]
                result.append(values[i] + w * (weight * projected))
            return tuple(result)

        start = tuple(
            jnp.concatenate([all_ref[member, :, span] for member in order], axis=0)
            for span in spans
        )
        values = lax.fori_loop(0, direct, one, start)
        for span, value in zip(spans, values):
            out_ref[:, span] = value[:part_rows]
        return carry

    lax.fori_loop(0, tiles // group, apply, 0)


def solve(windowed, part_rows, held, table, rows, everything):
    vmem = pl.BlockSpec(memory_space=pltpu.VMEM)
    block = pltpu.VMEM((NOBS, M, TILE), jnp.float32)
    return pl.pallas_call(
        functools.partial(solve_kernel, windowed, held),
        out_shape=jax.ShapeDtypeStruct((part_rows, held), jnp.float32),
        in_specs=[pl.BlockSpec(memory_space=pltpu.SMEM), vmem, vmem],
        out_specs=vmem,
        scratch_shapes=[
            block, block, block,
            pltpu.VMEM((NOBS, TILE), jnp.float32),
            pltpu.VMEM((NOBS, TILE), jnp.float32),
            pltpu.VMEM((NOBS, held // TILE, TILE), jnp.float32),
        ],
        name="solve",
    )(table, rows, everything)


def full_rows(mesh, ensemble, locations):
    part_rows, held = ensemble.shape
    states = mesh.shape["state"]
    offsets = locations - lax.axis_index("state") * held
    inside = ((offsets >= 0) & (offsets < held)).astype(jnp.float32)
    columns = jnp.take(ensemble, jnp.clip(offsets, 0, held - 1), axis=1) * inside[None, :]
    placed = jnp.zeros((REPS, part_rows, NOBS), jnp.float32)
    placed = lax.dynamic_update_slice(placed, columns[None], (lax.axis_index("rep"), 0, 0))
    stride = 1
    while stride < states:
        pairs = [(i, i ^ stride) for i in range(states)]
        placed = placed + lax.ppermute(placed, "state", pairs)
        stride *= 2
    stride = 1
    while stride < REPS:
        pairs = [(i, i ^ stride) for i in range(REPS)]
        placed = placed + lax.ppermute(placed, "rep", pairs)
        stride *= 2
    by_obs = jnp.transpose(placed, (2, 0, 1)).reshape(NOBS * REPS, 1, part_rows)
    return jnp.pad(by_obs, ((0, 0), (0, 0), (0, TILE - part_rows)))


def on_device(mesh, ensemble, obs_values, obs_error, obs_location):
    part_rows, held = ensemble.shape
    rows, everything, table, far = gather(mesh, ensemble, obs_location, obs_values, obs_error)
    return lax.cond(
        far[0, 0] == 0,
        lambda: solve(True, part_rows, held, table, rows, everything),
        lambda: solve(
            False, part_rows, held, table, full_rows(mesh, ensemble, obs_location), everything
        ),
    )


def solution(mesh):
    in_specs = (P("rep", "state"), P(), P(), P())
    out_specs = P("rep", "state")
    return jax.shard_map(
        functools.partial(on_device, mesh),
        mesh=mesh,
        in_specs=in_specs,
        out_specs=out_specs,
        check_vma=False,
    )
```

```python
import functools

import jax
import jax.numpy as jnp
from jax import lax
from jax.experimental import pallas as pl
from jax.experimental.pallas import tpu as pltpu
from jax.sharding import PartitionSpec as P

MESH = pl.DeviceIdType.MESH
M = 64
TILE = 128
HALF = 4096
REACH = 2 * HALF
LINK = REACH + TILE // 2
NOBS = 48
REPS = 4
CORES = 2
WINDOW = 4
DEPTH = 16
SLOTS = 8
CHUNKS = 4
ROWS = (2 * WINDOW + 1) * CORES * REPS


def taper(distance):
    ratio = distance * (1.0 / HALF)
    near_part = (((-0.25 * ratio + 0.5) * ratio + 0.625) * ratio - 5.0 / 3.0) * ratio * ratio + 1.0
    ratio_far = jnp.maximum(ratio, 1.0)
    far_part = (
        ((((ratio_far / 12.0 - 0.5) * ratio_far + 0.625) * ratio_far + 5.0 / 3.0) * ratio_far - 5.0)
        * ratio_far
        + 4.0
        - 2.0 / (3.0 * ratio_far)
    )
    return jnp.where(
        ratio <= 1.0, near_part, jnp.where(ratio < 2.0, far_part, jnp.zeros_like(ratio))
    )


def iota(shape, axis):
    return lax.broadcasted_iota(jnp.int32, shape, axis)


def gather_kernel(
    chips, held, loc_any, val_any, err_any, ens_ref, rows_ref, all_ref, table_out, far_out,
    loc_ref, val_ref, err_ref, far_ref, table_ref, small_sem, block_sem, fetch_ref, local_ref, pick_ref, local_sem, own_sem, late_sem, near_send, near_recv, row_send, row_recv,
    send_right, send_left, recv_left, recv_right, pass_right, pass_left, far_left, far_right,
):
    state = lax.axis_index("state")
    rep = lax.axis_index("rep")
    chip = state >> 1
    core = state & 1
    part_rows = ens_ref.shape[0]
    tiles = held // TILE

    load = pltpu.make_async_copy(ens_ref, fetch_ref, local_sem)
    load.start()
    smalls = [
        pltpu.make_async_copy(loc_any, loc_ref, small_sem.at[0]),
        pltpu.make_async_copy(val_any, val_ref, small_sem.at[1]),
        pltpu.make_async_copy(err_any, err_ref, small_sem.at[2]),
    ]
    for small in smalls:
        small.start()

    depth = chip & (DEPTH - 1)
    shifts = list(range(1, WINDOW + 1)) + list(range(-1, -WINDOW - 1, -1))
    valid = {n: (chip + n >= 0) & (chip + n < chips) for n in shifts}

    def key(place):
        return place + jnp.where((place >> 2) == 2, DEPTH, 0)

    ahead = {n: key((depth + n) & (DEPTH - 1)) > key(depth) for n in shifts}
    later = {n: valid[n] & ahead[n] for n in shifts}
    earlier = {n: valid[n] & jnp.logical_not(ahead[n]) for n in shifts}
    members = [(c, r) for c in range(CORES) for r in range(REPS)]
    beside = members[1:]
    cores_of = [core, 1 - core]
    reps_of = [(rep + r) & (REPS - 1) for r in range(REPS)]

    def target(shift, member):
        return (chip + shift) * CORES + cores_of[member[0]], reps_of[member[1]]

    def signal(semaphore, shift, member):
        pl.semaphore_signal(
            semaphore, inc=1, device_id=target(shift, member), device_id_type=MESH
        )

    def count_of(flags):
        return sum(flags[n].astype(jnp.int32) for n in shifts)

    right = (state, reps_of[1])
    left = (state, reps_of[3])
    width = held // CHUNKS

    def piece(ref, chunk):
        return ref.at[:, pl.ds(chunk * width, width)]

    def bulk(source, owner, chunk, target, send_sem, recv_sem):
        return pltpu.make_async_remote_copy(
            src_ref=piece(source, chunk),
            dst_ref=piece(all_ref.at[owner], chunk),
            send_sem=send_sem.at[chunk],
            recv_sem=recv_sem.at[chunk],
            device_id=target,
            device_id_type=MESH,
        )

    half = CHUNKS // 2
    to_right = [bulk(ens_ref, rep, c, right, send_right, recv_left) for c in range(CHUNKS)]
    to_left = [bulk(ens_ref, rep, c, left, send_left, recv_right) for c in range(CHUNKS)]
    barrier = pltpu.get_barrier_semaphore()
    wraps = {n: valid[n] & (((chip + n) & ~(DEPTH - 1)) != (chip & ~(DEPTH - 1))) for n in shifts}
    greetings = (
        len(beside)
        + count_of(earlier)
        + (len(members) - 1) * count_of({n: earlier[n] & wraps[n] for n in shifts})
    )
    for member in beside:
        signal(barrier, 0, member)
    for n in shifts:

        @pl.when(later[n])
        def _(n=n):
            signal(barrier, n, members[0])

    for n in shifts:

        @pl.when(later[n] & wraps[n])
        def _(n=n):
            for member in beside:
                signal(barrier, n, member)

    smalls[0].wait()
    load.wait()
    block_copy = pltpu.make_async_copy(fetch_ref, all_ref.at[rep], block_sem)
    block_copy.start()
    for tile in range(tiles):
        local_ref[tile] = fetch_ref[:, tile * TILE : (tile + 1) * TILE]
    lane = iota((part_rows, TILE), 1)
    diagonal = lane - iota((part_rows, TILE), 0)
    rank = jnp.int32(0)
    packed = jnp.zeros((part_rows, TILE), jnp.float32)
    for j in range(NOBS):
        offset = loc_ref[j] - state * held
        inside = (offset >= 0) & (offset < held)
        safe = jnp.clip(offset, 0, held - 1)
        tile = local_ref[safe >> 7]
        wanted = jnp.where(inside, safe & (TILE - 1), -1)
        column = jnp.sum(jnp.where(lane == wanted, tile, 0.0), axis=1, keepdims=True)
        place = jnp.where(inside, rank * part_rows, -TILE * 2)
        packed = jnp.where(diagonal == place, column, packed)
        rank = rank + inside.astype(jnp.int32)
    pick_ref[0] = jnp.sum(packed, axis=0, keepdims=True)

    pl.semaphore_wait(barrier, greetings)

    def send_row(shift, member):
        slot = ((WINDOW - shift) * CORES + core) * REPS + rep
        pltpu.make_async_remote_copy(
            src_ref=pick_ref.at[0],
            dst_ref=rows_ref.at[slot],
            send_sem=row_send.at[WINDOW + shift],
            recv_sem=row_recv.at[WINDOW - shift],
            device_id=target(shift, member),
            device_id_type=MESH,
        ).start()

    for n in range(WINDOW, 0, -1):

        @pl.when(earlier[n] & wraps[n])
        def _(n=n):
            for member in members:
                send_row(n, member)

    own_row = (WINDOW * CORES + core) * REPS + rep
    for member in beside:
        pltpu.make_async_remote_copy(
            src_ref=pick_ref.at[0],
            dst_ref=rows_ref.at[own_row],
            send_sem=near_send,
            recv_sem=near_recv,
            device_id=target(0, member),
            device_id_type=MESH,
        ).start()
    own = pltpu.make_async_copy(pick_ref.at[0], rows_ref.at[own_row], own_sem)
    own.start()
    for n in shifts:

        @pl.when(earlier[n])
        def _(n=n):
            signal(late_sem.at[WINDOW - n], n, members[0])

    def block(shift, number=len(members)):
        return rows_ref.at[pl.ds((WINDOW + shift) * len(members), number)]

    def send_block(shift):
        pltpu.make_async_remote_copy(
            src_ref=block(0),
            dst_ref=block(-shift),
            send_sem=row_send.at[WINDOW + shift],
            recv_sem=row_recv.at[WINDOW - shift],
            device_id=target(shift, members[0]),
            device_id_type=MESH,
        ).start()

    for step in range(CHUNKS):
        to_right[step].start()
        to_left[(step + half) % CHUNKS].start()

    own.wait()
    nearby = block(0, len(beside))
    pltpu.make_async_copy(nearby, nearby, near_recv).wait()
    for n in shifts:

        @pl.when(earlier[n] & jnp.logical_not(wraps[n]))
        def _(n=n):
            send_block(n)

    smalls[1].wait()
    smalls[2].wait()
    shards = iota((8, TILE), 1)
    first = shards * held
    zeros = jnp.zeros((8, TILE), jnp.int32)
    blank = jnp.zeros((1, TILE), jnp.int32)
    index = iota((1, TILE), 1)
    own_low = state * held - REACH
    own_high = state * held + held + REACH

    def relate(i, carry):
        lows, highs, count, far, low, high, total, direct, spots, slots, obs, touch, vals, errs = carry
        j = NOBS - 1 - i
        spot = loc_ref[j]
        near = (spot >= lows) & (spot <= highs)
        away = jnp.abs((spot >> 13) - (shards >> 1)) > WINDOW
        count = count + ((spot >> 12) == shards).astype(jnp.int32)
        far = jnp.where((near & away) | (count > SLOTS), 1, far)
        lows = jnp.where(near, jnp.minimum(lows, spot - LINK), lows)
        highs = jnp.where(near, jnp.maximum(highs, spot + LINK), highs)
        here = (spot >= low) & (spot <= high)
        low = jnp.where(here, jnp.minimum(low, spot - LINK), low)
        high = jnp.where(here, jnp.maximum(high, spot + LINK), high)
        touches = (spot >= own_low) & (spot <= own_high)
        slots = slots + ((spots >> 12) == (spot >> 12)).astype(jnp.int32)
        place = index == jnp.where(here, total, -1)
        spots = jnp.where(place, spot, spots)
        slots = jnp.where(place, 0, slots)
        obs = jnp.where(place, j, obs)
        vals = jnp.where(place, val_ref[j], vals)
        errs = jnp.where(place, err_ref[j], errs)
        touch = jnp.where(index == jnp.where(touches, direct, -1), total, touch)
        total = total + here.astype(jnp.int32)
        direct = direct + touches.astype(jnp.int32)
        return lows, highs, count, far, low, high, total, direct, spots, slots, obs, touch, vals, errs

    nothing = jnp.zeros((1, TILE), jnp.float32)
    related = lax.fori_loop(
        0,
        NOBS,
        relate,
        (
            first - REACH, first + held + REACH, zeros, zeros, own_low, own_high,
            jnp.int32(0), jnp.int32(0), blank - held, blank, blank, blank, nothing, nothing,
        ),
        unroll=4,
    )
    far, total, direct, spots, slots, obs, touch, vals, errs = (related[3],) + related[6:]
    far_ref[0, 0] = jnp.max(far)
    base = (((spots >> 13) - chip + WINDOW) * CORES + ((spots >> 12) & 1)) * REPS
    totals = jnp.where(index == 0, total, direct)
    columns = (spots, base, slots * part_rows, obs, touch, totals)
    for number, column in enumerate(columns):
        table_ref[number : number + 1, :] = column.astype(jnp.float32)
    table_ref[6:7, :] = vals
    table_ref[7:8, :] = errs
    outs = [
        pltpu.make_async_copy(far_ref, far_out, small_sem.at[3]),
        pltpu.make_async_copy(table_ref, table_out, small_sem.at[4]),
    ]
    for out in outs:
        out.start()

    relays = []
    for step in range(half):
        to_right[step].wait_recv()
        relay = bulk(all_ref.at[left[1]], left[1], step, right, pass_right, far_left)
        relay.start()
        relays.append(relay)
        to_left[half + step].wait_recv()
        relay = bulk(all_ref.at[right[1]], right[1], half + step, left, pass_left, far_right)
        relay.start()
        relays.append(relay)

    for n in shifts:

        @pl.when(later[n])
        def _(n=n):
            pl.semaphore_wait(late_sem.at[WINDOW + n], 1)
            send_block(n)

    for step in range(half):
        to_right[half + step].wait_recv()
        to_left[step].wait_recv()
    for relay in relays:
        relay.wait()
    for copy in to_right + to_left:
        copy.wait_send()
    pltpu.make_async_copy(nearby, nearby, near_send).wait()
    block_copy.wait()
    for out in outs:
        out.wait()

    for n in shifts:

        @pl.when(valid[n])
        def _(n=n):
            pltpu.make_async_copy(block(n), block(n), row_send.at[WINDOW + n]).wait()
            pltpu.make_async_copy(block(n), block(n), row_recv.at[WINDOW + n]).wait()


def gather(mesh, ensemble, locations, values, errors):
    part_rows, held = ensemble.shape
    dma = pltpu.SemaphoreType.DMA
    return pl.pallas_call(
        functools.partial(gather_kernel, mesh.shape["state"] // CORES, held),
        out_shape=(
            jax.ShapeDtypeStruct((ROWS, 1, TILE), jnp.float32),
            jax.ShapeDtypeStruct((REPS, part_rows, held), jnp.float32),
            jax.ShapeDtypeStruct((8, TILE), jnp.float32),
            jax.ShapeDtypeStruct((1, 1), jnp.int32),
        ),
        in_specs=[pl.BlockSpec(memory_space=pl.ANY)] * 4,
        out_specs=(pl.BlockSpec(memory_space=pl.ANY),) * 4,
        scratch_shapes=[
            pltpu.SMEM((NOBS,), jnp.int32),
            pltpu.SMEM((NOBS,), jnp.float32),
            pltpu.SMEM((NOBS,), jnp.float32),
            pltpu.SMEM((1, 1), jnp.int32),
            pltpu.VMEM((8, TILE), jnp.float32),
            dma((5,)), dma,
            pltpu.VMEM((part_rows, held), jnp.float32),
            pltpu.VMEM((held // TILE, part_rows, TILE), jnp.float32),
            pltpu.VMEM((1, 1, TILE), jnp.float32),
            dma, dma, pltpu.SemaphoreType.REGULAR((2 * WINDOW + 1,)),
            dma, dma, dma((2 * WINDOW + 1,)), dma((2 * WINDOW + 1,)),
            dma((CHUNKS,)), dma((CHUNKS,)), dma((CHUNKS,)), dma((CHUNKS,)),
            dma((CHUNKS,)), dma((CHUNKS,)), dma((CHUNKS,)), dma((CHUNKS,)),
        ],
        compiler_params=pltpu.CompilerParams(collective_id=0, has_side_effects=True),
        name="gather",
    )(locations, values, errors, ensemble)


def solve_kernel(
    windowed, held, table_ref, rows_ref, all_ref, out_ref,
    y_ref, u_ref, w_ref, center_ref, mutual_ref, tile_ref,
):
    state = lax.axis_index("state")
    rep = lax.axis_index("rep")
    part_rows = all_ref.shape[1]
    order = [(rep + step) & (REPS - 1) for step in range(REPS)]

    def entry(number, t):
        return table_ref[number, t].astype(jnp.int32)

    total = entry(5, 0)
    direct = entry(5, 1)
    diagonal = iota((part_rows, TILE), 1) - iota((part_rows, TILE), 0)

    def spread(t, carry):
        spot = entry(0, t)
        if windowed:
            base = entry(1, t)
            place = entry(2, t)
        else:
            base = entry(3, t) * REPS
            place = 0
        for step in range(REPS):
            row = jnp.broadcast_to(rows_ref[base + order[step]], (part_rows, TILE))
            column = jnp.sum(jnp.where(diagonal == place, row, 0.0), axis=1, keepdims=True)
            y_ref[t, step * part_rows : (step + 1) * part_rows, :] = jnp.broadcast_to(
                column, (part_rows, TILE)
            )
        center = (spot // TILE * TILE).astype(jnp.float32) + (TILE - 1) * 0.5
        center_ref[pl.ds(t, 1), :] = jnp.full((1, TILE), center, jnp.float32)
        return carry

    lax.fori_loop(0, total, spread, 0)

    tiles = held // TILE
    tile_centers = (state * held + iota((tiles, TILE), 0) * TILE).astype(jnp.float32) + (
        TILE - 1
    ) * 0.5

    def assimilate(i, carry):
        t = total - 1 - i
        spot = table_ref[0, t]
        error = table_ref[7, t]
        y = y_ref[t]
        mean = jnp.sum(y, axis=0, keepdims=True) * (1.0 / M)
        spread_of = y - mean
        variance = jnp.sum(spread_of * spread_of, axis=0, keepdims=True) * (1.0 / (M - 1))
        total_var = variance + error
        shrink = 1.0 / (1.0 + jnp.sqrt(error / total_var))
        u = spread_of * (1.0 / ((M - 1) * total_var))
        w = (table_ref[6, t] - mean) - shrink * spread_of
        u_ref[t] = u
        w_ref[t] = w
        mutual_ref[...] = taper(jnp.abs(center_ref[...] - spot))
        tile_ref[t] = taper(jnp.abs(tile_centers - spot))

        def update(k, inner):
            other = y_ref[k]
            projected = jnp.sum(u * other, axis=0, keepdims=True)
            y_ref[k] = other + w * (mutual_ref[pl.ds(k, 1), :] * projected)
            return inner

        lax.fori_loop(0, t, update, 0)
        return carry

    lax.fori_loop(0, total, assimilate, 0)
    group = 4

    def apply(g, carry):
        spans = [
            pl.ds(pl.multiple_of((g * group + i) * TILE, TILE), TILE) for i in range(group)
        ]

        def one(d, values):
            t = entry(4, direct - 1 - d)
            u = u_ref[t]
            w = w_ref[t]
            result = []
            for i in range(group):
                projected = jnp.sum(u * values[i], axis=0, keepdims=True)
                weight = tile_ref[t, pl.ds(g * group + i, 1), :]
                result.append(values[i] + w * (weight * projected))
            return tuple(result)

        start = tuple(
            jnp.concatenate([all_ref[member, :, span] for member in order], axis=0)
            for span in spans
        )
        values = lax.fori_loop(0, direct, one, start)
        for span, value in zip(spans, values):
            out_ref[:, span] = value[:part_rows]
        return carry

    lax.fori_loop(0, tiles // group, apply, 0)


def solve(windowed, part_rows, held, table, rows, everything):
    vmem = pl.BlockSpec(memory_space=pltpu.VMEM)
    block = pltpu.VMEM((NOBS, M, TILE), jnp.float32)
    return pl.pallas_call(
        functools.partial(solve_kernel, windowed, held),
        out_shape=jax.ShapeDtypeStruct((part_rows, held), jnp.float32),
        in_specs=[pl.BlockSpec(memory_space=pltpu.SMEM), vmem, vmem],
        out_specs=vmem,
        scratch_shapes=[
            block, block, block,
            pltpu.VMEM((NOBS, TILE), jnp.float32),
            pltpu.VMEM((NOBS, TILE), jnp.float32),
            pltpu.VMEM((NOBS, held // TILE, TILE), jnp.float32),
        ],
        name="solve",
    )(table, rows, everything)


def full_rows(mesh, ensemble, locations):
    part_rows, held = ensemble.shape
    states = mesh.shape["state"]
    offsets = locations - lax.axis_index("state") * held
    inside = ((offsets >= 0) & (offsets < held)).astype(jnp.float32)
    columns = jnp.take(ensemble, jnp.clip(offsets, 0, held - 1), axis=1) * inside[None, :]
    placed = jnp.zeros((REPS, part_rows, NOBS), jnp.float32)
    placed = lax.dynamic_update_slice(placed, columns[None], (lax.axis_index("rep"), 0, 0))
    stride = 1
    while stride < states:
        pairs = [(i, i ^ stride) for i in range(states)]
        placed = placed + lax.ppermute(placed, "state", pairs)
        stride *= 2
    stride = 1
    while stride < REPS:
        pairs = [(i, i ^ stride) for i in range(REPS)]
        placed = placed + lax.ppermute(placed, "rep", pairs)
        stride *= 2
    by_obs = jnp.transpose(placed, (2, 0, 1)).reshape(NOBS * REPS, 1, part_rows)
    return jnp.pad(by_obs, ((0, 0), (0, 0), (0, TILE - part_rows)))


def on_device(mesh, ensemble, obs_values, obs_error, obs_location):
    part_rows, held = ensemble.shape
    rows, everything, table, far = gather(mesh, ensemble, obs_location, obs_values, obs_error)
    return lax.cond(
        far[0, 0] == 0,
        lambda: solve(True, part_rows, held, table, rows, everything),
        lambda: solve(
            False, part_rows, held, table, full_rows(mesh, ensemble, obs_location), everything
        ),
    )


def solution(mesh):
    in_specs = (P("rep", "state"), P(), P(), P())
    out_specs = P("rep", "state")
    return jax.shard_map(
        functools.partial(on_device, mesh),
        mesh=mesh,
        in_specs=in_specs,
        out_specs=out_specs,
        check_vma=False,
    )
```

```python
import functools

import jax
import jax.numpy as jnp
from jax import lax
from jax.experimental import pallas as pl
from jax.experimental.pallas import tpu as pltpu
from jax.sharding import PartitionSpec as P

MESH = pl.DeviceIdType.MESH
M = 64
TILE = 128
HALF = 4096
REACH = 2 * HALF
LINK = REACH + TILE // 2
NOBS = 48
REPS = 4
CORES = 2
WINDOW = 4
DEPTH = 16
SLOTS = 8
CHUNKS = 4
ROWS = (2 * WINDOW + 1) * CORES * REPS


def taper(distance):
    ratio = distance * (1.0 / HALF)
    near_part = (((-0.25 * ratio + 0.5) * ratio + 0.625) * ratio - 5.0 / 3.0) * ratio * ratio + 1.0
    ratio_far = jnp.maximum(ratio, 1.0)
    far_part = (
        ((((ratio_far / 12.0 - 0.5) * ratio_far + 0.625) * ratio_far + 5.0 / 3.0) * ratio_far - 5.0)
        * ratio_far
        + 4.0
        - 2.0 / (3.0 * ratio_far)
    )
    return jnp.where(
        ratio <= 1.0, near_part, jnp.where(ratio < 2.0, far_part, jnp.zeros_like(ratio))
    )


def iota(shape, axis):
    return lax.broadcasted_iota(jnp.int32, shape, axis)


def gather_kernel(
    chips, held, loc_any, val_any, err_any, ens_ref, rows_ref, all_ref, table_out, far_out,
    loc_ref, val_ref, err_ref, far_ref, table_ref, small_sem, block_sem, fetch_ref, local_ref, pick_ref, local_sem, own_sem, late_sem, near_send, near_recv, row_send, row_recv,
    send_right, send_left, recv_left, recv_right, pass_right, pass_left, far_left, far_right,
):
    state = lax.axis_index("state")
    rep = lax.axis_index("rep")
    chip = state >> 1
    core = state & 1
    part_rows = ens_ref.shape[0]
    tiles = held // TILE

    load = pltpu.make_async_copy(ens_ref, fetch_ref, local_sem)
    load.start()
    smalls = [
        pltpu.make_async_copy(loc_any, loc_ref, small_sem.at[0]),
        pltpu.make_async_copy(val_any, val_ref, small_sem.at[1]),
        pltpu.make_async_copy(err_any, err_ref, small_sem.at[2]),
    ]
    for small in smalls:
        small.start()

    depth = chip & (DEPTH - 1)
    shifts = list(range(1, WINDOW + 1)) + list(range(-1, -WINDOW - 1, -1))
    valid = {n: (chip + n >= 0) & (chip + n < chips) for n in shifts}

    def key(place):
        return place + jnp.where((place >> 2) == 2, DEPTH, 0)

    ahead = {n: key((depth + n) & (DEPTH - 1)) > key(depth) for n in shifts}
    later = {n: valid[n] & ahead[n] for n in shifts}
    earlier = {n: valid[n] & jnp.logical_not(ahead[n]) for n in shifts}
    members = [(c, r) for c in range(CORES) for r in range(REPS)]
    beside = members[1:]
    peers = members[1:REPS]
    pair = members[REPS]
    cores_of = [core, 1 - core]
    reps_of = [(rep + r) & (REPS - 1) for r in range(REPS)]

    def target(shift, member):
        return (chip + shift) * CORES + cores_of[member[0]], reps_of[member[1]]

    def signal(semaphore, shift, member):
        pl.semaphore_signal(
            semaphore, inc=1, device_id=target(shift, member), device_id_type=MESH
        )

    def count_of(flags):
        return sum(flags[n].astype(jnp.int32) for n in shifts)

    right = (state, reps_of[1])
    left = (state, reps_of[3])
    width = held // CHUNKS

    def piece(ref, chunk):
        return ref.at[:, pl.ds(chunk * width, width)]

    def bulk(source, owner, chunk, target, send_sem, recv_sem):
        return pltpu.make_async_remote_copy(
            src_ref=piece(source, chunk),
            dst_ref=piece(all_ref.at[owner], chunk),
            send_sem=send_sem.at[chunk],
            recv_sem=recv_sem.at[chunk],
            device_id=target,
            device_id_type=MESH,
        )

    half = CHUNKS // 2
    to_right = [bulk(ens_ref, rep, c, right, send_right, recv_left) for c in range(CHUNKS)]
    to_left = [bulk(ens_ref, rep, c, left, send_left, recv_right) for c in range(CHUNKS)]
    barrier = pltpu.get_barrier_semaphore()
    wraps = {n: valid[n] & (((chip + n) & ~(DEPTH - 1)) != (chip & ~(DEPTH - 1))) for n in shifts}
    greetings = (
        len(peers)
        + (1 - core)
        + count_of(earlier)
        + (len(members) - 1) * count_of({n: earlier[n] & wraps[n] for n in shifts})
    )
    for member in peers:
        signal(barrier, 0, member)

    @pl.when(core == 1)
    def _():
        signal(barrier, 0, pair)

    for n in shifts:

        @pl.when(later[n])
        def _(n=n):
            signal(barrier, n, members[0])

    for n in shifts:

        @pl.when(later[n] & wraps[n])
        def _(n=n):
            for member in beside:
                signal(barrier, n, member)

    smalls[0].wait()
    load.wait()
    block_copy = pltpu.make_async_copy(fetch_ref, all_ref.at[rep], block_sem)
    block_copy.start()
    for tile in range(tiles):
        local_ref[tile] = fetch_ref[:, tile * TILE : (tile + 1) * TILE]
    lane = iota((part_rows, TILE), 1)
    diagonal = lane - iota((part_rows, TILE), 0)
    rank = jnp.int32(0)
    packed = jnp.zeros((part_rows, TILE), jnp.float32)
    for j in range(NOBS):
        offset = loc_ref[j] - state * held
        inside = (offset >= 0) & (offset < held)
        safe = jnp.clip(offset, 0, held - 1)
        tile = local_ref[safe >> 7]
        wanted = jnp.where(inside, safe & (TILE - 1), -1)
        column = jnp.sum(jnp.where(lane == wanted, tile, 0.0), axis=1, keepdims=True)
        place = jnp.where(inside, rank * part_rows, -TILE * 2)
        packed = jnp.where(diagonal == place, column, packed)
        rank = rank + inside.astype(jnp.int32)
    pick_ref[0] = jnp.sum(packed, axis=0, keepdims=True)

    pl.semaphore_wait(barrier, greetings)

    def send_row(shift, member):
        slot = ((WINDOW - shift) * CORES + core) * REPS + rep
        pltpu.make_async_remote_copy(
            src_ref=pick_ref.at[0],
            dst_ref=rows_ref.at[slot],
            send_sem=row_send.at[WINDOW + shift],
            recv_sem=row_recv.at[WINDOW - shift],
            device_id=target(shift, member),
            device_id_type=MESH,
        ).start()

    for n in range(WINDOW, 0, -1):

        @pl.when(earlier[n] & wraps[n])
        def _(n=n):
            for member in members:
                send_row(n, member)

    own_row = (WINDOW * CORES + core) * REPS + rep
    for member in peers:
        pltpu.make_async_remote_copy(
            src_ref=pick_ref.at[0],
            dst_ref=rows_ref.at[own_row],
            send_sem=near_send,
            recv_sem=near_recv,
            device_id=target(0, member),
            device_id_type=MESH,
        ).start()
    own = pltpu.make_async_copy(pick_ref.at[0], rows_ref.at[own_row], own_sem)
    own.start()

    @pl.when(core == 0)
    def _():
        signal(late_sem.at[WINDOW], 0, pair)

    for n in shifts:

        @pl.when(earlier[n])
        def _(n=n):
            signal(late_sem.at[WINDOW - n], n, members[0])

    def block(shift, number=len(members)):
        return rows_ref.at[pl.ds((WINDOW + shift) * len(members), number)]

    def send_block(shift):
        pltpu.make_async_remote_copy(
            src_ref=block(0),
            dst_ref=block(-shift),
            send_sem=row_send.at[WINDOW + shift],
            recv_sem=row_recv.at[WINDOW - shift],
            device_id=target(shift, members[0]),
            device_id_type=MESH,
        ).start()

    for step in range(CHUNKS):
        to_right[step].start()
        to_left[(step + half) % CHUNKS].start()

    half_block = rows_ref.at[pl.ds(WINDOW * len(members) + core * REPS, REPS)]
    to_pair = pltpu.make_async_remote_copy(
        src_ref=half_block,
        dst_ref=half_block,
        send_sem=row_send.at[WINDOW],
        recv_sem=row_recv.at[WINDOW],
        device_id=target(0, pair),
        device_id_type=MESH,
    )
    own.wait()
    nearby = block(0, len(peers))
    pltpu.make_async_copy(nearby, nearby, near_recv).wait()

    @pl.when(core == 1)
    def _():
        pl.semaphore_wait(late_sem.at[WINDOW], 1)

    to_pair.start()
    to_pair.wait_recv()
    for n in shifts:

        @pl.when(earlier[n] & jnp.logical_not(wraps[n]))
        def _(n=n):
            send_block(n)

    smalls[1].wait()
    smalls[2].wait()
    shards = iota((8, TILE), 1)
    first = shards * held
    zeros = jnp.zeros((8, TILE), jnp.int32)
    blank = jnp.zeros((1, TILE), jnp.int32)
    index = iota((1, TILE), 1)
    own_low = state * held - REACH
    own_high = state * held + held + REACH

    def relate(i, carry):
        lows, highs, count, far, low, high, total, direct, spots, slots, obs, touch, vals, errs = carry
        j = NOBS - 1 - i
        spot = loc_ref[j]
        near = (spot >= lows) & (spot <= highs)
        away = jnp.abs((spot >> 13) - (shards >> 1)) > WINDOW
        count = count + ((spot >> 12) == shards).astype(jnp.int32)
        far = jnp.where((near & away) | (count > SLOTS), 1, far)
        lows = jnp.where(near, jnp.minimum(lows, spot - LINK), lows)
        highs = jnp.where(near, jnp.maximum(highs, spot + LINK), highs)
        here = (spot >= low) & (spot <= high)
        low = jnp.where(here, jnp.minimum(low, spot - LINK), low)
        high = jnp.where(here, jnp.maximum(high, spot + LINK), high)
        touches = (spot >= own_low) & (spot <= own_high)
        slots = slots + ((spots >> 12) == (spot >> 12)).astype(jnp.int32)
        place = index == jnp.where(here, total, -1)
        spots = jnp.where(place, spot, spots)
        slots = jnp.where(place, 0, slots)
        obs = jnp.where(place, j, obs)
        vals = jnp.where(place, val_ref[j], vals)
        errs = jnp.where(place, err_ref[j], errs)
        touch = jnp.where(index == jnp.where(touches, direct, -1), total, touch)
        total = total + here.astype(jnp.int32)
        direct = direct + touches.astype(jnp.int32)
        return lows, highs, count, far, low, high, total, direct, spots, slots, obs, touch, vals, errs

    nothing = jnp.zeros((1, TILE), jnp.float32)
    related = lax.fori_loop(
        0,
        NOBS,
        relate,
        (
            first - REACH, first + held + REACH, zeros, zeros, own_low, own_high,
            jnp.int32(0), jnp.int32(0), blank - held, blank, blank, blank, nothing, nothing,
        ),
        unroll=4,
    )
    far, total, direct, spots, slots, obs, touch, vals, errs = (related[3],) + related[6:]
    far_ref[0, 0] = jnp.max(far)
    base = (((spots >> 13) - chip + WINDOW) * CORES + ((spots >> 12) & 1)) * REPS
    totals = jnp.where(index == 0, total, direct)
    columns = (spots, base, slots * part_rows, obs, touch, totals)
    for number, column in enumerate(columns):
        table_ref[number : number + 1, :] = column.astype(jnp.float32)
    table_ref[6:7, :] = vals
    table_ref[7:8, :] = errs
    outs = [
        pltpu.make_async_copy(far_ref, far_out, small_sem.at[3]),
        pltpu.make_async_copy(table_ref, table_out, small_sem.at[4]),
    ]
    for out in outs:
        out.start()

    relays = []
    for step in range(half):
        to_right[step].wait_recv()
        relay = bulk(all_ref.at[left[1]], left[1], step, right, pass_right, far_left)
        relay.start()
        relays.append(relay)
        to_left[half + step].wait_recv()
        relay = bulk(all_ref.at[right[1]], right[1], half + step, left, pass_left, far_right)
        relay.start()
        relays.append(relay)

    for n in shifts:

        @pl.when(later[n])
        def _(n=n):
            pl.semaphore_wait(late_sem.at[WINDOW + n], 1)
            send_block(n)

    for step in range(half):
        to_right[half + step].wait_recv()
        to_left[step].wait_recv()
    for relay in relays:
        relay.wait()
    for copy in to_right + to_left:
        copy.wait_send()
    pltpu.make_async_copy(nearby, nearby, near_send).wait()
    to_pair.wait_send()
    block_copy.wait()
    for out in outs:
        out.wait()

    for n in shifts:

        @pl.when(valid[n])
        def _(n=n):
            pltpu.make_async_copy(block(n), block(n), row_send.at[WINDOW + n]).wait()
            pltpu.make_async_copy(block(n), block(n), row_recv.at[WINDOW + n]).wait()


def gather(mesh, ensemble, locations, values, errors):
    part_rows, held = ensemble.shape
    dma = pltpu.SemaphoreType.DMA
    return pl.pallas_call(
        functools.partial(gather_kernel, mesh.shape["state"] // CORES, held),
        out_shape=(
            jax.ShapeDtypeStruct((ROWS, 1, TILE), jnp.float32),
            jax.ShapeDtypeStruct((REPS, part_rows, held), jnp.float32),
            jax.ShapeDtypeStruct((8, TILE), jnp.float32),
            jax.ShapeDtypeStruct((1, 1), jnp.int32),
        ),
        in_specs=[pl.BlockSpec(memory_space=pl.ANY)] * 4,
        out_specs=(pl.BlockSpec(memory_space=pl.ANY),) * 4,
        scratch_shapes=[
            pltpu.SMEM((NOBS,), jnp.int32),
            pltpu.SMEM((NOBS,), jnp.float32),
            pltpu.SMEM((NOBS,), jnp.float32),
            pltpu.SMEM((1, 1), jnp.int32),
            pltpu.VMEM((8, TILE), jnp.float32),
            dma((5,)), dma,
            pltpu.VMEM((part_rows, held), jnp.float32),
            pltpu.VMEM((held // TILE, part_rows, TILE), jnp.float32),
            pltpu.VMEM((1, 1, TILE), jnp.float32),
            dma, dma, pltpu.SemaphoreType.REGULAR((2 * WINDOW + 1,)),
            dma, dma, dma((2 * WINDOW + 1,)), dma((2 * WINDOW + 1,)),
            dma((CHUNKS,)), dma((CHUNKS,)), dma((CHUNKS,)), dma((CHUNKS,)),
            dma((CHUNKS,)), dma((CHUNKS,)), dma((CHUNKS,)), dma((CHUNKS,)),
        ],
        compiler_params=pltpu.CompilerParams(collective_id=0, has_side_effects=True),
        name="gather",
    )(locations, values, errors, ensemble)


def solve_kernel(
    windowed, held, table_ref, rows_ref, all_ref, out_ref,
    y_ref, u_ref, w_ref, center_ref, mutual_ref, tile_ref,
):
    state = lax.axis_index("state")
    rep = lax.axis_index("rep")
    part_rows = all_ref.shape[1]
    order = [(rep + step) & (REPS - 1) for step in range(REPS)]

    def entry(number, t):
        return table_ref[number, t].astype(jnp.int32)

    total = entry(5, 0)
    direct = entry(5, 1)
    diagonal = iota((part_rows, TILE), 1) - iota((part_rows, TILE), 0)

    def spread(t, carry):
        spot = entry(0, t)
        if windowed:
            base = entry(1, t)
            place = entry(2, t)
        else:
            base = entry(3, t) * REPS
            place = 0
        for step in range(REPS):
            row = jnp.broadcast_to(rows_ref[base + order[step]], (part_rows, TILE))
            column = jnp.sum(jnp.where(diagonal == place, row, 0.0), axis=1, keepdims=True)
            y_ref[t, step * part_rows : (step + 1) * part_rows, :] = jnp.broadcast_to(
                column, (part_rows, TILE)
            )
        center = (spot // TILE * TILE).astype(jnp.float32) + (TILE - 1) * 0.5
        center_ref[pl.ds(t, 1), :] = jnp.full((1, TILE), center, jnp.float32)
        return carry

    lax.fori_loop(0, total, spread, 0)

    tiles = held // TILE
    tile_centers = (state * held + iota((tiles, TILE), 0) * TILE).astype(jnp.float32) + (
        TILE - 1
    ) * 0.5

    def assimilate(i, carry):
        t = total - 1 - i
        spot = table_ref[0, t]
        error = table_ref[7, t]
        y = y_ref[t]
        mean = jnp.sum(y, axis=0, keepdims=True) * (1.0 / M)
        spread_of = y - mean
        variance = jnp.sum(spread_of * spread_of, axis=0, keepdims=True) * (1.0 / (M - 1))
        total_var = variance + error
        shrink = 1.0 / (1.0 + jnp.sqrt(error / total_var))
        u = spread_of * (1.0 / ((M - 1) * total_var))
        w = (table_ref[6, t] - mean) - shrink * spread_of
        u_ref[t] = u
        w_ref[t] = w
        mutual_ref[...] = taper(jnp.abs(center_ref[...] - spot))
        tile_ref[t] = taper(jnp.abs(tile_centers - spot))

        def update(k, inner):
            other = y_ref[k]
            projected = jnp.sum(u * other, axis=0, keepdims=True)
            y_ref[k] = other + w * (mutual_ref[pl.ds(k, 1), :] * projected)
            return inner

        lax.fori_loop(0, t, update, 0)
        return carry

    lax.fori_loop(0, total, assimilate, 0)
    group = 4

    def apply(g, carry):
        spans = [
            pl.ds(pl.multiple_of((g * group + i) * TILE, TILE), TILE) for i in range(group)
        ]

        def one(d, values):
            t = entry(4, direct - 1 - d)
            u = u_ref[t]
            w = w_ref[t]
            result = []
            for i in range(group):
                projected = jnp.sum(u * values[i], axis=0, keepdims=True)
                weight = tile_ref[t, pl.ds(g * group + i, 1), :]
                result.append(values[i] + w * (weight * projected))
            return tuple(result)

        start = tuple(
            jnp.concatenate([all_ref[member, :, span] for member in order], axis=0)
            for span in spans
        )
        values = lax.fori_loop(0, direct, one, start)
        for span, value in zip(spans, values):
            out_ref[:, span] = value[:part_rows]
        return carry

    lax.fori_loop(0, tiles // group, apply, 0)


def solve(windowed, part_rows, held, table, rows, everything):
    vmem = pl.BlockSpec(memory_space=pltpu.VMEM)
    block = pltpu.VMEM((NOBS, M, TILE), jnp.float32)
    return pl.pallas_call(
        functools.partial(solve_kernel, windowed, held),
        out_shape=jax.ShapeDtypeStruct((part_rows, held), jnp.float32),
        in_specs=[pl.BlockSpec(memory_space=pltpu.SMEM), vmem, vmem],
        out_specs=vmem,
        scratch_shapes=[
            block, block, block,
            pltpu.VMEM((NOBS, TILE), jnp.float32),
            pltpu.VMEM((NOBS, TILE), jnp.float32),
            pltpu.VMEM((NOBS, held // TILE, TILE), jnp.float32),
        ],
        name="solve",
    )(table, rows, everything)


def full_rows(mesh, ensemble, locations):
    part_rows, held = ensemble.shape
    states = mesh.shape["state"]
    offsets = locations - lax.axis_index("state") * held
    inside = ((offsets >= 0) & (offsets < held)).astype(jnp.float32)
    columns = jnp.take(ensemble, jnp.clip(offsets, 0, held - 1), axis=1) * inside[None, :]
    placed = jnp.zeros((REPS, part_rows, NOBS), jnp.float32)
    placed = lax.dynamic_update_slice(placed, columns[None], (lax.axis_index("rep"), 0, 0))
    stride = 1
    while stride < states:
        pairs = [(i, i ^ stride) for i in range(states)]
        placed = placed + lax.ppermute(placed, "state", pairs)
        stride *= 2
    stride = 1
    while stride < REPS:
        pairs = [(i, i ^ stride) for i in range(REPS)]
        placed = placed + lax.ppermute(placed, "rep", pairs)
        stride *= 2
    by_obs = jnp.transpose(placed, (2, 0, 1)).reshape(NOBS * REPS, 1, part_rows)
    return jnp.pad(by_obs, ((0, 0), (0, 0), (0, TILE - part_rows)))


def on_device(mesh, ensemble, obs_values, obs_error, obs_location):
    part_rows, held = ensemble.shape
    rows, everything, table, far = gather(mesh, ensemble, obs_location, obs_values, obs_error)
    return lax.cond(
        far[0, 0] == 0,
        lambda: solve(True, part_rows, held, table, rows, everything),
        lambda: solve(
            False, part_rows, held, table, full_rows(mesh, ensemble, obs_location), everything
        ),
    )


def solution(mesh):
    in_specs = (P("rep", "state"), P(), P(), P())
    out_specs = P("rep", "state")
    return jax.shard_map(
        functools.partial(on_device, mesh),
        mesh=mesh,
        in_specs=in_specs,
        out_specs=out_specs,
        check_vma=False,
    )
```

```python
import functools

import jax
import jax.numpy as jnp
from jax import lax
from jax.experimental import pallas as pl
from jax.experimental.pallas import tpu as pltpu
from jax.sharding import PartitionSpec as P

MESH = pl.DeviceIdType.MESH
M = 64
TILE = 128
HALF = 4096
REACH = 2 * HALF
LINK = REACH + TILE // 2
NOBS = 48
REPS = 4
CORES = 2
WINDOW = 4
DEPTH = 16
SLOTS = 8
CHUNKS = 4
BATCH = 4
ROWS = (2 * WINDOW + 1) * CORES * REPS


def taper(distance):
    ratio = distance * (1.0 / HALF)
    near_part = (((-0.25 * ratio + 0.5) * ratio + 0.625) * ratio - 5.0 / 3.0) * ratio * ratio + 1.0
    ratio_far = jnp.maximum(ratio, 1.0)
    far_part = (
        ((((ratio_far / 12.0 - 0.5) * ratio_far + 0.625) * ratio_far + 5.0 / 3.0) * ratio_far - 5.0)
        * ratio_far
        + 4.0
        - 2.0 / (3.0 * ratio_far)
    )
    return jnp.where(
        ratio <= 1.0, near_part, jnp.where(ratio < 2.0, far_part, jnp.zeros_like(ratio))
    )


def iota(shape, axis):
    return lax.broadcasted_iota(jnp.int32, shape, axis)


def gather_kernel(
    chips, held, loc_any, val_any, err_any, ens_ref, rows_ref, all_ref, table_out, far_out,
    loc_ref, val_ref, err_ref, far_ref, table_ref, small_sem, block_sem, fetch_ref, local_ref, pick_ref, local_sem, own_sem, late_sem, near_send, near_recv, row_send, row_recv,
    send_right, send_left, recv_left, recv_right, pass_right, pass_left, far_left, far_right,
):
    state = lax.axis_index("state")
    rep = lax.axis_index("rep")
    chip = state >> 1
    core = state & 1
    part_rows = ens_ref.shape[0]
    tiles = held // TILE

    load = pltpu.make_async_copy(ens_ref, fetch_ref, local_sem)
    load.start()
    smalls = [
        pltpu.make_async_copy(loc_any, loc_ref, small_sem.at[0]),
        pltpu.make_async_copy(val_any, val_ref, small_sem.at[1]),
        pltpu.make_async_copy(err_any, err_ref, small_sem.at[2]),
    ]
    for small in smalls:
        small.start()

    depth = chip & (DEPTH - 1)
    shifts = list(range(1, WINDOW + 1)) + list(range(-1, -WINDOW - 1, -1))
    valid = {n: (chip + n >= 0) & (chip + n < chips) for n in shifts}

    def key(place):
        return place + jnp.where((place >> 2) == 2, DEPTH, 0)

    ahead = {n: key((depth + n) & (DEPTH - 1)) > key(depth) for n in shifts}
    later = {n: valid[n] & ahead[n] for n in shifts}
    earlier = {n: valid[n] & jnp.logical_not(ahead[n]) for n in shifts}
    members = [(c, r) for c in range(CORES) for r in range(REPS)]
    beside = members[1:]
    peers = members[1:REPS]
    pair = members[REPS]
    cores_of = [core, 1 - core]
    reps_of = [(rep + r) & (REPS - 1) for r in range(REPS)]

    def target(shift, member):
        return (chip + shift) * CORES + cores_of[member[0]], reps_of[member[1]]

    def signal(semaphore, shift, member):
        pl.semaphore_signal(
            semaphore, inc=1, device_id=target(shift, member), device_id_type=MESH
        )

    def count_of(flags):
        return sum(flags[n].astype(jnp.int32) for n in shifts)

    right = (state, reps_of[1])
    left = (state, reps_of[3])
    width = held // CHUNKS

    def piece(ref, chunk):
        return ref.at[:, pl.ds(chunk * width, width)]

    def bulk(source, owner, chunk, target, send_sem, recv_sem):
        return pltpu.make_async_remote_copy(
            src_ref=piece(source, chunk),
            dst_ref=piece(all_ref.at[owner], chunk),
            send_sem=send_sem.at[chunk],
            recv_sem=recv_sem.at[chunk],
            device_id=target,
            device_id_type=MESH,
        )

    half = CHUNKS // 2
    to_right = [bulk(ens_ref, rep, c, right, send_right, recv_left) for c in range(CHUNKS)]
    to_left = [bulk(ens_ref, rep, c, left, send_left, recv_right) for c in range(CHUNKS)]
    barrier = pltpu.get_barrier_semaphore()
    wraps = {n: valid[n] & (((chip + n) & ~(DEPTH - 1)) != (chip & ~(DEPTH - 1))) for n in shifts}
    greetings = (
        len(peers)
        + (1 - core)
        + count_of(earlier)
        + (len(members) - 1) * count_of({n: earlier[n] & wraps[n] for n in shifts})
    )
    for member in peers:
        signal(barrier, 0, member)

    @pl.when(core == 1)
    def _():
        signal(barrier, 0, pair)

    for n in shifts:

        @pl.when(later[n])
        def _(n=n):
            signal(barrier, n, members[0])

    for n in shifts:

        @pl.when(later[n] & wraps[n])
        def _(n=n):
            for member in beside:
                signal(barrier, n, member)

    smalls[0].wait()
    load.wait()
    block_copy = pltpu.make_async_copy(fetch_ref, all_ref.at[rep], block_sem)
    block_copy.start()
    for tile in range(tiles):
        local_ref[tile] = fetch_ref[:, tile * TILE : (tile + 1) * TILE]
    lane = iota((part_rows, TILE), 1)
    diagonal = lane - iota((part_rows, TILE), 0)
    rank = jnp.int32(0)
    packed = jnp.zeros((part_rows, TILE), jnp.float32)
    for j in range(NOBS):
        offset = loc_ref[j] - state * held
        inside = (offset >= 0) & (offset < held)
        safe = jnp.clip(offset, 0, held - 1)
        tile = local_ref[safe >> 7]
        wanted = jnp.where(inside, safe & (TILE - 1), -1)
        column = jnp.sum(jnp.where(lane == wanted, tile, 0.0), axis=1, keepdims=True)
        place = jnp.where(inside, rank * part_rows, -TILE * 2)
        packed = jnp.where(diagonal == place, column, packed)
        rank = rank + inside.astype(jnp.int32)
    pick_ref[0] = jnp.sum(packed, axis=0, keepdims=True)

    pl.semaphore_wait(barrier, greetings)

    def send_row(shift, member):
        slot = ((WINDOW - shift) * CORES + core) * REPS + rep
        pltpu.make_async_remote_copy(
            src_ref=pick_ref.at[0],
            dst_ref=rows_ref.at[slot],
            send_sem=row_send.at[WINDOW + shift],
            recv_sem=row_recv.at[WINDOW - shift],
            device_id=target(shift, member),
            device_id_type=MESH,
        ).start()

    for n in range(WINDOW, 0, -1):

        @pl.when(earlier[n] & wraps[n])
        def _(n=n):
            for member in members:
                send_row(n, member)

    own_row = (WINDOW * CORES + core) * REPS + rep
    for member in peers:
        pltpu.make_async_remote_copy(
            src_ref=pick_ref.at[0],
            dst_ref=rows_ref.at[own_row],
            send_sem=near_send,
            recv_sem=near_recv,
            device_id=target(0, member),
            device_id_type=MESH,
        ).start()
    own = pltpu.make_async_copy(pick_ref.at[0], rows_ref.at[own_row], own_sem)
    own.start()

    @pl.when(core == 0)
    def _():
        signal(late_sem.at[WINDOW], 0, pair)

    for n in shifts:

        @pl.when(earlier[n])
        def _(n=n):
            signal(late_sem.at[WINDOW - n], n, members[0])

    def block(shift, number=len(members)):
        return rows_ref.at[pl.ds((WINDOW + shift) * len(members), number)]

    def send_block(shift):
        pltpu.make_async_remote_copy(
            src_ref=block(0),
            dst_ref=block(-shift),
            send_sem=row_send.at[WINDOW + shift],
            recv_sem=row_recv.at[WINDOW - shift],
            device_id=target(shift, members[0]),
            device_id_type=MESH,
        ).start()

    for step in range(CHUNKS):
        to_right[step].start()
        to_left[(step + half) % CHUNKS].start()

    half_block = rows_ref.at[pl.ds(WINDOW * len(members) + core * REPS, REPS)]
    to_pair = pltpu.make_async_remote_copy(
        src_ref=half_block,
        dst_ref=half_block,
        send_sem=row_send.at[WINDOW],
        recv_sem=row_recv.at[WINDOW],
        device_id=target(0, pair),
        device_id_type=MESH,
    )
    own.wait()
    nearby = block(0, len(peers))
    pltpu.make_async_copy(nearby, nearby, near_recv).wait()

    @pl.when(core == 1)
    def _():
        pl.semaphore_wait(late_sem.at[WINDOW], 1)

    to_pair.start()
    to_pair.wait_recv()
    for n in shifts:

        @pl.when(earlier[n] & jnp.logical_not(wraps[n]))
        def _(n=n):
            send_block(n)

    smalls[1].wait()
    smalls[2].wait()
    shards = iota((8, TILE), 1)
    first = shards * held
    zeros = jnp.zeros((8, TILE), jnp.int32)
    blank = jnp.zeros((1, TILE), jnp.int32)
    index = iota((1, TILE), 1)
    own_low = state * held - REACH
    own_high = state * held + held + REACH

    def relate(i, carry):
        lows, highs, count, far, low, high, total, direct, spots, slots, obs, touch, vals, errs = carry
        j = NOBS - 1 - i
        spot = loc_ref[j]
        near = (spot >= lows) & (spot <= highs)
        away = jnp.abs((spot >> 13) - (shards >> 1)) > WINDOW
        count = count + ((spot >> 12) == shards).astype(jnp.int32)
        far = jnp.where((near & away) | (count > SLOTS), 1, far)
        lows = jnp.where(near, jnp.minimum(lows, spot - LINK), lows)
        highs = jnp.where(near, jnp.maximum(highs, spot + LINK), highs)
        here = (spot >= low) & (spot <= high)
        low = jnp.where(here, jnp.minimum(low, spot - LINK), low)
        high = jnp.where(here, jnp.maximum(high, spot + LINK), high)
        touches = (spot >= own_low) & (spot <= own_high)
        slots = slots + ((spots >> 12) == (spot >> 12)).astype(jnp.int32)
        place = index == jnp.where(here, total, -1)
        spots = jnp.where(place, spot, spots)
        slots = jnp.where(place, 0, slots)
        obs = jnp.where(place, j, obs)
        vals = jnp.where(place, val_ref[j], vals)
        errs = jnp.where(place, err_ref[j], errs)
        touch = jnp.where(index == jnp.where(touches, direct, -1), total, touch)
        total = total + here.astype(jnp.int32)
        direct = direct + touches.astype(jnp.int32)
        return lows, highs, count, far, low, high, total, direct, spots, slots, obs, touch, vals, errs

    nothing = jnp.zeros((1, TILE), jnp.float32)
    related = lax.fori_loop(
        0,
        NOBS,
        relate,
        (
            first - REACH, first + held + REACH, zeros, zeros, own_low, own_high,
            jnp.int32(0), jnp.int32(0), blank - held, blank, blank, blank, nothing, nothing,
        ),
        unroll=4,
    )
    far, total, direct, spots, slots, obs, touch, vals, errs = (related[3],) + related[6:]
    far_ref[0, 0] = jnp.max(far)
    base = (((spots >> 13) - chip + WINDOW) * CORES + ((spots >> 12) & 1)) * REPS
    totals = jnp.where(index == 0, total, direct)
    columns = (spots, base, slots * part_rows, obs, touch, totals)
    for number, column in enumerate(columns):
        table_ref[number : number + 1, :] = column.astype(jnp.float32)
    table_ref[6:7, :] = vals
    table_ref[7:8, :] = errs
    outs = [
        pltpu.make_async_copy(far_ref, far_out, small_sem.at[3]),
        pltpu.make_async_copy(table_ref, table_out, small_sem.at[4]),
    ]
    for out in outs:
        out.start()

    relays = []
    for step in range(half):
        to_right[step].wait_recv()
        relay = bulk(all_ref.at[left[1]], left[1], step, right, pass_right, far_left)
        relay.start()
        relays.append(relay)
        to_left[half + step].wait_recv()
        relay = bulk(all_ref.at[right[1]], right[1], half + step, left, pass_left, far_right)
        relay.start()
        relays.append(relay)

    for n in shifts:

        @pl.when(later[n])
        def _(n=n):
            pl.semaphore_wait(late_sem.at[WINDOW + n], 1)
            send_block(n)

    for step in range(half):
        to_right[half + step].wait_recv()
        to_left[step].wait_recv()
    for relay in relays:
        relay.wait()
    for copy in to_right + to_left:
        copy.wait_send()
    pltpu.make_async_copy(nearby, nearby, near_send).wait()
    to_pair.wait_send()
    block_copy.wait()
    for out in outs:
        out.wait()

    for n in shifts:

        @pl.when(valid[n])
        def _(n=n):
            pltpu.make_async_copy(block(n), block(n), row_send.at[WINDOW + n]).wait()
            pltpu.make_async_copy(block(n), block(n), row_recv.at[WINDOW + n]).wait()


def gather(mesh, ensemble, locations, values, errors):
    part_rows, held = ensemble.shape
    dma = pltpu.SemaphoreType.DMA
    return pl.pallas_call(
        functools.partial(gather_kernel, mesh.shape["state"] // CORES, held),
        out_shape=(
            jax.ShapeDtypeStruct((ROWS, 1, TILE), jnp.float32),
            jax.ShapeDtypeStruct((REPS, part_rows, held), jnp.float32),
            jax.ShapeDtypeStruct((8, TILE), jnp.float32),
            jax.ShapeDtypeStruct((1, 1), jnp.int32),
        ),
        in_specs=[pl.BlockSpec(memory_space=pl.ANY)] * 4,
        out_specs=(pl.BlockSpec(memory_space=pl.ANY),) * 4,
        scratch_shapes=[
            pltpu.SMEM((NOBS,), jnp.int32),
            pltpu.SMEM((NOBS,), jnp.float32),
            pltpu.SMEM((NOBS,), jnp.float32),
            pltpu.SMEM((1, 1), jnp.int32),
            pltpu.VMEM((8, TILE), jnp.float32),
            dma((5,)), dma,
            pltpu.VMEM((part_rows, held), jnp.float32),
            pltpu.VMEM((held // TILE, part_rows, TILE), jnp.float32),
            pltpu.VMEM((1, 1, TILE), jnp.float32),
            dma, dma, pltpu.SemaphoreType.REGULAR((2 * WINDOW + 1,)),
            dma, dma, dma((2 * WINDOW + 1,)), dma((2 * WINDOW + 1,)),
            dma((CHUNKS,)), dma((CHUNKS,)), dma((CHUNKS,)), dma((CHUNKS,)),
            dma((CHUNKS,)), dma((CHUNKS,)), dma((CHUNKS,)), dma((CHUNKS,)),
        ],
        compiler_params=pltpu.CompilerParams(collective_id=0, has_side_effects=True),
        name="gather",
    )(locations, values, errors, ensemble)


def solve_kernel(
    windowed, held, table_ref, rows_ref, all_ref, out_ref,
    y_ref, u_ref, w_ref, center_ref, mutual_ref, tile_ref, done_ref, out_sem,
):
    state = lax.axis_index("state")
    rep = lax.axis_index("rep")
    part_rows = all_ref.shape[1]
    order = [(rep + step) & (REPS - 1) for step in range(REPS)]

    def entry(number, t):
        return table_ref[number, t].astype(jnp.int32)

    total = entry(5, 0)
    direct = entry(5, 1)
    diagonal = iota((part_rows, TILE), 1) - iota((part_rows, TILE), 0)

    def spread(t):
        spot = entry(0, t)
        if windowed:
            base = jnp.clip(entry(1, t), 0, ROWS - REPS)
            place = entry(2, t)
        else:
            base = entry(3, t) * REPS
            place = 0
        for step in range(REPS):
            row = jnp.broadcast_to(rows_ref[base + order[step]], (part_rows, TILE))
            column = jnp.sum(jnp.where(diagonal == place, row, 0.0), axis=1, keepdims=True)
            y_ref[t, step * part_rows : (step + 1) * part_rows, :] = jnp.broadcast_to(
                column, (part_rows, TILE)
            )
        center = ((spot >> 7) << 7).astype(jnp.float32) + (TILE - 1) * 0.5
        center_ref[pl.ds(t, 1), :] = jnp.full((1, TILE), center, jnp.float32)

    def spread_batch(b, carry):
        for i in range(BATCH):
            spread(b * BATCH + i)
        return carry

    def batches(number):
        return (number + BATCH - 1) // BATCH

    lax.fori_loop(0, batches(total), spread_batch, 0)

    tiles = held // TILE
    tile_centers = (state * held + iota((tiles, TILE), 0) * TILE).astype(jnp.float32) + (
        TILE - 1
    ) * 0.5

    def assimilate(i, carry):
        t = total - 1 - i
        spot = table_ref[0, t]
        error = table_ref[7, t]
        y = y_ref[t]
        mean = jnp.sum(y, axis=0, keepdims=True) * (1.0 / M)
        spread_of = y - mean
        variance = jnp.sum(spread_of * spread_of, axis=0, keepdims=True) * (1.0 / (M - 1))
        total_var = variance + error
        shrink = 1.0 / (1.0 + jnp.sqrt(error / total_var))
        u = spread_of * (1.0 / ((M - 1) * total_var))
        w = (table_ref[6, t] - mean) - shrink * spread_of
        u_ref[t] = u
        w_ref[t] = w
        mutual_ref[...] = taper(jnp.abs(center_ref[...] - spot))
        tile_ref[t] = taper(jnp.abs(tile_centers - spot))

        def update(b, inner):
            first = b * BATCH
            others = [y_ref[first + i] for i in range(BATCH)]
            for i, other in enumerate(others):
                projected = jnp.sum(u * other, axis=0, keepdims=True)
                others[i] = other + w * (mutual_ref[pl.ds(first + i, 1), :] * projected)
            for i, other in enumerate(others):
                y_ref[first + i] = other
            return inner

        lax.fori_loop(0, batches(t), update, 0)
        return carry

    lax.fori_loop(0, total, assimilate, 0)
    group = 4

    def apply(g, carry):
        spans = [
            pl.ds(pl.multiple_of((g * group + i) * TILE, TILE), TILE) for i in range(group)
        ]

        def one(d, values):
            t = entry(4, direct - 1 - d)
            u = u_ref[t]
            w = w_ref[t]
            result = []
            for i in range(group):
                projected = jnp.sum(u * values[i], axis=0, keepdims=True)
                weight = tile_ref[t, pl.ds(g * group + i, 1), :]
                result.append(values[i] + w * (weight * projected))
            return tuple(result)

        start = tuple(
            jnp.concatenate([all_ref[member, :, span] for member in order], axis=0)
            for span in spans
        )
        values = lax.fori_loop(0, direct, one, start)
        for span, value in zip(spans, values):
            done_ref[:, span] = value[:part_rows]
        width = group * TILE
        wide = pl.ds(pl.multiple_of(g * width, width), width)
        pltpu.make_async_copy(done_ref.at[:, wide], out_ref.at[:, wide], out_sem).start()
        return carry

    lax.fori_loop(0, tiles // group, apply, 0)
    pltpu.make_async_copy(done_ref, out_ref, out_sem).wait()


def solve(windowed, part_rows, held, table, rows, everything):
    vmem = pl.BlockSpec(memory_space=pltpu.VMEM)
    block = pltpu.VMEM((NOBS, M, TILE), jnp.float32)
    return pl.pallas_call(
        functools.partial(solve_kernel, windowed, held),
        out_shape=jax.ShapeDtypeStruct((part_rows, held), jnp.float32),
        in_specs=[pl.BlockSpec(memory_space=pltpu.SMEM), vmem, vmem],
        out_specs=pl.BlockSpec(memory_space=pl.ANY),
        compiler_params=pltpu.CompilerParams(vmem_limit_bytes=65918864),
        scratch_shapes=[
            block, block, block,
            pltpu.VMEM((NOBS, TILE), jnp.float32),
            pltpu.VMEM((NOBS, TILE), jnp.float32),
            pltpu.VMEM((NOBS, held // TILE, TILE), jnp.float32),
            pltpu.VMEM((part_rows, held), jnp.float32),
            pltpu.SemaphoreType.DMA,
        ],
        name="solve",
    )(table, rows, everything)


def full_rows(mesh, ensemble, locations):
    part_rows, held = ensemble.shape
    states = mesh.shape["state"]
    offsets = locations - lax.axis_index("state") * held
    inside = ((offsets >= 0) & (offsets < held)).astype(jnp.float32)
    columns = jnp.take(ensemble, jnp.clip(offsets, 0, held - 1), axis=1) * inside[None, :]
    placed = jnp.zeros((REPS, part_rows, NOBS), jnp.float32)
    placed = lax.dynamic_update_slice(placed, columns[None], (lax.axis_index("rep"), 0, 0))
    stride = 1
    while stride < states:
        pairs = [(i, i ^ stride) for i in range(states)]
        placed = placed + lax.ppermute(placed, "state", pairs)
        stride *= 2
    stride = 1
    while stride < REPS:
        pairs = [(i, i ^ stride) for i in range(REPS)]
        placed = placed + lax.ppermute(placed, "rep", pairs)
        stride *= 2
    by_obs = jnp.transpose(placed, (2, 0, 1)).reshape(NOBS * REPS, 1, part_rows)
    return jnp.pad(by_obs, ((0, 0), (0, 0), (0, TILE - part_rows)))


def on_device(mesh, ensemble, obs_values, obs_error, obs_location):
    part_rows, held = ensemble.shape
    rows, everything, table, far = gather(mesh, ensemble, obs_location, obs_values, obs_error)
    return lax.switch(
        far[0, 0],
        (
            lambda: solve(True, part_rows, held, table, rows, everything),
            lambda: solve(
                False, part_rows, held, table, full_rows(mesh, ensemble, obs_location), everything
            ),
        ),
    )


def solution(mesh):
    in_specs = (P("rep", "state"), P(), P(), P())
    out_specs = P("rep", "state")
    return jax.shard_map(
        functools.partial(on_device, mesh),
        mesh=mesh,
        in_specs=in_specs,
        out_specs=out_specs,
        check_vma=False,
    )
```

```python
import functools

import jax
import jax.numpy as jnp
from jax import lax
from jax.experimental import pallas as pl
from jax.experimental.pallas import tpu as pltpu
from jax.sharding import PartitionSpec as P

MESH = pl.DeviceIdType.MESH
M = 64
TILE = 128
HALF = 4096
REACH = 2 * HALF
LINK = REACH + TILE // 2
NOBS = 48
REPS = 4
CORES = 2
WINDOW = 4
DEPTH = 16
SLOTS = 8
CHUNKS = 4
BATCH = 4
ROWS = (2 * WINDOW + 1) * CORES * REPS


def taper(distance):
    ratio = distance * (1.0 / HALF)
    near_part = (((-0.25 * ratio + 0.5) * ratio + 0.625) * ratio - 5.0 / 3.0) * ratio * ratio + 1.0
    ratio_far = jnp.maximum(ratio, 1.0)
    far_part = (
        ((((ratio_far / 12.0 - 0.5) * ratio_far + 0.625) * ratio_far + 5.0 / 3.0) * ratio_far - 5.0)
        * ratio_far
        + 4.0
        - 2.0 / (3.0 * ratio_far)
    )
    return jnp.where(
        ratio <= 1.0, near_part, jnp.where(ratio < 2.0, far_part, jnp.zeros_like(ratio))
    )


def iota(shape, axis):
    return lax.broadcasted_iota(jnp.int32, shape, axis)


def gather_kernel(
    chips, held, loc_any, val_any, err_any, ens_ref, rows_ref, all_ref, table_out, far_out,
    loc_ref, val_ref, err_ref, far_ref, table_ref, small_sem, block_sem, fetch_ref, local_ref, pick_ref, local_sem, own_sem, late_sem, near_send, near_recv, row_send, row_recv,
    send_right, send_left, recv_left, recv_right, pass_right, pass_left, far_left, far_right,
):
    state = lax.axis_index("state")
    rep = lax.axis_index("rep")
    chip = state >> 1
    core = state & 1
    part_rows = ens_ref.shape[0]
    tiles = held // TILE

    load = pltpu.make_async_copy(ens_ref, fetch_ref, local_sem)
    load.start()
    smalls = [
        pltpu.make_async_copy(loc_any, loc_ref, small_sem.at[0]),
        pltpu.make_async_copy(val_any, val_ref, small_sem.at[1]),
        pltpu.make_async_copy(err_any, err_ref, small_sem.at[2]),
    ]
    for small in smalls:
        small.start()

    depth = chip & (DEPTH - 1)
    shifts = list(range(1, WINDOW + 1)) + list(range(-1, -WINDOW - 1, -1))
    valid = {n: (chip + n >= 0) & (chip + n < chips) for n in shifts}

    def key(place):
        return place + jnp.where((place >> 2) == 2, DEPTH, 0)

    ahead = {n: key((depth + n) & (DEPTH - 1)) > key(depth) for n in shifts}
    later = {n: valid[n] & ahead[n] for n in shifts}
    earlier = {n: valid[n] & jnp.logical_not(ahead[n]) for n in shifts}
    members = [(c, r) for c in range(CORES) for r in range(REPS)]
    beside = members[1:]
    peers = members[1:REPS]
    pair = members[REPS]
    cores_of = [core, 1 - core]
    reps_of = [(rep + r) & (REPS - 1) for r in range(REPS)]

    def target(shift, member):
        return (chip + shift) * CORES + cores_of[member[0]], reps_of[member[1]]

    def signal(semaphore, shift, member):
        pl.semaphore_signal(
            semaphore, inc=1, device_id=target(shift, member), device_id_type=MESH
        )

    def count_of(flags):
        return sum(flags[n].astype(jnp.int32) for n in shifts)

    right = (state, reps_of[1])
    left = (state, reps_of[3])
    width = held // CHUNKS

    def piece(ref, chunk):
        return ref.at[:, pl.ds(chunk * width, width)]

    def bulk(source, owner, chunk, target, send_sem, recv_sem):
        return pltpu.make_async_remote_copy(
            src_ref=piece(source, chunk),
            dst_ref=piece(all_ref.at[owner], chunk),
            send_sem=send_sem.at[chunk],
            recv_sem=recv_sem.at[chunk],
            device_id=target,
            device_id_type=MESH,
        )

    half = CHUNKS // 2
    to_right = [bulk(ens_ref, rep, c, right, send_right, recv_left) for c in range(CHUNKS)]
    to_left = [bulk(ens_ref, rep, c, left, send_left, recv_right) for c in range(CHUNKS)]
    barrier = pltpu.get_barrier_semaphore()

    def straight(n):
        other = depth + n
        apart = (chip + n) ^ chip
        low = (depth > 0) & (other > 0) & (depth < DEPTH // 2) & (other < DEPTH // 2)
        return valid[n] & (((apart & (DEPTH // 2)) != 0) | (low & ((apart & WINDOW) != 0)))

    crosses = {n: straight(n) for n in shifts}
    greetings = (
        len(peers)
        + (1 - core)
        + count_of(earlier)
        + (len(members) - 1) * count_of({n: earlier[n] & crosses[n] for n in shifts})
    )
    for member in peers:
        signal(barrier, 0, member)

    @pl.when(core == 1)
    def _():
        signal(barrier, 0, pair)

    for n in shifts:

        @pl.when(later[n])
        def _(n=n):
            signal(barrier, n, members[0])

    for n in shifts:

        @pl.when(later[n] & crosses[n])
        def _(n=n):
            for member in beside:
                signal(barrier, n, member)

    smalls[0].wait()
    load.wait()
    block_copy = pltpu.make_async_copy(fetch_ref, all_ref.at[rep], block_sem)
    block_copy.start()
    for tile in range(tiles):
        local_ref[tile] = fetch_ref[:, tile * TILE : (tile + 1) * TILE]
    lane = iota((part_rows, TILE), 1)
    diagonal = lane - iota((part_rows, TILE), 0)
    rank = jnp.int32(0)
    packed = jnp.zeros((part_rows, TILE), jnp.float32)
    for j in range(NOBS):
        offset = loc_ref[j] - state * held
        inside = (offset >= 0) & (offset < held)
        safe = jnp.clip(offset, 0, held - 1)
        tile = local_ref[safe >> 7]
        wanted = jnp.where(inside, safe & (TILE - 1), -1)
        column = jnp.sum(jnp.where(lane == wanted, tile, 0.0), axis=1, keepdims=True)
        place = jnp.where(inside, rank * part_rows, -TILE * 2)
        packed = jnp.where(diagonal == place, column, packed)
        rank = rank + inside.astype(jnp.int32)
    pick_ref[0] = jnp.sum(packed, axis=0, keepdims=True)

    pl.semaphore_wait(barrier, greetings)

    def send_row(shift, member):
        slot = ((WINDOW - shift) * CORES + core) * REPS + rep
        pltpu.make_async_remote_copy(
            src_ref=pick_ref.at[0],
            dst_ref=rows_ref.at[slot],
            send_sem=row_send.at[WINDOW + shift],
            recv_sem=row_recv.at[WINDOW - shift],
            device_id=target(shift, member),
            device_id_type=MESH,
        ).start()

    for n in sorted(shifts, key=abs, reverse=True):

        @pl.when(earlier[n] & crosses[n])
        def _(n=n):
            for member in members:
                send_row(n, member)

    own_row = (WINDOW * CORES + core) * REPS + rep
    for member in peers:
        pltpu.make_async_remote_copy(
            src_ref=pick_ref.at[0],
            dst_ref=rows_ref.at[own_row],
            send_sem=near_send,
            recv_sem=near_recv,
            device_id=target(0, member),
            device_id_type=MESH,
        ).start()
    own = pltpu.make_async_copy(pick_ref.at[0], rows_ref.at[own_row], own_sem)
    own.start()

    @pl.when(core == 0)
    def _():
        signal(late_sem.at[WINDOW], 0, pair)

    for n in shifts:

        @pl.when(earlier[n])
        def _(n=n):
            signal(late_sem.at[WINDOW - n], n, members[0])

    def block(shift, number=len(members)):
        return rows_ref.at[pl.ds((WINDOW + shift) * len(members), number)]

    def send_block(shift):
        pltpu.make_async_remote_copy(
            src_ref=block(0),
            dst_ref=block(-shift),
            send_sem=row_send.at[WINDOW + shift],
            recv_sem=row_recv.at[WINDOW - shift],
            device_id=target(shift, members[0]),
            device_id_type=MESH,
        ).start()

    for step in range(CHUNKS):
        to_right[step].start()
        to_left[(step + half) % CHUNKS].start()

    half_block = rows_ref.at[pl.ds(WINDOW * len(members) + core * REPS, REPS)]
    to_pair = pltpu.make_async_remote_copy(
        src_ref=half_block,
        dst_ref=half_block,
        send_sem=row_send.at[WINDOW],
        recv_sem=row_recv.at[WINDOW],
        device_id=target(0, pair),
        device_id_type=MESH,
    )
    own.wait()
    nearby = block(0, len(peers))
    pltpu.make_async_copy(nearby, nearby, near_recv).wait()

    @pl.when(core == 1)
    def _():
        pl.semaphore_wait(late_sem.at[WINDOW], 1)

    to_pair.start()
    to_pair.wait_recv()
    for n in shifts:

        @pl.when(earlier[n] & jnp.logical_not(crosses[n]))
        def _(n=n):
            send_block(n)

    relays = []
    for step in range(half):
        to_right[step].wait_recv()
        relay = bulk(all_ref.at[left[1]], left[1], step, right, pass_right, far_left)
        relay.start()
        relays.append(relay)
        to_left[half + step].wait_recv()
        relay = bulk(all_ref.at[right[1]], right[1], half + step, left, pass_left, far_right)
        relay.start()
        relays.append(relay)

    smalls[1].wait()
    smalls[2].wait()
    shards = iota((8, TILE), 1)
    first = shards * held
    zeros = jnp.zeros((8, TILE), jnp.int32)
    blank = jnp.zeros((1, TILE), jnp.int32)
    index = iota((1, TILE), 1)
    own_low = state * held - REACH
    own_high = state * held + held + REACH

    def relate(i, carry):
        lows, highs, count, far, low, high, total, direct, spots, slots, obs, touch, vals, errs = carry
        j = NOBS - 1 - i
        spot = loc_ref[j]
        near = (spot >= lows) & (spot <= highs)
        away = jnp.abs((spot >> 13) - (shards >> 1)) > WINDOW
        count = count + ((spot >> 12) == shards).astype(jnp.int32)
        far = jnp.where((near & away) | (count > SLOTS), 1, far)
        lows = jnp.where(near, jnp.minimum(lows, spot - LINK), lows)
        highs = jnp.where(near, jnp.maximum(highs, spot + LINK), highs)
        here = (spot >= low) & (spot <= high)
        low = jnp.where(here, jnp.minimum(low, spot - LINK), low)
        high = jnp.where(here, jnp.maximum(high, spot + LINK), high)
        touches = (spot >= own_low) & (spot <= own_high)
        slots = slots + ((spots >> 12) == (spot >> 12)).astype(jnp.int32)
        place = index == jnp.where(here, total, -1)
        spots = jnp.where(place, spot, spots)
        slots = jnp.where(place, 0, slots)
        obs = jnp.where(place, j, obs)
        vals = jnp.where(place, val_ref[j], vals)
        errs = jnp.where(place, err_ref[j], errs)
        touch = jnp.where(index == jnp.where(touches, direct, -1), total, touch)
        total = total + here.astype(jnp.int32)
        direct = direct + touches.astype(jnp.int32)
        return lows, highs, count, far, low, high, total, direct, spots, slots, obs, touch, vals, errs

    nothing = jnp.zeros((1, TILE), jnp.float32)
    related = lax.fori_loop(
        0,
        NOBS,
        relate,
        (
            first - REACH, first + held + REACH, zeros, zeros, own_low, own_high,
            jnp.int32(0), jnp.int32(0), blank - held, blank, blank, blank, nothing, nothing,
        ),
        unroll=4,
    )
    far, total, direct, spots, slots, obs, touch, vals, errs = (related[3],) + related[6:]
    far_ref[0, 0] = jnp.max(far)
    base = (((spots >> 13) - chip + WINDOW) * CORES + ((spots >> 12) & 1)) * REPS
    totals = jnp.where(index == 0, total, direct)
    columns = (spots, base, slots * part_rows, obs, touch, totals)
    for number, column in enumerate(columns):
        table_ref[number : number + 1, :] = column.astype(jnp.float32)
    table_ref[6:7, :] = vals
    table_ref[7:8, :] = errs
    outs = [
        pltpu.make_async_copy(far_ref, far_out, small_sem.at[3]),
        pltpu.make_async_copy(table_ref, table_out, small_sem.at[4]),
    ]
    for out in outs:
        out.start()

    for n in shifts:

        @pl.when(later[n])
        def _(n=n):
            pl.semaphore_wait(late_sem.at[WINDOW + n], 1)
            send_block(n)

    for step in range(half):
        to_right[half + step].wait_recv()
        to_left[step].wait_recv()
    for relay in relays:
        relay.wait()
    for copy in to_right + to_left:
        copy.wait_send()
    pltpu.make_async_copy(nearby, nearby, near_send).wait()
    to_pair.wait_send()
    block_copy.wait()
    for out in outs:
        out.wait()

    for n in shifts:

        @pl.when(valid[n])
        def _(n=n):
            pltpu.make_async_copy(block(n), block(n), row_send.at[WINDOW + n]).wait()
            pltpu.make_async_copy(block(n), block(n), row_recv.at[WINDOW + n]).wait()


def gather(mesh, ensemble, locations, values, errors):
    part_rows, held = ensemble.shape
    dma = pltpu.SemaphoreType.DMA
    return pl.pallas_call(
        functools.partial(gather_kernel, mesh.shape["state"] // CORES, held),
        out_shape=(
            jax.ShapeDtypeStruct((ROWS, 1, TILE), jnp.float32),
            jax.ShapeDtypeStruct((REPS, part_rows, held), jnp.float32),
            jax.ShapeDtypeStruct((8, TILE), jnp.float32),
            jax.ShapeDtypeStruct((1, 1), jnp.int32),
        ),
        in_specs=[pl.BlockSpec(memory_space=pl.ANY)] * 4,
        out_specs=(pl.BlockSpec(memory_space=pl.ANY),) * 4,
        scratch_shapes=[
            pltpu.SMEM((NOBS,), jnp.int32),
            pltpu.SMEM((NOBS,), jnp.float32),
            pltpu.SMEM((NOBS,), jnp.float32),
            pltpu.SMEM((1, 1), jnp.int32),
            pltpu.VMEM((8, TILE), jnp.float32),
            dma((5,)), dma,
            pltpu.VMEM((part_rows, held), jnp.float32),
            pltpu.VMEM((held // TILE, part_rows, TILE), jnp.float32),
            pltpu.VMEM((1, 1, TILE), jnp.float32),
            dma, dma, pltpu.SemaphoreType.REGULAR((2 * WINDOW + 1,)),
            dma, dma, dma((2 * WINDOW + 1,)), dma((2 * WINDOW + 1,)),
            dma((CHUNKS,)), dma((CHUNKS,)), dma((CHUNKS,)), dma((CHUNKS,)),
            dma((CHUNKS,)), dma((CHUNKS,)), dma((CHUNKS,)), dma((CHUNKS,)),
        ],
        compiler_params=pltpu.CompilerParams(collective_id=0, has_side_effects=True),
        name="gather",
    )(locations, values, errors, ensemble)


def solve_kernel(
    windowed, held, table_ref, rows_ref, all_ref, out_ref,
    y_ref, u_ref, w_ref, center_ref, mutual_ref, tile_ref, done_ref, out_sem,
):
    state = lax.axis_index("state")
    rep = lax.axis_index("rep")
    part_rows = all_ref.shape[1]
    order = [(rep + step) & (REPS - 1) for step in range(REPS)]

    def entry(number, t):
        return table_ref[number, t].astype(jnp.int32)

    total = entry(5, 0)
    direct = entry(5, 1)
    diagonal = iota((part_rows, TILE), 1) - iota((part_rows, TILE), 0)

    def spread(t):
        spot = entry(0, t)
        if windowed:
            base = jnp.clip(entry(1, t), 0, ROWS - REPS)
            place = entry(2, t)
        else:
            base = entry(3, t) * REPS
            place = 0
        for step in range(REPS):
            row = jnp.broadcast_to(rows_ref[base + order[step]], (part_rows, TILE))
            column = jnp.sum(jnp.where(diagonal == place, row, 0.0), axis=1, keepdims=True)
            y_ref[t, step * part_rows : (step + 1) * part_rows, :] = jnp.broadcast_to(
                column, (part_rows, TILE)
            )
        center = ((spot >> 7) << 7).astype(jnp.float32) + (TILE - 1) * 0.5
        center_ref[pl.ds(t, 1), :] = jnp.full((1, TILE), center, jnp.float32)

    def spread_batch(b, carry):
        for i in range(BATCH):
            spread(b * BATCH + i)
        return carry

    def batches(number):
        return (number + BATCH - 1) // BATCH

    lax.fori_loop(0, batches(total), spread_batch, 0)

    tiles = held // TILE
    tile_centers = (state * held + iota((tiles, TILE), 0) * TILE).astype(jnp.float32) + (
        TILE - 1
    ) * 0.5

    def assimilate(i, carry):
        t = total - 1 - i
        spot = table_ref[0, t]
        error = table_ref[7, t]
        y = y_ref[t]
        mean = jnp.sum(y, axis=0, keepdims=True) * (1.0 / M)
        spread_of = y - mean
        variance = jnp.sum(spread_of * spread_of, axis=0, keepdims=True) * (1.0 / (M - 1))
        total_var = variance + error
        shrink = 1.0 / (1.0 + jnp.sqrt(error / total_var))
        u = spread_of * (1.0 / ((M - 1) * total_var))
        w = (table_ref[6, t] - mean) - shrink * spread_of
        u_ref[t] = u
        w_ref[t] = w
        mutual_ref[...] = taper(jnp.abs(center_ref[...] - spot))
        tile_ref[t] = taper(jnp.abs(tile_centers - spot))

        def update(b, inner):
            first = b * BATCH
            others = [y_ref[first + i] for i in range(BATCH)]
            for i, other in enumerate(others):
                projected = jnp.sum(u * other, axis=0, keepdims=True)
                others[i] = other + w * (mutual_ref[pl.ds(first + i, 1), :] * projected)
            for i, other in enumerate(others):
                y_ref[first + i] = other
            return inner

        lax.fori_loop(0, batches(t), update, 0)
        return carry

    lax.fori_loop(0, total, assimilate, 0)
    group = 4

    def apply(g, carry):
        spans = [
            pl.ds(pl.multiple_of((g * group + i) * TILE, TILE), TILE) for i in range(group)
        ]

        def one(d, values):
            t = entry(4, direct - 1 - d)
            u = u_ref[t]
            w = w_ref[t]
            result = []
            for i in range(group):
                projected = jnp.sum(u * values[i], axis=0, keepdims=True)
                weight = tile_ref[t, pl.ds(g * group + i, 1), :]
                result.append(values[i] + w * (weight * projected))
            return tuple(result)

        start = tuple(
            jnp.concatenate([all_ref[member, :, span] for member in order], axis=0)
            for span in spans
        )
        values = lax.fori_loop(0, direct, one, start)
        for span, value in zip(spans, values):
            done_ref[:, span] = value[:part_rows]
        width = group * TILE
        wide = pl.ds(pl.multiple_of(g * width, width), width)
        pltpu.make_async_copy(done_ref.at[:, wide], out_ref.at[:, wide], out_sem).start()
        return carry

    lax.fori_loop(0, tiles // group, apply, 0)
    pltpu.make_async_copy(done_ref, out_ref, out_sem).wait()


def solve(windowed, part_rows, held, table, rows, everything):
    vmem = pl.BlockSpec(memory_space=pltpu.VMEM)
    block = pltpu.VMEM((NOBS, M, TILE), jnp.float32)
    return pl.pallas_call(
        functools.partial(solve_kernel, windowed, held),
        out_shape=jax.ShapeDtypeStruct((part_rows, held), jnp.float32),
        in_specs=[pl.BlockSpec(memory_space=pltpu.SMEM), vmem, vmem],
        out_specs=pl.BlockSpec(memory_space=pl.ANY),
        compiler_params=pltpu.CompilerParams(vmem_limit_bytes=65918864),
        scratch_shapes=[
            block, block, block,
            pltpu.VMEM((NOBS, TILE), jnp.float32),
            pltpu.VMEM((NOBS, TILE), jnp.float32),
            pltpu.VMEM((NOBS, held // TILE, TILE), jnp.float32),
            pltpu.VMEM((part_rows, held), jnp.float32),
            pltpu.SemaphoreType.DMA,
        ],
        name="solve",
    )(table, rows, everything)


def full_rows(mesh, ensemble, locations):
    part_rows, held = ensemble.shape
    states = mesh.shape["state"]
    offsets = locations - lax.axis_index("state") * held
    inside = ((offsets >= 0) & (offsets < held)).astype(jnp.float32)
    columns = jnp.take(ensemble, jnp.clip(offsets, 0, held - 1), axis=1) * inside[None, :]
    placed = jnp.zeros((REPS, part_rows, NOBS), jnp.float32)
    placed = lax.dynamic_update_slice(placed, columns[None], (lax.axis_index("rep"), 0, 0))
    stride = 1
    while stride < states:
        pairs = [(i, i ^ stride) for i in range(states)]
        placed = placed + lax.ppermute(placed, "state", pairs)
        stride *= 2
    stride = 1
    while stride < REPS:
        pairs = [(i, i ^ stride) for i in range(REPS)]
        placed = placed + lax.ppermute(placed, "rep", pairs)
        stride *= 2
    by_obs = jnp.transpose(placed, (2, 0, 1)).reshape(NOBS * REPS, 1, part_rows)
    return jnp.pad(by_obs, ((0, 0), (0, 0), (0, TILE - part_rows)))


def on_device(mesh, ensemble, obs_values, obs_error, obs_location):
    part_rows, held = ensemble.shape
    rows, everything, table, far = gather(mesh, ensemble, obs_location, obs_values, obs_error)
    return lax.switch(
        far[0, 0],
        (
            lambda: solve(True, part_rows, held, table, rows, everything),
            lambda: solve(
                False, part_rows, held, table, full_rows(mesh, ensemble, obs_location), everything
            ),
        ),
    )


def solution(mesh):
    in_specs = (P("rep", "state"), P(), P(), P())
    out_specs = P("rep", "state")
    return jax.shard_map(
        functools.partial(on_device, mesh),
        mesh=mesh,
        in_specs=in_specs,
        out_specs=out_specs,
        check_vma=False,
    )
```

```python
import functools

import jax
import jax.numpy as jnp
from jax import lax
from jax.experimental import pallas as pl
from jax.experimental.pallas import tpu as pltpu
from jax.sharding import PartitionSpec as P

MESH = pl.DeviceIdType.MESH
M = 64
TILE = 128
HALF = 4096
REACH = 2 * HALF
LINK = REACH + TILE // 2
NOBS = 48
REPS = 4
CORES = 2
WINDOW = 4
DEPTH = 16
SLOTS = 8
CHUNKS = 4
BATCH = 4
ROWS = (2 * WINDOW + 1) * CORES * REPS


def taper(distance):
    ratio = distance * (1.0 / HALF)
    near_part = (((-0.25 * ratio + 0.5) * ratio + 0.625) * ratio - 5.0 / 3.0) * ratio * ratio + 1.0
    ratio_far = jnp.maximum(ratio, 1.0)
    far_part = (
        ((((ratio_far / 12.0 - 0.5) * ratio_far + 0.625) * ratio_far + 5.0 / 3.0) * ratio_far - 5.0)
        * ratio_far
        + 4.0
        - 2.0 / (3.0 * ratio_far)
    )
    return jnp.where(
        ratio <= 1.0, near_part, jnp.where(ratio < 2.0, far_part, jnp.zeros_like(ratio))
    )


def iota(shape, axis):
    return lax.broadcasted_iota(jnp.int32, shape, axis)


def gather_kernel(
    chips, held, loc_any, val_any, err_any, ens_ref, rows_ref, all_ref, table_out, far_out,
    loc_ref, val_ref, err_ref, far_ref, table_ref, small_sem, block_sem, fetch_ref, local_ref, pick_ref, local_sem, own_sem, late_sem, near_send, near_recv, row_send, row_recv,
    send_right, send_left, recv_left, recv_right, pass_right, pass_left, far_left, far_right,
):
    state = lax.axis_index("state")
    rep = lax.axis_index("rep")
    chip = state >> 1
    core = state & 1
    part_rows = ens_ref.shape[0]
    tiles = held // TILE

    load = pltpu.make_async_copy(ens_ref, fetch_ref, local_sem)
    load.start()
    smalls = [
        pltpu.make_async_copy(loc_any, loc_ref, small_sem.at[0]),
        pltpu.make_async_copy(val_any, val_ref, small_sem.at[1]),
        pltpu.make_async_copy(err_any, err_ref, small_sem.at[2]),
    ]
    for small in smalls:
        small.start()

    depth = chip & (DEPTH - 1)
    shifts = list(range(1, WINDOW + 1)) + list(range(-1, -WINDOW - 1, -1))
    valid = {n: (chip + n >= 0) & (chip + n < chips) for n in shifts}

    def key(place):
        return place + jnp.where((place >> 2) == 2, DEPTH, 0)

    ahead = {n: key((depth + n) & (DEPTH - 1)) > key(depth) for n in shifts}
    later = {n: valid[n] & ahead[n] for n in shifts}
    earlier = {n: valid[n] & jnp.logical_not(ahead[n]) for n in shifts}
    members = [(c, r) for c in range(CORES) for r in range(REPS)]
    beside = members[1:]
    peers = members[1:REPS]
    pair = members[REPS]
    cores_of = [core, 1 - core]
    reps_of = [(rep + r) & (REPS - 1) for r in range(REPS)]

    def target(shift, member):
        return (chip + shift) * CORES + cores_of[member[0]], reps_of[member[1]]

    def signal(semaphore, shift, member):
        pl.semaphore_signal(
            semaphore, inc=1, device_id=target(shift, member), device_id_type=MESH
        )

    def count_of(flags):
        return sum(flags[n].astype(jnp.int32) for n in shifts)

    right = (state, reps_of[1])
    left = (state, reps_of[3])
    width = held // CHUNKS

    def piece(ref, chunk):
        return ref.at[:, pl.ds(chunk * width, width)]

    def bulk(source, owner, chunk, target, send_sem, recv_sem):
        return pltpu.make_async_remote_copy(
            src_ref=piece(source, chunk),
            dst_ref=piece(all_ref.at[owner], chunk),
            send_sem=send_sem.at[chunk],
            recv_sem=recv_sem.at[chunk],
            device_id=target,
            device_id_type=MESH,
        )

    half = CHUNKS // 2
    to_right = [bulk(ens_ref, rep, c, right, send_right, recv_left) for c in range(CHUNKS)]
    to_left = [bulk(ens_ref, rep, c, left, send_left, recv_right) for c in range(CHUNKS)]
    barrier = pltpu.get_barrier_semaphore()

    def straight(n):
        other = depth + n
        apart = (chip + n) ^ chip
        low = (depth > 0) & (other > 0) & (depth < DEPTH // 2) & (other < DEPTH // 2)
        return valid[n] & (((apart & (DEPTH // 2)) != 0) | (low & ((apart & WINDOW) != 0)))

    crosses = {n: straight(n) for n in shifts}
    greetings = (
        len(peers)
        + (1 - core)
        + count_of(earlier)
        + (len(members) - 1) * count_of({n: earlier[n] & crosses[n] for n in shifts})
    )
    for member in peers:
        signal(barrier, 0, member)

    @pl.when(core == 1)
    def _():
        signal(barrier, 0, pair)

    for n in shifts:

        @pl.when(later[n])
        def _(n=n):
            signal(barrier, n, members[0])

    for n in shifts:

        @pl.when(later[n] & crosses[n])
        def _(n=n):
            for member in beside:
                signal(barrier, n, member)

    smalls[0].wait()
    load.wait()
    block_copy = pltpu.make_async_copy(fetch_ref, all_ref.at[rep], block_sem)
    block_copy.start()
    for tile in range(tiles):
        local_ref[tile] = fetch_ref[:, tile * TILE : (tile + 1) * TILE]
    lane = iota((part_rows, TILE), 1)
    diagonal = lane - iota((part_rows, TILE), 0)
    rank = jnp.int32(0)
    packed = jnp.zeros((part_rows, TILE), jnp.float32)
    for j in range(NOBS):
        offset = loc_ref[j] - state * held
        inside = (offset >= 0) & (offset < held)
        safe = jnp.clip(offset, 0, held - 1)
        tile = local_ref[safe >> 7]
        wanted = jnp.where(inside, safe & (TILE - 1), -1)
        column = jnp.sum(jnp.where(lane == wanted, tile, 0.0), axis=1, keepdims=True)
        place = jnp.where(inside, rank * part_rows, -TILE * 2)
        packed = jnp.where(diagonal == place, column, packed)
        rank = rank + inside.astype(jnp.int32)
    pick_ref[0] = jnp.sum(packed, axis=0, keepdims=True)

    pl.semaphore_wait(barrier, greetings)

    def send_row(shift, member):
        slot = ((WINDOW - shift) * CORES + core) * REPS + rep
        pltpu.make_async_remote_copy(
            src_ref=pick_ref.at[0],
            dst_ref=rows_ref.at[slot],
            send_sem=row_send.at[WINDOW + shift],
            recv_sem=row_recv.at[WINDOW - shift],
            device_id=target(shift, member),
            device_id_type=MESH,
        ).start()

    for n in sorted(shifts, key=abs, reverse=True):

        @pl.when(earlier[n] & crosses[n])
        def _(n=n):
            for member in members:
                send_row(n, member)

    own_row = (WINDOW * CORES + core) * REPS + rep
    for member in peers:
        pltpu.make_async_remote_copy(
            src_ref=pick_ref.at[0],
            dst_ref=rows_ref.at[own_row],
            send_sem=near_send,
            recv_sem=near_recv,
            device_id=target(0, member),
            device_id_type=MESH,
        ).start()
    own = pltpu.make_async_copy(pick_ref.at[0], rows_ref.at[own_row], own_sem)
    own.start()

    @pl.when(core == 0)
    def _():
        signal(late_sem.at[WINDOW], 0, pair)

    for n in shifts:

        @pl.when(earlier[n])
        def _(n=n):
            signal(late_sem.at[WINDOW - n], n, members[0])

    def block(shift, number=len(members)):
        return rows_ref.at[pl.ds((WINDOW + shift) * len(members), number)]

    def send_block(shift):
        pltpu.make_async_remote_copy(
            src_ref=block(0),
            dst_ref=block(-shift),
            send_sem=row_send.at[WINDOW + shift],
            recv_sem=row_recv.at[WINDOW - shift],
            device_id=target(shift, members[0]),
            device_id_type=MESH,
        ).start()

    for step in range(CHUNKS):
        to_right[step].start()
        to_left[(step + half) % CHUNKS].start()

    half_block = rows_ref.at[pl.ds(WINDOW * len(members) + core * REPS, REPS)]
    to_pair = pltpu.make_async_remote_copy(
        src_ref=half_block,
        dst_ref=half_block,
        send_sem=row_send.at[WINDOW],
        recv_sem=row_recv.at[WINDOW],
        device_id=target(0, pair),
        device_id_type=MESH,
    )
    own.wait()
    nearby = block(0, len(peers))
    pltpu.make_async_copy(nearby, nearby, near_recv).wait()

    @pl.when(core == 1)
    def _():
        pl.semaphore_wait(late_sem.at[WINDOW], 1)

    to_pair.start()
    to_pair.wait_recv()
    for n in shifts:

        @pl.when(earlier[n] & jnp.logical_not(crosses[n]))
        def _(n=n):
            send_block(n)

    relays = []
    for step in range(half):
        to_right[step].wait_recv()
        relay = bulk(all_ref.at[left[1]], left[1], step, right, pass_right, far_left)
        relay.start()
        relays.append(relay)
        to_left[half + step].wait_recv()
        relay = bulk(all_ref.at[right[1]], right[1], half + step, left, pass_left, far_right)
        relay.start()
        relays.append(relay)

    smalls[1].wait()
    smalls[2].wait()
    shards = iota((8, TILE), 1)
    first = shards * held
    zeros = jnp.zeros((8, TILE), jnp.int32)
    blank = jnp.zeros((1, TILE), jnp.int32)
    index = iota((1, TILE), 1)
    own_low = state * held - REACH
    own_high = state * held + held + REACH

    def relate(i, carry):
        lows, highs, count, far, low, high, total, direct, spots, slots, obs, touch, vals, errs = carry
        j = NOBS - 1 - i
        spot = loc_ref[j]
        near = (spot >= lows) & (spot <= highs)
        away = jnp.abs((spot >> 13) - (shards >> 1)) > WINDOW
        count = count + ((spot >> 12) == shards).astype(jnp.int32)
        far = jnp.where((near & away) | (count > SLOTS), 1, far)
        lows = jnp.where(near, jnp.minimum(lows, spot - LINK), lows)
        highs = jnp.where(near, jnp.maximum(highs, spot + LINK), highs)
        here = (spot >= low) & (spot <= high)
        low = jnp.where(here, jnp.minimum(low, spot - LINK), low)
        high = jnp.where(here, jnp.maximum(high, spot + LINK), high)
        touches = (spot >= own_low) & (spot <= own_high)
        slots = slots + ((spots >> 12) == (spot >> 12)).astype(jnp.int32)
        place = index == jnp.where(here, total, -1)
        spots = jnp.where(place, spot, spots)
        slots = jnp.where(place, 0, slots)
        obs = jnp.where(place, j, obs)
        vals = jnp.where(place, val_ref[j], vals)
        errs = jnp.where(place, err_ref[j], errs)
        touch = jnp.where(index == jnp.where(touches, direct, -1), total, touch)
        total = total + here.astype(jnp.int32)
        direct = direct + touches.astype(jnp.int32)
        return lows, highs, count, far, low, high, total, direct, spots, slots, obs, touch, vals, errs

    nothing = jnp.zeros((1, TILE), jnp.float32)
    related = lax.fori_loop(
        0,
        NOBS,
        relate,
        (
            first - REACH, first + held + REACH, zeros, zeros, own_low, own_high,
            jnp.int32(0), jnp.int32(0), blank - held, blank, blank, blank, nothing, nothing,
        ),
        unroll=4,
    )
    far, total, direct, spots, slots, obs, touch, vals, errs = (related[3],) + related[6:]
    far_ref[0, 0] = jnp.max(far)
    base = (((spots >> 13) - chip + WINDOW) * CORES + ((spots >> 12) & 1)) * REPS
    totals = jnp.where(index == 0, total, direct)
    columns = (spots, base, slots * part_rows, obs, touch, totals)
    for number, column in enumerate(columns):
        table_ref[number : number + 1, :] = column.astype(jnp.float32)
    table_ref[6:7, :] = vals
    table_ref[7:8, :] = errs
    outs = [
        pltpu.make_async_copy(far_ref, far_out, small_sem.at[3]),
        pltpu.make_async_copy(table_ref, table_out, small_sem.at[4]),
    ]
    for out in outs:
        out.start()

    for n in shifts:

        @pl.when(later[n])
        def _(n=n):
            pl.semaphore_wait(late_sem.at[WINDOW + n], 1)
            send_block(n)

    for step in range(half):
        to_right[half + step].wait_recv()
        to_left[step].wait_recv()
    for relay in relays:
        relay.wait()
    for copy in to_right + to_left:
        copy.wait_send()
    pltpu.make_async_copy(nearby, nearby, near_send).wait()
    to_pair.wait_send()
    block_copy.wait()
    for out in outs:
        out.wait()

    for n in shifts:

        @pl.when(valid[n])
        def _(n=n):
            pltpu.make_async_copy(block(n), block(n), row_send.at[WINDOW + n]).wait()
            pltpu.make_async_copy(block(n), block(n), row_recv.at[WINDOW + n]).wait()


def gather(mesh, ensemble, locations, values, errors):
    part_rows, held = ensemble.shape
    dma = pltpu.SemaphoreType.DMA
    return pl.pallas_call(
        functools.partial(gather_kernel, mesh.shape["state"] // CORES, held),
        out_shape=(
            jax.ShapeDtypeStruct((ROWS, 1, TILE), jnp.float32),
            jax.ShapeDtypeStruct((REPS, part_rows, held), jnp.float32),
            jax.ShapeDtypeStruct((8, TILE), jnp.float32),
            jax.ShapeDtypeStruct((1, 1), jnp.int32),
        ),
        in_specs=[pl.BlockSpec(memory_space=pl.ANY)] * 4,
        out_specs=(pl.BlockSpec(memory_space=pl.ANY),) * 4,
        scratch_shapes=[
            pltpu.SMEM((NOBS,), jnp.int32),
            pltpu.SMEM((NOBS,), jnp.float32),
            pltpu.SMEM((NOBS,), jnp.float32),
            pltpu.SMEM((1, 1), jnp.int32),
            pltpu.VMEM((8, TILE), jnp.float32),
            dma((5,)), dma,
            pltpu.VMEM((part_rows, held), jnp.float32),
            pltpu.VMEM((held // TILE, part_rows, TILE), jnp.float32),
            pltpu.VMEM((1, 1, TILE), jnp.float32),
            dma, dma, pltpu.SemaphoreType.REGULAR((2 * WINDOW + 1,)),
            dma, dma, dma((2 * WINDOW + 1,)), dma((2 * WINDOW + 1,)),
            dma((CHUNKS,)), dma((CHUNKS,)), dma((CHUNKS,)), dma((CHUNKS,)),
            dma((CHUNKS,)), dma((CHUNKS,)), dma((CHUNKS,)), dma((CHUNKS,)),
        ],
        compiler_params=pltpu.CompilerParams(collective_id=0, has_side_effects=True),
        name="gather",
    )(locations, values, errors, ensemble)


def solve_kernel(
    windowed, held, table_ref, rows_ref, all_ref, out_ref,
    y_ref, u_ref, w_ref, center_ref, mutual_ref, tile_ref, done_ref, out_sem,
):
    state = lax.axis_index("state")
    rep = lax.axis_index("rep")
    part_rows = all_ref.shape[1]
    order = [(rep + step) & (REPS - 1) for step in range(REPS)]

    def entry(number, t):
        return table_ref[number, t].astype(jnp.int32)

    total = entry(5, 0)
    direct = entry(5, 1)
    diagonal = iota((part_rows, TILE), 1) - iota((part_rows, TILE), 0)

    def spread(t):
        spot = entry(0, t)
        if windowed:
            base = jnp.clip(entry(1, t), 0, ROWS - REPS)
            place = entry(2, t)
        else:
            base = entry(3, t) * REPS
            place = 0
        for step in range(REPS):
            row = jnp.broadcast_to(rows_ref[base + order[step]], (part_rows, TILE))
            column = jnp.sum(jnp.where(diagonal == place, row, 0.0), axis=1, keepdims=True)
            y_ref[t, step * part_rows : (step + 1) * part_rows, :] = jnp.broadcast_to(
                column, (part_rows, TILE)
            )
        center = ((spot >> 7) << 7).astype(jnp.float32) + (TILE - 1) * 0.5
        center_ref[pl.ds(t, 1), :] = jnp.full((1, TILE), center, jnp.float32)

    def spread_batch(b, carry):
        for i in range(BATCH):
            spread(b * BATCH + i)
        return carry

    def batches(number):
        return (number + BATCH - 1) // BATCH

    lax.fori_loop(0, batches(total), spread_batch, 0)

    tiles = held // TILE
    tile_centers = (state * held + iota((tiles, TILE), 0) * TILE).astype(jnp.float32) + (
        TILE - 1
    ) * 0.5

    def assimilate(i, carry):
        t = total - 1 - i
        spot = table_ref[0, t]
        error = table_ref[7, t]
        y = y_ref[t]
        mean = jnp.sum(y, axis=0, keepdims=True) * (1.0 / M)
        spread_of = y - mean
        variance = jnp.sum(spread_of * spread_of, axis=0, keepdims=True) * (1.0 / (M - 1))
        total_var = variance + error
        shrink = 1.0 / (1.0 + jnp.sqrt(error / total_var))
        u = spread_of * (1.0 / ((M - 1) * total_var))
        w = (table_ref[6, t] - mean) - shrink * spread_of
        u_ref[t] = u
        w_ref[t] = w
        mutual_ref[...] = taper(jnp.abs(center_ref[...] - spot))
        tile_ref[t] = taper(jnp.abs(tile_centers - spot))

        def update(b, inner):
            first = b * BATCH
            others = [y_ref[first + i] for i in range(BATCH)]
            for i, other in enumerate(others):
                projected = jnp.sum(u * other, axis=0, keepdims=True)
                others[i] = other + w * (mutual_ref[pl.ds(first + i, 1), :] * projected)
            for i, other in enumerate(others):
                y_ref[first + i] = other
            return inner

        lax.fori_loop(0, batches(t), update, 0)
        return carry

    lax.fori_loop(0, total, assimilate, 0)
    group = 8

    def apply(g, carry):
        spans = [
            pl.ds(pl.multiple_of((g * group + i) * TILE, TILE), TILE) for i in range(group)
        ]

        def one(d, values):
            t = entry(4, direct - 1 - d)
            u = u_ref[t]
            w = w_ref[t]
            result = []
            for i in range(group):
                projected = jnp.sum(u * values[i], axis=0, keepdims=True)
                weight = tile_ref[t, pl.ds(g * group + i, 1), :]
                result.append(values[i] + w * (weight * projected))
            return tuple(result)

        start = tuple(
            jnp.concatenate([all_ref[member, :, span] for member in order], axis=0)
            for span in spans
        )
        values = lax.fori_loop(0, direct, one, start)
        for span, value in zip(spans, values):
            done_ref[:, span] = value[:part_rows]
        width = group * TILE
        wide = pl.ds(pl.multiple_of(g * width, width), width)
        pltpu.make_async_copy(done_ref.at[:, wide], out_ref.at[:, wide], out_sem).start()
        return carry

    lax.fori_loop(0, tiles // group, apply, 0)
    pltpu.make_async_copy(done_ref, out_ref, out_sem).wait()


def solve(windowed, part_rows, held, table, rows, everything):
    vmem = pl.BlockSpec(memory_space=pltpu.VMEM)
    block = pltpu.VMEM((NOBS, M, TILE), jnp.float32)
    return pl.pallas_call(
        functools.partial(solve_kernel, windowed, held),
        out_shape=jax.ShapeDtypeStruct((part_rows, held), jnp.float32),
        in_specs=[pl.BlockSpec(memory_space=pltpu.SMEM), vmem, vmem],
        out_specs=pl.BlockSpec(memory_space=pl.ANY),
        compiler_params=pltpu.CompilerParams(vmem_limit_bytes=65918864),
        scratch_shapes=[
            block, block, block,
            pltpu.VMEM((NOBS, TILE), jnp.float32),
            pltpu.VMEM((NOBS, TILE), jnp.float32),
            pltpu.VMEM((NOBS, held // TILE, TILE), jnp.float32),
            pltpu.VMEM((part_rows, held), jnp.float32),
            pltpu.SemaphoreType.DMA,
        ],
        name="solve",
    )(table, rows, everything)


def full_rows(mesh, ensemble, locations):
    part_rows, held = ensemble.shape
    states = mesh.shape["state"]
    offsets = locations - lax.axis_index("state") * held
    inside = ((offsets >= 0) & (offsets < held)).astype(jnp.float32)
    columns = jnp.take(ensemble, jnp.clip(offsets, 0, held - 1), axis=1) * inside[None, :]
    placed = jnp.zeros((REPS, part_rows, NOBS), jnp.float32)
    placed = lax.dynamic_update_slice(placed, columns[None], (lax.axis_index("rep"), 0, 0))
    stride = 1
    while stride < states:
        pairs = [(i, i ^ stride) for i in range(states)]
        placed = placed + lax.ppermute(placed, "state", pairs)
        stride *= 2
    stride = 1
    while stride < REPS:
        pairs = [(i, i ^ stride) for i in range(REPS)]
        placed = placed + lax.ppermute(placed, "rep", pairs)
        stride *= 2
    by_obs = jnp.transpose(placed, (2, 0, 1)).reshape(NOBS * REPS, 1, part_rows)
    return jnp.pad(by_obs, ((0, 0), (0, 0), (0, TILE - part_rows)))


def on_device(mesh, ensemble, obs_values, obs_error, obs_location):
    part_rows, held = ensemble.shape
    rows, everything, table, far = gather(mesh, ensemble, obs_location, obs_values, obs_error)
    return lax.switch(
        far[0, 0],
        (
            lambda: solve(True, part_rows, held, table, rows, everything),
            lambda: solve(
                False, part_rows, held, table, full_rows(mesh, ensemble, obs_location), everything
            ),
        ),
    )


def solution(mesh):
    in_specs = (P("rep", "state"), P(), P(), P())
    out_specs = P("rep", "state")
    return jax.shard_map(
        functools.partial(on_device, mesh),
        mesh=mesh,
        in_specs=in_specs,
        out_specs=out_specs,
        check_vma=False,
    )
```

```python
import functools

import jax
import jax.numpy as jnp
from jax import lax
from jax.experimental import pallas as pl
from jax.experimental.pallas import tpu as pltpu
from jax.sharding import PartitionSpec as P

MESH = pl.DeviceIdType.MESH
M = 64
TILE = 128
HALF = 4096
REACH = 2 * HALF
LINK = REACH + TILE // 2
NOBS = 48
REPS = 4
CORES = 2
WINDOW = 4
DEPTH = 16
SLOTS = 8
CHUNKS = 4
BATCH = 4
ROWS = (2 * WINDOW + 1) * CORES * REPS


def taper(distance):
    ratio = distance * (1.0 / HALF)
    near_part = (((-0.25 * ratio + 0.5) * ratio + 0.625) * ratio - 5.0 / 3.0) * ratio * ratio + 1.0
    ratio_far = jnp.maximum(ratio, 1.0)
    far_part = (
        ((((ratio_far / 12.0 - 0.5) * ratio_far + 0.625) * ratio_far + 5.0 / 3.0) * ratio_far - 5.0)
        * ratio_far
        + 4.0
        - 2.0 / (3.0 * ratio_far)
    )
    return jnp.where(
        ratio <= 1.0, near_part, jnp.where(ratio < 2.0, far_part, jnp.zeros_like(ratio))
    )


def iota(shape, axis):
    return lax.broadcasted_iota(jnp.int32, shape, axis)


def gather_kernel(
    chips, held, loc_any, val_any, err_any, ens_ref, rows_ref, all_ref, table_out, far_out,
    loc_ref, val_ref, err_ref, far_ref, table_ref, small_sem, block_sem, fetch_ref, local_ref, pick_ref, local_sem, own_sem, late_sem, near_send, near_recv, row_send, row_recv,
    send_right, send_left, recv_left, recv_right, pass_right, pass_left, far_left, far_right,
):
    state = lax.axis_index("state")
    rep = lax.axis_index("rep")
    chip = state >> 1
    core = state & 1
    part_rows = ens_ref.shape[0]
    tiles = held // TILE

    depth = chip & (DEPTH - 1)
    shifts = list(range(1, WINDOW + 1)) + list(range(-1, -WINDOW - 1, -1))
    valid = {n: (chip + n >= 0) & (chip + n < chips) for n in shifts}

    def key(place):
        return place + jnp.where((place >> 2) == 2, DEPTH, 0)

    ahead = {n: key((depth + n) & (DEPTH - 1)) > key(depth) for n in shifts}
    later = {n: valid[n] & ahead[n] for n in shifts}
    earlier = {n: valid[n] & jnp.logical_not(ahead[n]) for n in shifts}
    members = [(c, r) for c in range(CORES) for r in range(REPS)]
    beside = members[1:]
    peers = members[1:REPS]
    pair = members[REPS]
    cores_of = [core, 1 - core]
    reps_of = [(rep + r) & (REPS - 1) for r in range(REPS)]

    def target(shift, member):
        return (chip + shift) * CORES + cores_of[member[0]], reps_of[member[1]]

    def signal(semaphore, shift, member):
        pl.semaphore_signal(
            semaphore, inc=1, device_id=target(shift, member), device_id_type=MESH
        )

    def count_of(flags):
        return sum(flags[n].astype(jnp.int32) for n in shifts)

    right = (state, reps_of[1])
    left = (state, reps_of[3])
    width = held // CHUNKS

    def piece(ref, chunk):
        return ref.at[:, pl.ds(chunk * width, width)]

    def bulk(source, owner, chunk, target, send_sem, recv_sem):
        return pltpu.make_async_remote_copy(
            src_ref=piece(source, chunk),
            dst_ref=piece(all_ref.at[owner], chunk),
            send_sem=send_sem.at[chunk],
            recv_sem=recv_sem.at[chunk],
            device_id=target,
            device_id_type=MESH,
        )

    half = CHUNKS // 2
    to_right = [bulk(ens_ref, rep, c, right, send_right, recv_left) for c in range(CHUNKS)]
    to_left = [bulk(ens_ref, rep, c, left, send_left, recv_right) for c in range(CHUNKS)]
    barrier = pltpu.get_barrier_semaphore()

    def straight(n):
        other = depth + n
        apart = (chip + n) ^ chip
        low = (depth > 0) & (other > 0) & (depth < DEPTH // 2) & (other < DEPTH // 2)
        return valid[n] & (((apart & (DEPTH // 2)) != 0) | (low & ((apart & WINDOW) != 0)))

    crosses = {n: straight(n) for n in shifts}
    greetings = (
        len(peers)
        + (1 - core)
        + count_of(earlier)
        + (len(members) - 1) * count_of({n: earlier[n] & crosses[n] for n in shifts})
    )
    for member in peers:
        signal(barrier, 0, member)

    @pl.when(core == 1)
    def _():
        signal(barrier, 0, pair)

    load = pltpu.make_async_copy(ens_ref, fetch_ref, local_sem)
    load.start()
    smalls = [
        pltpu.make_async_copy(loc_any, loc_ref, small_sem.at[0]),
        pltpu.make_async_copy(val_any, val_ref, small_sem.at[1]),
        pltpu.make_async_copy(err_any, err_ref, small_sem.at[2]),
    ]
    for small in smalls:
        small.start()

    for n in shifts:

        @pl.when(later[n])
        def _(n=n):
            signal(barrier, n, members[0])

    for n in shifts:

        @pl.when(later[n] & crosses[n])
        def _(n=n):
            for member in beside:
                signal(barrier, n, member)

    smalls[0].wait()
    load.wait()
    block_copy = pltpu.make_async_copy(fetch_ref, all_ref.at[rep], block_sem)
    block_copy.start()
    for tile in range(tiles):
        local_ref[tile] = fetch_ref[:, tile * TILE : (tile + 1) * TILE]
    lane = iota((part_rows, TILE), 1)
    diagonal = lane - iota((part_rows, TILE), 0)
    rank = jnp.int32(0)
    packed = jnp.zeros((part_rows, TILE), jnp.float32)
    for j in range(NOBS):
        offset = loc_ref[j] - state * held
        inside = (offset >= 0) & (offset < held)
        safe = jnp.clip(offset, 0, held - 1)
        tile = local_ref[safe >> 7]
        wanted = jnp.where(inside, safe & (TILE - 1), -1)
        column = jnp.sum(jnp.where(lane == wanted, tile, 0.0), axis=1, keepdims=True)
        place = jnp.where(inside, rank * part_rows, -TILE * 2)
        packed = jnp.where(diagonal == place, column, packed)
        rank = rank + inside.astype(jnp.int32)
    pick_ref[0] = jnp.sum(packed, axis=0, keepdims=True)

    pl.semaphore_wait(barrier, greetings)

    def send_row(shift, member):
        slot = ((WINDOW - shift) * CORES + core) * REPS + rep
        pltpu.make_async_remote_copy(
            src_ref=pick_ref.at[0],
            dst_ref=rows_ref.at[slot],
            send_sem=row_send.at[WINDOW + shift],
            recv_sem=row_recv.at[WINDOW - shift],
            device_id=target(shift, member),
            device_id_type=MESH,
        ).start()

    for n in sorted(shifts, key=abs, reverse=True):

        @pl.when(earlier[n] & crosses[n])
        def _(n=n):
            for member in members:
                send_row(n, member)

    own_row = (WINDOW * CORES + core) * REPS + rep
    for member in peers:
        pltpu.make_async_remote_copy(
            src_ref=pick_ref.at[0],
            dst_ref=rows_ref.at[own_row],
            send_sem=near_send,
            recv_sem=near_recv,
            device_id=target(0, member),
            device_id_type=MESH,
        ).start()
    own = pltpu.make_async_copy(pick_ref.at[0], rows_ref.at[own_row], own_sem)
    own.start()

    @pl.when(core == 0)
    def _():
        signal(late_sem.at[WINDOW], 0, pair)

    for n in shifts:

        @pl.when(earlier[n])
        def _(n=n):
            signal(late_sem.at[WINDOW - n], n, members[0])

    def block(shift, number=len(members)):
        return rows_ref.at[pl.ds((WINDOW + shift) * len(members), number)]

    def send_block(shift):
        pltpu.make_async_remote_copy(
            src_ref=block(0),
            dst_ref=block(-shift),
            send_sem=row_send.at[WINDOW + shift],
            recv_sem=row_recv.at[WINDOW - shift],
            device_id=target(shift, members[0]),
            device_id_type=MESH,
        ).start()

    for step in range(CHUNKS):
        to_right[step].start()
        to_left[(step + half) % CHUNKS].start()

    half_block = rows_ref.at[pl.ds(WINDOW * len(members) + core * REPS, REPS)]
    to_pair = pltpu.make_async_remote_copy(
        src_ref=half_block,
        dst_ref=half_block,
        send_sem=row_send.at[WINDOW],
        recv_sem=row_recv.at[WINDOW],
        device_id=target(0, pair),
        device_id_type=MESH,
    )
    own.wait()
    nearby = block(0, len(peers))
    pltpu.make_async_copy(nearby, nearby, near_recv).wait()

    @pl.when(core == 1)
    def _():
        pl.semaphore_wait(late_sem.at[WINDOW], 1)

    to_pair.start()
    to_pair.wait_recv()
    for n in shifts:

        @pl.when(earlier[n] & jnp.logical_not(crosses[n]))
        def _(n=n):
            send_block(n)

    relays = []
    for step in range(half):
        to_right[step].wait_recv()
        relay = bulk(all_ref.at[left[1]], left[1], step, right, pass_right, far_left)
        relay.start()
        relays.append(relay)
        to_left[half + step].wait_recv()
        relay = bulk(all_ref.at[right[1]], right[1], half + step, left, pass_left, far_right)
        relay.start()
        relays.append(relay)

    smalls[1].wait()
    smalls[2].wait()
    shards = iota((8, TILE), 1)
    first = shards * held
    zeros = jnp.zeros((8, TILE), jnp.int32)
    blank = jnp.zeros((1, TILE), jnp.int32)
    index = iota((1, TILE), 1)
    own_low = state * held - REACH
    own_high = state * held + held + REACH

    def relate(i, carry):
        lows, highs, count, far, low, high, total, direct, spots, slots, obs, touch, vals, errs = carry
        j = NOBS - 1 - i
        spot = loc_ref[j]
        near = (spot >= lows) & (spot <= highs)
        away = jnp.abs((spot >> 13) - (shards >> 1)) > WINDOW
        count = count + ((spot >> 12) == shards).astype(jnp.int32)
        far = jnp.where((near & away) | (count > SLOTS), 1, far)
        lows = jnp.where(near, jnp.minimum(lows, spot - LINK), lows)
        highs = jnp.where(near, jnp.maximum(highs, spot + LINK), highs)
        here = (spot >= low) & (spot <= high)
        low = jnp.where(here, jnp.minimum(low, spot - LINK), low)
        high = jnp.where(here, jnp.maximum(high, spot + LINK), high)
        touches = (spot >= own_low) & (spot <= own_high)
        slots = slots + ((spots >> 12) == (spot >> 12)).astype(jnp.int32)
        place = index == jnp.where(here, total, -1)
        spots = jnp.where(place, spot, spots)
        slots = jnp.where(place, 0, slots)
        obs = jnp.where(place, j, obs)
        vals = jnp.where(place, val_ref[j], vals)
        errs = jnp.where(place, err_ref[j], errs)
        touch = jnp.where(index == jnp.where(touches, direct, -1), total, touch)
        total = total + here.astype(jnp.int32)
        direct = direct + touches.astype(jnp.int32)
        return lows, highs, count, far, low, high, total, direct, spots, slots, obs, touch, vals, errs

    nothing = jnp.zeros((1, TILE), jnp.float32)
    related = lax.fori_loop(
        0,
        NOBS,
        relate,
        (
            first - REACH, first + held + REACH, zeros, zeros, own_low, own_high,
            jnp.int32(0), jnp.int32(0), blank - held, blank, blank, blank, nothing, nothing,
        ),
        unroll=4,
    )
    far, total, direct, spots, slots, obs, touch, vals, errs = (related[3],) + related[6:]
    far_ref[0, 0] = jnp.max(far)
    base = (((spots >> 13) - chip + WINDOW) * CORES + ((spots >> 12) & 1)) * REPS
    totals = jnp.where(index == 0, total, direct)
    columns = (spots, base, slots * part_rows, obs, touch, totals)
    for number, column in enumerate(columns):
        table_ref[number : number + 1, :] = column.astype(jnp.float32)
    table_ref[6:7, :] = vals
    table_ref[7:8, :] = errs
    outs = [
        pltpu.make_async_copy(far_ref, far_out, small_sem.at[3]),
        pltpu.make_async_copy(table_ref, table_out, small_sem.at[4]),
    ]
    for out in outs:
        out.start()

    for n in shifts:

        @pl.when(later[n])
        def _(n=n):
            pl.semaphore_wait(late_sem.at[WINDOW + n], 1)
            send_block(n)

    for step in range(half):
        to_right[half + step].wait_recv()
        to_left[step].wait_recv()
    for relay in relays:
        relay.wait()
    for copy in to_right + to_left:
        copy.wait_send()
    pltpu.make_async_copy(nearby, nearby, near_send).wait()
    to_pair.wait_send()
    block_copy.wait()
    for out in outs:
        out.wait()

    for n in shifts:

        @pl.when(valid[n])
        def _(n=n):
            pltpu.make_async_copy(block(n), block(n), row_send.at[WINDOW + n]).wait()
            pltpu.make_async_copy(block(n), block(n), row_recv.at[WINDOW + n]).wait()


def gather(mesh, ensemble, locations, values, errors):
    part_rows, held = ensemble.shape
    dma = pltpu.SemaphoreType.DMA
    return pl.pallas_call(
        functools.partial(gather_kernel, mesh.shape["state"] // CORES, held),
        out_shape=(
            jax.ShapeDtypeStruct((ROWS, 1, TILE), jnp.float32),
            jax.ShapeDtypeStruct((REPS, part_rows, held), jnp.float32),
            jax.ShapeDtypeStruct((8, TILE), jnp.float32),
            jax.ShapeDtypeStruct((1, 1), jnp.int32),
        ),
        in_specs=[pl.BlockSpec(memory_space=pl.ANY)] * 4,
        out_specs=(pl.BlockSpec(memory_space=pl.ANY),) * 4,
        scratch_shapes=[
            pltpu.SMEM((NOBS,), jnp.int32),
            pltpu.SMEM((NOBS,), jnp.float32),
            pltpu.SMEM((NOBS,), jnp.float32),
            pltpu.SMEM((1, 1), jnp.int32),
            pltpu.VMEM((8, TILE), jnp.float32),
            dma((5,)), dma,
            pltpu.VMEM((part_rows, held), jnp.float32),
            pltpu.VMEM((held // TILE, part_rows, TILE), jnp.float32),
            pltpu.VMEM((1, 1, TILE), jnp.float32),
            dma, dma, pltpu.SemaphoreType.REGULAR((2 * WINDOW + 1,)),
            dma, dma, dma((2 * WINDOW + 1,)), dma((2 * WINDOW + 1,)),
            dma((CHUNKS,)), dma((CHUNKS,)), dma((CHUNKS,)), dma((CHUNKS,)),
            dma((CHUNKS,)), dma((CHUNKS,)), dma((CHUNKS,)), dma((CHUNKS,)),
        ],
        compiler_params=pltpu.CompilerParams(collective_id=0, has_side_effects=True),
        name="gather",
    )(locations, values, errors, ensemble)


def solve_kernel(
    windowed, held, table_ref, rows_ref, all_ref, out_ref,
    y_ref, u_ref, w_ref, center_ref, mutual_ref, tile_ref, done_ref, out_sem,
):
    state = lax.axis_index("state")
    rep = lax.axis_index("rep")
    part_rows = all_ref.shape[1]
    order = [(rep + step) & (REPS - 1) for step in range(REPS)]

    def entry(number, t):
        return table_ref[number, t].astype(jnp.int32)

    total = entry(5, 0)
    direct = entry(5, 1)
    diagonal = iota((part_rows, TILE), 1) - iota((part_rows, TILE), 0)

    def spread(t):
        spot = entry(0, t)
        if windowed:
            base = jnp.clip(entry(1, t), 0, ROWS - REPS)
            place = entry(2, t)
        else:
            base = entry(3, t) * REPS
            place = 0
        for step in range(REPS):
            row = jnp.broadcast_to(rows_ref[base + order[step]], (part_rows, TILE))
            column = jnp.sum(jnp.where(diagonal == place, row, 0.0), axis=1, keepdims=True)
            y_ref[t, step * part_rows : (step + 1) * part_rows, :] = jnp.broadcast_to(
                column, (part_rows, TILE)
            )
        center = ((spot >> 7) << 7).astype(jnp.float32) + (TILE - 1) * 0.5
        center_ref[pl.ds(t, 1), :] = jnp.full((1, TILE), center, jnp.float32)

    def spread_batch(b, carry):
        for i in range(BATCH):
            spread(b * BATCH + i)
        return carry

    def batches(number):
        return (number + BATCH - 1) // BATCH

    lax.fori_loop(0, batches(total), spread_batch, 0)

    tiles = held // TILE
    tile_centers = (state * held + iota((tiles, TILE), 0) * TILE).astype(jnp.float32) + (
        TILE - 1
    ) * 0.5

    def assimilate(i, carry):
        t = total - 1 - i
        spot = table_ref[0, t]
        error = table_ref[7, t]
        y = y_ref[t]
        mean = jnp.sum(y, axis=0, keepdims=True) * (1.0 / M)
        spread_of = y - mean
        variance = jnp.sum(spread_of * spread_of, axis=0, keepdims=True) * (1.0 / (M - 1))
        total_var = variance + error
        shrink = 1.0 / (1.0 + jnp.sqrt(error / total_var))
        u = spread_of * (1.0 / ((M - 1) * total_var))
        w = (table_ref[6, t] - mean) - shrink * spread_of
        u_ref[t] = u
        w_ref[t] = w
        mutual_ref[...] = taper(jnp.abs(center_ref[...] - spot))
        tile_ref[t] = taper(jnp.abs(tile_centers - spot))

        def update(b, inner):
            first = b * BATCH
            others = [y_ref[first + i] for i in range(BATCH)]
            for i, other in enumerate(others):
                projected = jnp.sum(u * other, axis=0, keepdims=True)
                others[i] = other + w * (mutual_ref[pl.ds(first + i, 1), :] * projected)
            for i, other in enumerate(others):
                y_ref[first + i] = other
            return inner

        lax.fori_loop(0, batches(t), update, 0)
        return carry

    lax.fori_loop(0, total, assimilate, 0)
    group = 4

    def apply(g, carry):
        spans = [
            pl.ds(pl.multiple_of((g * group + i) * TILE, TILE), TILE) for i in range(group)
        ]

        def one(d, values):
            t = entry(4, direct - 1 - d)
            u = u_ref[t]
            w = w_ref[t]
            result = []
            for i in range(group):
                projected = jnp.sum(u * values[i], axis=0, keepdims=True)
                weight = tile_ref[t, pl.ds(g * group + i, 1), :]
                result.append(values[i] + w * (weight * projected))
            return tuple(result)

        start = tuple(
            jnp.concatenate([all_ref[member, :, span] for member in order], axis=0)
            for span in spans
        )
        values = lax.fori_loop(0, direct, one, start)
        for span, value in zip(spans, values):
            done_ref[:, span] = value[:part_rows]
        width = group * TILE
        wide = pl.ds(pl.multiple_of(g * width, width), width)
        pltpu.make_async_copy(done_ref.at[:, wide], out_ref.at[:, wide], out_sem).start()
        return carry

    lax.fori_loop(0, tiles // group, apply, 0)
    pltpu.make_async_copy(done_ref, out_ref, out_sem).wait()


def solve(windowed, part_rows, held, table, rows, everything):
    vmem = pl.BlockSpec(memory_space=pltpu.VMEM)
    block = pltpu.VMEM((NOBS, M, TILE), jnp.float32)
    return pl.pallas_call(
        functools.partial(solve_kernel, windowed, held),
        out_shape=jax.ShapeDtypeStruct((part_rows, held), jnp.float32),
        in_specs=[pl.BlockSpec(memory_space=pltpu.SMEM), vmem, vmem],
        out_specs=pl.BlockSpec(memory_space=pl.ANY),
        compiler_params=pltpu.CompilerParams(vmem_limit_bytes=65918864),
        scratch_shapes=[
            block, block, block,
            pltpu.VMEM((NOBS, TILE), jnp.float32),
            pltpu.VMEM((NOBS, TILE), jnp.float32),
            pltpu.VMEM((NOBS, held // TILE, TILE), jnp.float32),
            pltpu.VMEM((part_rows, held), jnp.float32),
            pltpu.SemaphoreType.DMA,
        ],
        name="solve",
    )(table, rows, everything)


def full_rows(mesh, ensemble, locations):
    part_rows, held = ensemble.shape
    states = mesh.shape["state"]
    offsets = locations - lax.axis_index("state") * held
    inside = ((offsets >= 0) & (offsets < held)).astype(jnp.float32)
    columns = jnp.take(ensemble, jnp.clip(offsets, 0, held - 1), axis=1) * inside[None, :]
    placed = jnp.zeros((REPS, part_rows, NOBS), jnp.float32)
    placed = lax.dynamic_update_slice(placed, columns[None], (lax.axis_index("rep"), 0, 0))
    stride = 1
    while stride < states:
        pairs = [(i, i ^ stride) for i in range(states)]
        placed = placed + lax.ppermute(placed, "state", pairs)
        stride *= 2
    stride = 1
    while stride < REPS:
        pairs = [(i, i ^ stride) for i in range(REPS)]
        placed = placed + lax.ppermute(placed, "rep", pairs)
        stride *= 2
    by_obs = jnp.transpose(placed, (2, 0, 1)).reshape(NOBS * REPS, 1, part_rows)
    return jnp.pad(by_obs, ((0, 0), (0, 0), (0, TILE - part_rows)))


def on_device(mesh, ensemble, obs_values, obs_error, obs_location):
    part_rows, held = ensemble.shape
    rows, everything, table, far = gather(mesh, ensemble, obs_location, obs_values, obs_error)
    return lax.switch(
        far[0, 0],
        (
            lambda: solve(True, part_rows, held, table, rows, everything),
            lambda: solve(
                False, part_rows, held, table, full_rows(mesh, ensemble, obs_location), everything
            ),
        ),
    )


def solution(mesh):
    in_specs = (P("rep", "state"), P(), P(), P())
    out_specs = P("rep", "state")
    return jax.shard_map(
        functools.partial(on_device, mesh),
        mesh=mesh,
        in_specs=in_specs,
        out_specs=out_specs,
        check_vma=False,
    )
```

```python
import functools

import jax
import jax.numpy as jnp
from jax import lax
from jax.experimental import pallas as pl
from jax.experimental.pallas import tpu as pltpu
from jax.sharding import PartitionSpec as P

MESH = pl.DeviceIdType.MESH
M = 64
TILE = 128
HALF = 4096
REACH = 2 * HALF
LINK = REACH + TILE // 2
NOBS = 48
REPS = 4
CORES = 2
WINDOW = 4
DEPTH = 16
SLOTS = 8
CHUNKS = 4
BATCH = 4
ROWS = (2 * WINDOW + 1) * CORES * REPS


def taper(distance):
    ratio = distance * (1.0 / HALF)
    near_part = (((-0.25 * ratio + 0.5) * ratio + 0.625) * ratio - 5.0 / 3.0) * ratio * ratio + 1.0
    ratio_far = jnp.maximum(ratio, 1.0)
    far_part = (
        ((((ratio_far / 12.0 - 0.5) * ratio_far + 0.625) * ratio_far + 5.0 / 3.0) * ratio_far - 5.0)
        * ratio_far
        + 4.0
        - 2.0 / (3.0 * ratio_far)
    )
    return jnp.where(
        ratio <= 1.0, near_part, jnp.where(ratio < 2.0, far_part, jnp.zeros_like(ratio))
    )


def iota(shape, axis):
    return lax.broadcasted_iota(jnp.int32, shape, axis)


def gather_kernel(
    chips, held, loc_any, val_any, err_any, ens_ref, rows_ref, all_ref, table_out, far_out,
    loc_ref, val_ref, err_ref, far_ref, table_ref, small_sem, block_sem, fetch_ref, local_ref, pick_ref, local_sem, own_sem, late_sem, near_send, near_recv, row_send, row_recv,
    send_right, send_left, recv_left, recv_right, pass_right, pass_left, far_left, far_right,
):
    state = lax.axis_index("state")
    rep = lax.axis_index("rep")
    chip = state >> 1
    core = state & 1
    part_rows = ens_ref.shape[0]
    tiles = held // TILE

    depth = chip & (DEPTH - 1)
    shifts = list(range(1, WINDOW + 1)) + list(range(-1, -WINDOW - 1, -1))
    valid = {n: (chip + n >= 0) & (chip + n < chips) for n in shifts}

    def key(place):
        return place + jnp.where((place >> 2) == 2, DEPTH, 0)

    ahead = {n: key((depth + n) & (DEPTH - 1)) > key(depth) for n in shifts}
    later = {n: valid[n] & ahead[n] for n in shifts}
    earlier = {n: valid[n] & jnp.logical_not(ahead[n]) for n in shifts}
    members = [(c, r) for c in range(CORES) for r in range(REPS)]
    beside = members[1:]
    peers = members[1:REPS]
    pair = members[REPS]
    cores_of = [core, 1 - core]
    reps_of = [(rep + r) & (REPS - 1) for r in range(REPS)]

    def target(shift, member):
        return (chip + shift) * CORES + cores_of[member[0]], reps_of[member[1]]

    def signal(semaphore, shift, member):
        pl.semaphore_signal(
            semaphore, inc=1, device_id=target(shift, member), device_id_type=MESH
        )

    def count_of(flags):
        return sum(flags[n].astype(jnp.int32) for n in shifts)

    right = (state, reps_of[1])
    left = (state, reps_of[3])
    width = held // CHUNKS

    def piece(ref, chunk):
        return ref.at[:, pl.ds(chunk * width, width)]

    def bulk(source, owner, chunk, target, send_sem, recv_sem):
        return pltpu.make_async_remote_copy(
            src_ref=piece(source, chunk),
            dst_ref=piece(all_ref.at[owner], chunk),
            send_sem=send_sem.at[chunk],
            recv_sem=recv_sem.at[chunk],
            device_id=target,
            device_id_type=MESH,
        )

    half = CHUNKS // 2
    to_right = [bulk(ens_ref, rep, c, right, send_right, recv_left) for c in range(CHUNKS)]
    to_left = [bulk(ens_ref, rep, c, left, send_left, recv_right) for c in range(CHUNKS)]
    barrier = pltpu.get_barrier_semaphore()

    def straight(n):
        other = depth + n
        apart = (chip + n) ^ chip
        low = (depth > 0) & (other > 0) & (depth < DEPTH // 2) & (other < DEPTH // 2)
        return valid[n] & (((apart & (DEPTH // 2)) != 0) | (low & ((apart & WINDOW) != 0)))

    crosses = {n: straight(n) for n in shifts}
    greetings = (
        len(peers)
        + (1 - core)
        + count_of(earlier)
        + (len(members) - 1) * count_of({n: earlier[n] & crosses[n] for n in shifts})
    )
    for member in peers:
        signal(barrier, 0, member)

    @pl.when(core == 1)
    def _():
        signal(barrier, 0, pair)

    load = pltpu.make_async_copy(ens_ref, fetch_ref, local_sem)
    load.start()
    smalls = [
        pltpu.make_async_copy(loc_any, loc_ref, small_sem.at[0]),
        pltpu.make_async_copy(val_any, val_ref, small_sem.at[1]),
        pltpu.make_async_copy(err_any, err_ref, small_sem.at[2]),
    ]
    for small in smalls:
        small.start()

    for n in shifts:

        @pl.when(later[n])
        def _(n=n):
            signal(barrier, n, members[0])

    for n in shifts:

        @pl.when(later[n] & crosses[n])
        def _(n=n):
            for member in beside:
                signal(barrier, n, member)

    smalls[0].wait()
    load.wait()
    block_copy = pltpu.make_async_copy(fetch_ref, all_ref.at[rep], block_sem)
    block_copy.start()
    for tile in range(tiles):
        local_ref[tile] = fetch_ref[:, tile * TILE : (tile + 1) * TILE]
    lane = iota((part_rows, TILE), 1)
    diagonal = lane - iota((part_rows, TILE), 0)
    rank = jnp.int32(0)
    packed = jnp.zeros((part_rows, TILE), jnp.float32)
    for j in range(NOBS):
        offset = loc_ref[j] - state * held
        inside = (offset >= 0) & (offset < held)
        safe = jnp.clip(offset, 0, held - 1)
        tile = local_ref[safe >> 7]
        wanted = jnp.where(inside, safe & (TILE - 1), -1)
        column = jnp.sum(jnp.where(lane == wanted, tile, 0.0), axis=1, keepdims=True)
        place = jnp.where(inside, rank * part_rows, -TILE * 2)
        packed = jnp.where(diagonal == place, column, packed)
        rank = rank + inside.astype(jnp.int32)
    pick_ref[0] = jnp.sum(packed, axis=0, keepdims=True)

    pl.semaphore_wait(barrier, greetings)

    def send_row(shift, member):
        slot = ((WINDOW - shift) * CORES + core) * REPS + rep
        pltpu.make_async_remote_copy(
            src_ref=pick_ref.at[0],
            dst_ref=rows_ref.at[slot],
            send_sem=row_send.at[WINDOW + shift],
            recv_sem=row_recv.at[WINDOW - shift],
            device_id=target(shift, member),
            device_id_type=MESH,
        ).start()

    for n in sorted(shifts, key=abs, reverse=True):

        @pl.when(earlier[n] & crosses[n])
        def _(n=n):
            for member in members:
                send_row(n, member)

    own_row = (WINDOW * CORES + core) * REPS + rep
    for member in peers:
        pltpu.make_async_remote_copy(
            src_ref=pick_ref.at[0],
            dst_ref=rows_ref.at[own_row],
            send_sem=near_send,
            recv_sem=near_recv,
            device_id=target(0, member),
            device_id_type=MESH,
        ).start()
    own = pltpu.make_async_copy(pick_ref.at[0], rows_ref.at[own_row], own_sem)
    own.start()

    @pl.when(core == 0)
    def _():
        signal(late_sem.at[WINDOW], 0, pair)

    for n in shifts:

        @pl.when(earlier[n])
        def _(n=n):
            signal(late_sem.at[WINDOW - n], n, members[0])

    def block(shift, number=len(members)):
        return rows_ref.at[pl.ds((WINDOW + shift) * len(members), number)]

    def send_block(shift):
        pltpu.make_async_remote_copy(
            src_ref=block(0),
            dst_ref=block(-shift),
            send_sem=row_send.at[WINDOW + shift],
            recv_sem=row_recv.at[WINDOW - shift],
            device_id=target(shift, members[0]),
            device_id_type=MESH,
        ).start()

    for step in range(CHUNKS):
        to_right[step].start()
        to_left[(step + half) % CHUNKS].start()

    half_block = rows_ref.at[pl.ds(WINDOW * len(members) + core * REPS, REPS)]
    to_pair = pltpu.make_async_remote_copy(
        src_ref=half_block,
        dst_ref=half_block,
        send_sem=row_send.at[WINDOW],
        recv_sem=row_recv.at[WINDOW],
        device_id=target(0, pair),
        device_id_type=MESH,
    )
    own.wait()
    nearby = block(0, len(peers))
    pltpu.make_async_copy(nearby, nearby, near_recv).wait()

    @pl.when(core == 1)
    def _():
        pl.semaphore_wait(late_sem.at[WINDOW], 1)

    to_pair.start()
    to_pair.wait_recv()
    for n in shifts:

        @pl.when(earlier[n] & jnp.logical_not(crosses[n]))
        def _(n=n):
            send_block(n)

    relays = []
    for step in range(half):
        to_right[step].wait_recv()
        relay = bulk(all_ref.at[left[1]], left[1], step, right, pass_right, far_left)
        relay.start()
        relays.append(relay)
        to_left[half + step].wait_recv()
        relay = bulk(all_ref.at[right[1]], right[1], half + step, left, pass_left, far_right)
        relay.start()
        relays.append(relay)

    smalls[1].wait()
    smalls[2].wait()
    shards = iota((8, TILE), 1)
    first = shards * held
    zeros = jnp.zeros((8, TILE), jnp.int32)
    blank = jnp.zeros((1, TILE), jnp.int32)
    index = iota((1, TILE), 1)
    own_low = state * held - REACH
    own_high = state * held + held + REACH

    def relate(i, carry):
        lows, highs, count, far, low, high, total, direct, spots, slots, obs, touch, vals, errs = carry
        j = NOBS - 1 - i
        spot = loc_ref[j]
        near = (spot >= lows) & (spot <= highs)
        away = jnp.abs((spot >> 13) - (shards >> 1)) > WINDOW
        count = count + ((spot >> 12) == shards).astype(jnp.int32)
        far = jnp.where((near & away) | (count > SLOTS), 1, far)
        lows = jnp.where(near, jnp.minimum(lows, spot - LINK), lows)
        highs = jnp.where(near, jnp.maximum(highs, spot + LINK), highs)
        here = (spot >= low) & (spot <= high)
        low = jnp.where(here, jnp.minimum(low, spot - LINK), low)
        high = jnp.where(here, jnp.maximum(high, spot + LINK), high)
        touches = (spot >= own_low) & (spot <= own_high)
        slots = slots + ((spots >> 12) == (spot >> 12)).astype(jnp.int32)
        place = index == jnp.where(here, total, -1)
        spots = jnp.where(place, spot, spots)
        slots = jnp.where(place, 0, slots)
        obs = jnp.where(place, j, obs)
        vals = jnp.where(place, val_ref[j], vals)
        errs = jnp.where(place, err_ref[j], errs)
        touch = jnp.where(index == jnp.where(touches, direct, -1), total, touch)
        total = total + here.astype(jnp.int32)
        direct = direct + touches.astype(jnp.int32)
        return lows, highs, count, far, low, high, total, direct, spots, slots, obs, touch, vals, errs

    nothing = jnp.zeros((1, TILE), jnp.float32)
    related = lax.fori_loop(
        0,
        NOBS,
        relate,
        (
            first - REACH, first + held + REACH, zeros, zeros, own_low, own_high,
            jnp.int32(0), jnp.int32(0), blank - held, blank, blank, blank, nothing, nothing,
        ),
        unroll=4,
    )
    far, total, direct, spots, slots, obs, touch, vals, errs = (related[3],) + related[6:]
    far_ref[0, 0] = jnp.max(far)
    base = (((spots >> 13) - chip + WINDOW) * CORES + ((spots >> 12) & 1)) * REPS
    totals = jnp.where(index == 0, total, direct)
    columns = (spots, base, slots * part_rows, obs, touch, totals)
    for number, column in enumerate(columns):
        table_ref[number : number + 1, :] = column.astype(jnp.float32)
    table_ref[6:7, :] = vals
    table_ref[7:8, :] = errs
    outs = [
        pltpu.make_async_copy(far_ref, far_out, small_sem.at[3]),
        pltpu.make_async_copy(table_ref, table_out, small_sem.at[4]),
    ]
    for out in outs:
        out.start()

    for n in shifts:

        @pl.when(later[n])
        def _(n=n):
            pl.semaphore_wait(late_sem.at[WINDOW + n], 1)
            send_block(n)

    for step in range(half):
        to_right[half + step].wait_recv()
        to_left[step].wait_recv()
    for relay in relays:
        relay.wait()
    for copy in to_right + to_left:
        copy.wait_send()
    pltpu.make_async_copy(nearby, nearby, near_send).wait()
    to_pair.wait_send()
    block_copy.wait()
    for out in outs:
        out.wait()

    for n in shifts:

        @pl.when(valid[n])
        def _(n=n):
            pltpu.make_async_copy(block(n), block(n), row_send.at[WINDOW + n]).wait()
            pltpu.make_async_copy(block(n), block(n), row_recv.at[WINDOW + n]).wait()


def gather(mesh, ensemble, locations, values, errors):
    part_rows, held = ensemble.shape
    dma = pltpu.SemaphoreType.DMA
    return pl.pallas_call(
        functools.partial(gather_kernel, mesh.shape["state"] // CORES, held),
        out_shape=(
            jax.ShapeDtypeStruct((ROWS, 1, TILE), jnp.float32),
            jax.ShapeDtypeStruct((REPS, part_rows, held), jnp.float32),
            jax.ShapeDtypeStruct((8, TILE), jnp.float32),
            jax.ShapeDtypeStruct((1, 1), jnp.int32),
        ),
        in_specs=[pl.BlockSpec(memory_space=pl.ANY)] * 4,
        out_specs=(pl.BlockSpec(memory_space=pl.ANY),) * 4,
        scratch_shapes=[
            pltpu.SMEM((NOBS,), jnp.int32),
            pltpu.SMEM((NOBS,), jnp.float32),
            pltpu.SMEM((NOBS,), jnp.float32),
            pltpu.SMEM((1, 1), jnp.int32),
            pltpu.VMEM((8, TILE), jnp.float32),
            dma((5,)), dma,
            pltpu.VMEM((part_rows, held), jnp.float32),
            pltpu.VMEM((held // TILE, part_rows, TILE), jnp.float32),
            pltpu.VMEM((1, 1, TILE), jnp.float32),
            dma, dma, pltpu.SemaphoreType.REGULAR((2 * WINDOW + 1,)),
            dma, dma, dma((2 * WINDOW + 1,)), dma((2 * WINDOW + 1,)),
            dma((CHUNKS,)), dma((CHUNKS,)), dma((CHUNKS,)), dma((CHUNKS,)),
            dma((CHUNKS,)), dma((CHUNKS,)), dma((CHUNKS,)), dma((CHUNKS,)),
        ],
        compiler_params=pltpu.CompilerParams(collective_id=0, has_side_effects=True),
        name="gather",
    )(locations, values, errors, ensemble)


def solve_kernel(
    windowed, held, table_ref, rows_ref, all_ref, out_ref,
    y_ref, u_ref, w_ref, center_ref, mutual_ref, tile_ref, done_ref, out_sem,
):
    state = lax.axis_index("state")
    rep = lax.axis_index("rep")
    part_rows = all_ref.shape[1]
    order = [(rep + step) & (REPS - 1) for step in range(REPS)]

    def entry(number, t):
        return table_ref[number, t].astype(jnp.int32)

    total = entry(5, 0)
    direct = entry(5, 1)
    diagonal = iota((part_rows, TILE), 1) - iota((part_rows, TILE), 0)

    def spread(t):
        spot = entry(0, t)
        if windowed:
            base = jnp.clip(entry(1, t), 0, ROWS - REPS)
            place = entry(2, t)
        else:
            base = entry(3, t) * REPS
            place = 0
        for step in range(REPS):
            row = jnp.broadcast_to(rows_ref[base + order[step]], (part_rows, TILE))
            column = jnp.sum(jnp.where(diagonal == place, row, 0.0), axis=1, keepdims=True)
            y_ref[t, step * part_rows : (step + 1) * part_rows, :] = jnp.broadcast_to(
                column, (part_rows, TILE)
            )
        center = ((spot >> 7) << 7).astype(jnp.float32) + (TILE - 1) * 0.5
        center_ref[pl.ds(t, 1), :] = jnp.full((1, TILE), center, jnp.float32)

    def spread_batch(b, carry):
        for i in range(BATCH):
            spread(b * BATCH + i)
        return carry

    def batches(number):
        return (number + BATCH - 1) // BATCH

    lax.fori_loop(0, batches(total), spread_batch, 0)

    tiles = held // TILE
    tile_centers = (state * held + iota((tiles, TILE), 0) * TILE).astype(jnp.float32) + (
        TILE - 1
    ) * 0.5

    def assimilate(i, carry):
        t = total - 1 - i
        spot = table_ref[0, t]
        error = table_ref[7, t]
        y = y_ref[t]
        mean = jnp.sum(y, axis=0, keepdims=True) * (1.0 / M)
        spread_of = y - mean
        variance = jnp.sum(spread_of * spread_of, axis=0, keepdims=True) * (1.0 / (M - 1))
        total_var = variance + error
        shrink = 1.0 / (1.0 + jnp.sqrt(error / total_var))
        u = spread_of * (1.0 / ((M - 1) * total_var))
        w = (table_ref[6, t] - mean) - shrink * spread_of
        u_ref[t] = u
        w_ref[t] = w
        mutual_ref[...] = taper(jnp.abs(center_ref[...] - spot))
        tile_ref[t] = taper(jnp.abs(tile_centers - spot))

        def update(b, inner):
            first = b * BATCH
            others = [y_ref[first + i] for i in range(BATCH)]
            for i, other in enumerate(others):
                projected = jnp.sum(u * other, axis=0, keepdims=True)
                others[i] = other + w * (mutual_ref[pl.ds(first + i, 1), :] * projected)
            for i, other in enumerate(others):
                y_ref[first + i] = other
            return inner

        lax.fori_loop(0, batches(t), update, 0)
        return carry

    lax.fori_loop(0, total, assimilate, 0)
    group = 8

    def apply(g, carry):
        spans = [
            pl.ds(pl.multiple_of((g * group + i) * TILE, TILE), TILE) for i in range(group)
        ]

        def one(d, values):
            t = entry(4, direct - 1 - d)
            u = u_ref[t]
            w = w_ref[t]
            result = []
            for i in range(group):
                projected = jnp.sum(u * values[i], axis=0, keepdims=True)
                weight = tile_ref[t, pl.ds(g * group + i, 1), :]
                result.append(values[i] + w * (weight * projected))
            return tuple(result)

        start = tuple(
            jnp.concatenate([all_ref[member, :, span] for member in order], axis=0)
            for span in spans
        )
        values = lax.fori_loop(0, direct, one, start)
        for span, value in zip(spans, values):
            done_ref[:, span] = value[:part_rows]
        width = group * TILE
        wide = pl.ds(pl.multiple_of(g * width, width), width)
        pltpu.make_async_copy(done_ref.at[:, wide], out_ref.at[:, wide], out_sem).start()
        return carry

    lax.fori_loop(0, tiles // group, apply, 0)
    pltpu.make_async_copy(done_ref, out_ref, out_sem).wait()


def solve(windowed, part_rows, held, table, rows, everything):
    vmem = pl.BlockSpec(memory_space=pltpu.VMEM)
    block = pltpu.VMEM((NOBS, M, TILE), jnp.float32)
    return pl.pallas_call(
        functools.partial(solve_kernel, windowed, held),
        out_shape=jax.ShapeDtypeStruct((part_rows, held), jnp.float32),
        in_specs=[pl.BlockSpec(memory_space=pltpu.SMEM), vmem, vmem],
        out_specs=pl.BlockSpec(memory_space=pl.ANY),
        compiler_params=pltpu.CompilerParams(vmem_limit_bytes=65918864),
        scratch_shapes=[
            block, block, block,
            pltpu.VMEM((NOBS, TILE), jnp.float32),
            pltpu.VMEM((NOBS, TILE), jnp.float32),
            pltpu.VMEM((NOBS, held // TILE, TILE), jnp.float32),
            pltpu.VMEM((part_rows, held), jnp.float32),
            pltpu.SemaphoreType.DMA,
        ],
        name="solve",
    )(table, rows, everything)


def full_rows(mesh, ensemble, locations):
    part_rows, held = ensemble.shape
    states = mesh.shape["state"]
    offsets = locations - lax.axis_index("state") * held
    inside = ((offsets >= 0) & (offsets < held)).astype(jnp.float32)
    columns = jnp.take(ensemble, jnp.clip(offsets, 0, held - 1), axis=1) * inside[None, :]
    placed = jnp.zeros((REPS, part_rows, NOBS), jnp.float32)
    placed = lax.dynamic_update_slice(placed, columns[None], (lax.axis_index("rep"), 0, 0))
    stride = 1
    while stride < states:
        pairs = [(i, i ^ stride) for i in range(states)]
        placed = placed + lax.ppermute(placed, "state", pairs)
        stride *= 2
    stride = 1
    while stride < REPS:
        pairs = [(i, i ^ stride) for i in range(REPS)]
        placed = placed + lax.ppermute(placed, "rep", pairs)
        stride *= 2
    by_obs = jnp.transpose(placed, (2, 0, 1)).reshape(NOBS * REPS, 1, part_rows)
    return jnp.pad(by_obs, ((0, 0), (0, 0), (0, TILE - part_rows)))


def on_device(mesh, ensemble, obs_values, obs_error, obs_location):
    part_rows, held = ensemble.shape
    rows, everything, table, far = gather(mesh, ensemble, obs_location, obs_values, obs_error)
    return lax.switch(
        far[0, 0],
        (
            lambda: solve(True, part_rows, held, table, rows, everything),
            lambda: solve(
                False, part_rows, held, table, full_rows(mesh, ensemble, obs_location), everything
            ),
        ),
    )


def solution(mesh):
    in_specs = (P("rep", "state"), P(), P(), P())
    out_specs = P("rep", "state")
    return jax.shard_map(
        functools.partial(on_device, mesh),
        mesh=mesh,
        in_specs=in_specs,
        out_specs=out_specs,
        check_vma=False,
    )
```
